32 devices in a mesh: pts: 8 (over y, x, core), cols: 4 (over z).
Axes of the slice: x: 2, y: 2, z: 4, core: 2. Of those that a mesh axis runs over, the one named last changes fastest.
Arguments:
- snapshot: float32 [1024, 2048], P('pts', 'cols'), may hold values from -18 to 18
- weights: float32 [1024], P('pts'), may hold values from 0.25 to 9
- damping: int32 [3, 2], replicated, may hold values from 1 to 8
Outputs:
- rotated: float32 [1024, 2048], P('pts', 'cols')
The draws below stay inside these ranges and needn't reach their ends.
All inputs are finite; a program needn't handle non-finite values.
Results may differ from the reference program's by a relative error of at most 0.0003.
Values sent between devices are 32-bit elements; how exact they have to be, the bound alone decides.
No kernel may reach another device: no remote copies, remote signals or barrier semaphores. Data moves between devices by JAX's collectives and lax.ppermute only.
A program may use at most 64 MiB of HBM per device.

```python
import jax
import jax.numpy as jnp
from jax import lax

B = 256
STEPS = 3
NS_ITERS = 3
PAIRS = 4
POINTS = 1024
COLUMNS = 2048


def draw_snapshot(key, part):
    key_noise = jax.random.fold_in(key, 11)
    key_scale = jax.random.fold_in(key, 12)
    noise = jnp.clip(jax.random.normal(key_noise, (POINTS, COLUMNS), jnp.float32), -6.0, 6.0)
    column_scale = jnp.exp(jax.random.uniform(key_scale, (COLUMNS,), jnp.float32, jnp.log(0.3), jnp.log(3.0)))
    return noise * column_scale[None, :]


def draw_weights(key, part):
    key_rough = jax.random.fold_in(key, 21)
    positions = jnp.arange(POINTS, dtype=jnp.float32)
    rising = 1.0 + 2.0 * positions / (POINTS - 1)
    rough = jnp.exp(jax.random.uniform(key_rough, (POINTS,), jnp.float32, jnp.log(0.5), jnp.log(2.0)))
    return rising * rough


def place_ends(array, key, least, high):
    longest = array.shape.index(max(array.shape))
    spots = []
    for shift in (0, 1):
        where = [jax.random.randint(jax.random.fold_in(key, axis), (), 0, length) for axis, length in enumerate(array.shape)]
        where[longest] = (where[longest] + shift) % array.shape[longest]
        spots.append(tuple(where))
    return array.at[spots[0]].set(least).at[spots[1]].set(high)


def setup_inputs(seed: int = 0) -> dict:
    key_list = jax.random.split(jax.random.key(seed), 4)
    return {
        "snapshot": draw_snapshot(jax.random.fold_in(key_list[3], 71), 0),
        "weights": draw_weights(jax.random.fold_in(key_list[3], 71), 0),
        "damping": place_ends(jax.random.randint(key_list[2], (STEPS, 2), 1, 9), jax.random.fold_in(key_list[2], 1), 1, 8).astype(jnp.int32),
    }


EPSILON = 1e-06

def dot_full(left, right):
    return jnp.dot(left, right, precision=lax.Precision.HIGHEST, preferred_element_type=jnp.float32)

def inner_full(left, right):
    return lax.dot_general(left, right, (((0,), (0,)), ((), ())), precision=lax.Precision.HIGHEST, preferred_element_type=jnp.float32)

def inverse_root(square, scale):
    identity = jnp.eye(square.shape[0], dtype=jnp.float32)
    current = square / scale
    factor = identity
    for turn_index in range(NS_ITERS):
        if turn_index == 0:
            middle = 1.5 * identity - 0.5 * current
            factor = middle
        else:
            middle = 1.5 * identity - 0.5 * dot_full(factor, current)
            factor = dot_full(middle, factor)
        if turn_index + 1 < NS_ITERS:
            current = dot_full(current, middle)
    return factor / jnp.sqrt(scale)

def side_factors(coupling, scale):
    identity = jnp.eye(coupling.shape[0], dtype=jnp.float32)
    square = identity + dot_full(coupling, coupling.T)
    factor = inverse_root(square, scale)
    return (factor, dot_full(coupling.T, factor))

def rotate_pair(upper_block, lower_block, point_weight, damping_now):
    weighted = point_weight * lower_block
    pair_gram = inner_full(upper_block, weighted)
    norm_upper = lax.optimization_barrier(jnp.sum(point_weight * upper_block * upper_block, axis=0))
    norm_lower = lax.optimization_barrier(jnp.sum(weighted * lower_block, axis=0))
    coupling = damping_now * pair_gram / jnp.sqrt((norm_upper[:, None] + EPSILON) * (norm_lower[None, :] + EPSILON))
    scale = 1.0 + jnp.sum(coupling * coupling)
    upper_factor, upper_cross = side_factors(coupling, scale)
    lower_factor, lower_cross = side_factors(coupling.T, scale)
    new_upper = dot_full(upper_block, upper_factor) - dot_full(lower_block, upper_cross)
    new_lower = dot_full(upper_block, lower_cross) + dot_full(lower_block, lower_factor)
    return (new_upper, new_lower)

def reference(snapshot, weights, damping):
    blocks = snapshot.reshape(POINTS, PAIRS, 2, B)
    uppers = jnp.transpose(blocks[:, :, 0, :], (1, 0, 2))
    lowers = jnp.transpose(blocks[:, :, 1, :], (1, 0, 2))
    point_weight = weights[:, None]
    for step_index in range(STEPS):
        numer = damping[step_index, 0].astype(jnp.float32)
        denom = damping[step_index, 1].astype(jnp.float32)
        damping_now = numer / (numer + denom)
        moved = jnp.roll(lowers, step_index, axis=0)

        def one_pair(pair_blocks):
            return rotate_pair(pair_blocks[0], pair_blocks[1], point_weight, damping_now)
        uppers, moved = lax.map(one_pair, (uppers, moved))
        lowers = jnp.roll(moved, -step_index, axis=0)
    joined = jnp.stack([uppers, lowers], axis=2)
    return jnp.transpose(joined, (1, 0, 2, 3)).reshape(POINTS, COLUMNS)
```

```python
import jax
import jax.numpy as jnp
from jax import lax
from jax.sharding import PartitionSpec as P

STEPS = 3
EPSILON = 1e-06


def shifted(value, axis, steps):
    count = lax.axis_size(axis)
    pairs = [(source, (source + steps) % count) for source in range(count)]
    return lax.ppermute(value, axis, pairs)


def swapped(value, bits):
    count = lax.axis_size("pts")
    return lax.ppermute(value, "pts", [(source, source ^ bits) for source in range(count)])


def chip_sum(value):
    count = lax.axis_size("pts")
    bit = 2
    while bit < count:
        if 2 * bit < count:
            parts = [swapped(value, bits) for bits in (3 * bit, 2 * bit, bit)]
            bit *= 4
        else:
            parts = [swapped(value, bit)]
            bit *= 2
        value = sum(parts, value)
    return value


def dot_high(left, right, dims=((1,), (0,))):
    return lax.dot_general(
        left, right, (dims, ((), ())), precision=lax.Precision.HIGH, preferred_element_type=jnp.float32
    )


def rows_swapped(value):
    half = value.shape[0] // 2
    return jnp.concatenate([value[half:], value[:half]], axis=0)


def inverse_root(square, scale):
    identity = jnp.eye(square.shape[0], dtype=jnp.float32)
    base = (identity + square) / scale
    second = dot_high(base, base)
    first = 1.5 * identity - 0.5 * base
    first_square = 2.25 * identity - 1.5 * base + 0.25 * second
    both = 1.5 * first - 0.5 * dot_high(1.5 * base - 0.5 * second, first_square)
    cubic = dot_high(dot_high(base, both), dot_high(both, both))
    return (1.5 * both - 0.5 * cubic) / jnp.sqrt(scale)


def body(snapshot, weights, damping):
    rows, columns = snapshot.shape
    width = columns // 2
    half = width // 2
    first_core = lax.axis_index("pts") % 2 == 0

    def own_first(block):
        left, right = block[:, :half], block[:, half:]
        return jnp.concatenate(
            [jnp.where(first_core, left, right), jnp.where(first_core, right, left)], axis=1
        )

    point_weight = jnp.concatenate([weights, swapped(weights, 1)])[:, None]
    other = swapped(snapshot, 1)
    upper = own_first(jnp.concatenate([snapshot[:, :width], other[:, :width]], axis=0))
    lower = own_first(jnp.concatenate([snapshot[:, width:], other[:, width:]], axis=0))
    own = lower[:, :half]
    for step in range(STEPS):
        weighted = point_weight * own
        gram = dot_high(upper, weighted, ((0,), (0,)))
        norm_lower = jnp.sum(weighted * own, axis=0)
        norm_upper = jnp.sum(point_weight * upper[:, :half] * upper[:, :half], axis=0)
        norms = jnp.concatenate([norm_lower[None], norm_upper[None], jnp.zeros((6, half), jnp.float32)])
        payload = chip_sum(jnp.concatenate([gram, norms], axis=0))
        remote = swapped(payload, 1)
        if step > 0:
            lower = jnp.concatenate([own, rows_swapped(swapped(own, 1))], axis=1)
        gram = jnp.concatenate([payload[:width], rows_swapped(remote[:width])], axis=1)
        norm_lower = jnp.concatenate([payload[width], remote[width]])
        norm_upper = jnp.concatenate([payload[width + 1], remote[width + 1]])
        numer = damping[step, 0].astype(jnp.float32)
        denom = damping[step, 1].astype(jnp.float32)
        coupling = (
            numer
            / (numer + denom)
            * gram
            * lax.rsqrt(norm_upper + EPSILON)[:, None]
            * lax.rsqrt(norm_lower + EPSILON)[None, :]
        )
        scale = 1.0 + jnp.sum(coupling * coupling)
        upper_factor = inverse_root(dot_high(coupling, coupling, ((1,), (1,))), scale)
        lower_factor = inverse_root(dot_high(coupling, coupling, ((0,), (0,))), scale)
        cross = dot_high(upper_factor, coupling)
        if step + 1 < STEPS:
            own = dot_high(upper, cross[:, :half]) + dot_high(lower, lower_factor[:, :half])
            own = shifted(own, "cols", 1)
            upper = dot_high(upper, upper_factor) - dot_high(lower, cross, ((1,), (1,)))
        else:
            upper, lower = upper[:rows], lower[:rows]
            moved = dot_high(upper, cross) + dot_high(lower, lower_factor)
            moved = shifted(own_first(moved), "cols", 1 - STEPS)
            upper = own_first(dot_high(upper, upper_factor) - dot_high(lower, cross, ((1,), (1,))))
    return jnp.concatenate([upper, moved], axis=1)


def solution(mesh):
    placed = (P("pts", "cols"), P("pts"), P())
    return jax.shard_map(
        body, mesh=mesh, in_specs=placed, out_specs=P("pts", "cols"), check_vma=False
    )
```

```python
import functools

import jax
import jax.numpy as jnp
from jax import lax
from jax.experimental import pallas as pl
from jax.experimental.pallas import tpu as pltpu
from jax.sharding import PartitionSpec as P

STEPS = 3
EPSILON = 1e-06
F32 = jnp.float32


def shifted(value, axis, steps):
    count = lax.axis_size(axis)
    pairs = [(source, (source + steps) % count) for source in range(count)]
    return lax.ppermute(value, axis, pairs)


def swapped(value, even_bits, odd_bits):
    count = lax.axis_size("pts")
    pairs = [(source, source ^ (odd_bits if source % 2 else even_bits)) for source in range(count)]
    return lax.ppermute(value, "pts", pairs)


def chip_sum(value):
    count = lax.axis_size("pts")
    bit = 2
    while bit < count:
        if 2 * bit < count:
            rounds = [(bit, 2 * bit), (2 * bit, bit)]
        else:
            rounds = [(bit, bit)]
        for even_bits, odd_bits in rounds:
            value = value + swapped(value, even_bits, odd_bits)
        bit *= 2 ** len(rounds)
    return value


def dot_high(left, right, dims=((1,), (0,))):
    return lax.dot_general(
        left, right, (dims, ((), ())), precision=lax.Precision.HIGH, preferred_element_type=F32
    )


def two_parts(value):
    high = value.astype(jnp.bfloat16)
    return high, (value - high.astype(F32)).astype(jnp.bfloat16)


def as_left(value):
    high, low = two_parts(value)
    return jnp.concatenate([high, high, low], axis=1)


def as_right(value):
    high, low = two_parts(value)
    return jnp.concatenate([high, low, high], axis=0)


def product(left, right):
    return jnp.dot(left, right, preferred_element_type=F32)


def product_bt(left, right):
    high, low = two_parts(right)
    return lax.dot_general(
        as_left(left),
        jnp.concatenate([high, low, high], axis=1),
        (((1,), (1,)), ((), ())),
        preferred_element_type=F32,
    )


def halves_swapped(value):
    half = value.shape[0] // 2
    return jnp.concatenate([value[half:], value[:half]], axis=0)


def inverse_root(square, inverse_scale, columns):
    width = square.shape[0]
    rows = lax.broadcasted_iota(jnp.int32, (width, width), 0)
    cols = lax.broadcasted_iota(jnp.int32, (width, width), 1)
    identity = jnp.where(rows == cols, 1.0, 0.0).astype(F32)
    base = (identity + square) * inverse_scale
    base_left = as_left(base)
    second = product(base_left, as_right(base))
    first = 1.5 * identity - 0.5 * base
    first_square = 2.25 * identity - 1.5 * base + 0.25 * second
    both = 1.5 * first - 0.5 * product(as_left(1.5 * base - 0.5 * second), as_right(first_square))
    both_right = as_right(both)
    cubic_left = product(base_left, both_right)
    cubic_right = product(as_left(both), both_right[:, :columns])
    cubic = product(as_left(cubic_left), as_right(cubic_right))
    return 1.5 * both[:, :columns] - 0.5 * cubic


def joined(own, other):
    return jnp.concatenate([own, halves_swapped(other)], axis=1)


def lower_kernel(rows, columns, damp, own_sum, other_sum, upper, own, other, moved, coupling_out, scale_out):
    width = upper.shape[0]
    gram = joined(own_sum[:width], other_sum[:width])
    norms = jnp.concatenate([own_sum[width:], other_sum[width:]], axis=1)
    inverse = lax.rsqrt(norms + EPSILON)
    coupling = gram * (damp[0] * inverse.T[:, 1:2]) * inverse[0:1]
    scale = 1.0 + jnp.sum(coupling * coupling, keepdims=True)
    coupling_out[...] = coupling
    scale_out[...] = jnp.broadcast_to(scale, scale_out.shape)
    coupling_right = as_right(coupling)
    square = product(as_left(coupling.T), coupling_right)
    factor = inverse_root(square, 1.0 / scale, columns) * lax.rsqrt(scale)
    lower = joined(own[...], other[...])[:rows]
    mixed = lower + product(as_left(upper[:rows]), coupling_right)
    moved[...] = product(as_left(mixed), as_right(factor))


def upper_kernel(coupling_ref, scale_ref, upper, own, other, *rest):
    coupling = coupling_ref[...]
    scale = scale_ref[0:1, 0:1]
    factor = inverse_root(product_bt(coupling, coupling), 1.0 / scale, coupling.shape[1])
    factor = factor * lax.rsqrt(scale)
    rows = rest[-1].shape[0]
    lower = joined(own[...], other[...])[:rows]
    mixed = upper[:rows] - product_bt(lower, coupling)
    upper = product(as_left(mixed), as_right(factor))
    if len(rest) == 1:
        rest[0][...] = upper
        return
    weight, gram_left, norm_out, upper_out = rest
    upper_out[...] = upper
    weighted = weight[...] * upper
    norm_out[...] = jnp.sum(weighted * upper, axis=0, keepdims=True)[:, : norm_out.shape[1]]
    gram_left[...] = as_left(weighted.T)


def gram_kernel(gram_left, norm_upper, weight, own_ref, payload):
    width = gram_left.shape[0]
    own = own_ref[...]
    payload[:width] = product(gram_left[...], as_right(own))
    norm_lower = jnp.sum(weight[...] * own * own, axis=0, keepdims=True)
    rows = lax.broadcasted_iota(jnp.int32, (8, own.shape[1]), 0)
    payload[width:] = jnp.where(rows == 0, norm_lower, jnp.where(rows == 1, norm_upper[...], 0.0))


def in_vmem(kernel, outs, *args, scalars=0):
    specs = [pl.BlockSpec(memory_space=pltpu.SMEM)] * scalars
    specs += [pl.BlockSpec(memory_space=pltpu.VMEM)] * (len(args) - scalars)
    return pl.pallas_call(
        kernel,
        out_shape=[jax.ShapeDtypeStruct(shape, dtype) for shape, dtype in outs],
        in_specs=specs,
        out_specs=[pl.BlockSpec(memory_space=pltpu.VMEM)] * len(outs),
        compiler_params=pltpu.CompilerParams(vmem_limit_bytes=24 << 20),
    )(*args)


def body(snapshot, weights, damping):
    rows, columns = snapshot.shape
    width = columns // 2
    half = width // 2
    first_core = lax.axis_index("pts") % 2 == 0

    def own_first(block):
        left, right = block[:, :half], block[:, half:]
        return jnp.concatenate(
            [jnp.where(first_core, left, right), jnp.where(first_core, right, left)], axis=1
        )

    weight = jnp.concatenate([weights, swapped(weights, 1, 1)])[:, None]
    far = swapped(snapshot, 1, 1)
    upper = own_first(jnp.concatenate([snapshot[:, :width], far[:, :width]], axis=0))
    lower = own_first(jnp.concatenate([snapshot[:, width:], far[:, width:]], axis=0))
    own, other = lower[:, :half], halves_swapped(lower[:, half:])
    weighted = weight * upper
    gram = dot_high(weighted, own, ((0,), (0,)))
    norm_lower = jnp.sum(weight * own * own, axis=0)
    norm_upper = jnp.sum(weighted[:, :half] * upper[:, :half], axis=0)
    norms = jnp.concatenate([norm_lower[None], norm_upper[None], jnp.zeros((6, half), F32)])
    payload = jnp.concatenate([gram, norms], axis=0)
    damps = damping[:, 0].astype(F32) / (damping[:, 0] + damping[:, 1]).astype(F32)
    whole = (2 * rows, width)
    for step in range(STEPS):
        last = step + 1 == STEPS
        payload = chip_sum(payload)
        remote = swapped(payload, 1, 1)
        if step > 0:
            other = swapped(own, 1, 1)
        shape = (rows, width) if last else (2 * rows, half)
        moved, coupling, scale = in_vmem(
            functools.partial(lower_kernel, *shape),
            [(shape, F32), ((width, width), F32), ((8, 128), F32)],
            damps[step : step + 1],
            payload,
            remote,
            upper,
            own,
            other,
            scalars=1,
        )
        if last:
            moved = shifted(own_first(moved), "cols", 1 - STEPS)
            (upper,) = in_vmem(upper_kernel, [(shape, F32)], coupling, scale, upper, own, other)
            return jnp.concatenate([own_first(upper), moved], axis=1)
        gram_left, norm_upper, upper = in_vmem(
            upper_kernel,
            [((width, 6 * rows), jnp.bfloat16), ((1, half), F32), (whole, F32)],
            coupling,
            scale,
            upper,
            own,
            other,
            weight,
        )
        own = shifted(moved, "cols", 1)
        (payload,) = in_vmem(
            gram_kernel, [((width + 8, half), F32)], gram_left, norm_upper, weight, own
        )


def solution(mesh):
    placed = (P("pts", "cols"), P("pts"), P())
    return jax.shard_map(
        body, mesh=mesh, in_specs=placed, out_specs=P("pts", "cols"), check_vma=False
    )
```

```python
import functools

import jax
import jax.numpy as jnp
from jax import lax
from jax.experimental import pallas as pl
from jax.experimental.pallas import tpu as pltpu
from jax.sharding import PartitionSpec as P

STEPS = 3
EPSILON = 1e-06
F32 = jnp.float32


def shifted(value, axis, steps):
    count = lax.axis_size(axis)
    pairs = [(source, (source + steps) % count) for source in range(count)]
    return lax.ppermute(value, axis, pairs)


def swapped(value, even_bits, odd_bits):
    count = lax.axis_size("pts")
    pairs = [(source, source ^ (odd_bits if source % 2 else even_bits)) for source in range(count)]
    return lax.ppermute(value, "pts", pairs)


def chip_sum(value, beside=None):
    count = lax.axis_size("pts")
    bit = 2
    while bit < count:
        if 2 * bit < count:
            rounds = [(bit, 2 * bit), (2 * bit, bit)]
        else:
            rounds = [(bit, bit)]
        for even_bits, odd_bits in rounds:
            value = value + swapped(value, even_bits, odd_bits)
            if beside is not None:
                value, beside = lax.optimization_barrier((value, beside))
        bit *= 2 ** len(rounds)
    return value, beside


def two_parts(value):
    high = value.astype(jnp.bfloat16)
    return high, (value - high.astype(F32)).astype(jnp.bfloat16)


def as_left(value):
    high, low = two_parts(value)
    return jnp.concatenate([high, high, low], axis=1)


def as_right(value):
    high, low = two_parts(value)
    return jnp.concatenate([high, low, high], axis=0)


def product(left, right):
    return jnp.dot(left, right, preferred_element_type=F32)


def product_tl(left, right):
    high, low = two_parts(left)
    return lax.dot_general(
        jnp.concatenate([high, high, low], axis=0),
        right,
        (((0,), (0,)), ((), ())),
        preferred_element_type=F32,
    )


def product_bt(left, right):
    high, low = two_parts(right)
    return lax.dot_general(
        as_left(left),
        jnp.concatenate([high, low, high], axis=1),
        (((1,), (1,)), ((), ())),
        preferred_element_type=F32,
    )


def halves_swapped(value):
    half = value.shape[0] // 2
    return jnp.concatenate([value[half:], value[:half]], axis=0)


def unit(width):
    rows = lax.broadcasted_iota(jnp.int32, (width, width), 0)
    columns = lax.broadcasted_iota(jnp.int32, (width, width), 1)
    return jnp.where(rows == columns, 1.0, 0.0).astype(F32)


def times_inverse_root(left, square, scale, columns):
    identity = unit(square.shape[0])
    base = (identity + square) * (1.0 / scale)
    base_right = as_right(base)
    left_parts = as_left(left)
    second = product(as_left(base), base_right)
    left_base = product(left_parts, base_right)
    first_square = 2.25 * identity - 1.5 * base + 0.25 * second
    both = 2.25 * identity - 0.75 * base
    both = both - 0.5 * product(as_left(1.5 * base - 0.5 * second), as_right(first_square))
    both_right = as_right(both)
    both_square = product(as_left(both), both_right[:, :columns])
    left_both = product(left_parts, both_right[:, :columns])
    left_cubic = product(as_left(product(as_left(left_base), both_right)), as_right(both_square))
    return (1.5 * left_both - 0.5 * left_cubic) * lax.rsqrt(scale)


def joined(own, other):
    return jnp.concatenate([own, halves_swapped(other)], axis=1)


def own_half(half):
    own = (lax.axis_index("pts") % 2) * half
    return pl.multiple_of(own, half), pl.multiple_of(half - own, half)


def start_blocks(near, far):
    width = near.shape[1] // 2
    own, other = own_half(width // 2)

    def taken(start):
        piece = (slice(None), pl.ds(start, width // 2))
        return jnp.concatenate([near[piece], far[piece]], axis=0)

    upper = jnp.concatenate([taken(own), taken(other)], axis=1)
    return upper, jnp.concatenate([taken(width + own), taken(width + other)], axis=1)


def later_blocks(upper, own, other):
    return upper[...], joined(own[...], other[...])


def stored(ref, value):
    half = ref.shape[1] // 2
    own, other = own_half(half)
    ref[:, pl.ds(own, half)] = value[:, :half]
    ref[:, pl.ds(other, half)] = value[:, half:]


def start_kernel(near, weight, own_part, other_part):
    width = near.shape[1] // 2
    half = width // 2
    own, other = own_half(half)
    point_weight = jnp.broadcast_to(weight[...], (8, weight.shape[1])).T[:, 0:1]
    upper_own, upper_other = near[:, pl.ds(own, half)], near[:, pl.ds(other, half)]
    upper = jnp.concatenate([upper_own, upper_other], axis=1)
    rows = lax.broadcasted_iota(jnp.int32, (8, half), 0)
    for start, norm_of, out in ((own, upper_own, own_part), (other, upper_other, other_part)):
        lower = near[:, pl.ds(width + start, half)]
        weighted = point_weight * lower
        gram = product_tl(upper, as_right(weighted))
        out[:width] = gram if out is own_part else halves_swapped(gram)
        norm_lower = jnp.sum(weighted * lower, axis=0, keepdims=True)
        norm_upper = jnp.sum(point_weight * norm_of * norm_of, axis=0, keepdims=True)
        out[width:] = jnp.where(rows == 0, norm_lower, jnp.where(rows == 1, norm_upper, 0.0))


def lower_kernel(blocks, last, damp, own_sum, other_sum, *refs):
    *block_refs, moved, coupling_out, scale_out = refs
    width = coupling_out.shape[0]
    upper, lower = blocks(*block_refs)
    gram = joined(own_sum[:width], other_sum[:width])
    norms = jnp.concatenate([own_sum[width:], other_sum[width:]], axis=1)
    inverse = lax.rsqrt(norms + EPSILON)
    coupling = gram * (damp[0:1, 0:1] * inverse.T[:, 1:2]) * inverse[0:1]
    scale = 1.0 + jnp.sum(coupling * coupling, keepdims=True)
    coupling_out[...] = coupling
    scale_out[...] = jnp.broadcast_to(scale, scale_out.shape)
    coupling_right = as_right(coupling)
    square = product_tl(coupling, coupling_right)
    rows, columns = moved.shape
    mixed = lower[:rows] + product(as_left(upper[:rows]), coupling_right)
    result = times_inverse_root(mixed, square, scale, columns)
    if last:
        stored(moved, result)
    else:
        moved[...] = result


def rotated_upper(blocks, rows, coupling_ref, scale_ref, *block_refs):
    coupling = coupling_ref[...]
    upper, lower = blocks(*block_refs)
    mixed = upper[:rows] - product_bt(lower[:rows], coupling)
    square = product_bt(coupling, coupling)
    return times_inverse_root(mixed, square, scale_ref[0:1, 0:1], coupling.shape[1])


def upper_kernel(blocks, weight, *refs):
    *ins, gram_left, norm_out, upper_out = refs
    upper = rotated_upper(blocks, upper_out.shape[0], *ins)
    upper_out[...] = upper
    weighted = weight[...] * upper
    norm_out[...] = jnp.sum(weighted * upper, axis=0, keepdims=True)[:, : norm_out.shape[1]]
    gram_left[...] = as_left(weighted.T)


def last_upper_kernel(blocks, *refs):
    *ins, out, held, sent = refs
    stored(held, rotated_upper(blocks, held.shape[0], *ins))
    copy = pltpu.make_async_copy(held, out.at[:, pl.ds(0, held.shape[1])], sent)
    copy.start()
    copy.wait()


def last_lower_kernel(lower, filled, out, sent):
    del filled
    width = lower.shape[1]
    copy = pltpu.make_async_copy(lower, out.at[:, pl.ds(width, width)], sent)
    copy.start()
    copy.wait()


def gram_kernel(gram_left, norm_upper, weight, own_ref, payload):
    width = gram_left.shape[0]
    own = own_ref[...]
    payload[:width] = product(gram_left[...], as_right(own))
    norm_lower = jnp.sum(weight[...] * own * own, axis=0, keepdims=True)
    rows = lax.broadcasted_iota(jnp.int32, (8, own.shape[1]), 0)
    payload[width:] = jnp.where(rows == 0, norm_lower, jnp.where(rows == 1, norm_upper[...], 0.0))


ON_CHIP = pl.BlockSpec(memory_space=pltpu.VMEM)
ANYWHERE = pl.BlockSpec(memory_space=pl.ANY)
GRANT = pltpu.CompilerParams(vmem_limit_bytes=24 << 20)


def in_vmem(kernel, outs, *args):
    return pl.pallas_call(
        kernel,
        out_shape=[jax.ShapeDtypeStruct(shape, dtype) for shape, dtype in outs],
        in_specs=[ON_CHIP] * len(args),
        out_specs=[ON_CHIP] * len(outs),
        compiler_params=GRANT,
    )(*args)


def body(snapshot, weights, damping):
    rows, columns = snapshot.shape
    width = columns // 2
    half = width // 2
    whole = (2 * rows, width)
    own_part, other_part = in_vmem(start_kernel, [((width + 8, half), F32)] * 2, snapshot, weights[None])
    payload = own_part + swapped(other_part, 1, 1)
    weight = jnp.concatenate([weights, swapped(weights, 1, 1)])[:, None]
    blocks, held, arriving = start_blocks, (snapshot,), swapped(snapshot, 1, 1)
    damps = damping[:, 0].astype(F32) / (damping[:, 0] + damping[:, 1]).astype(F32)
    damps = jnp.broadcast_to(damps[:, None], (STEPS, 128))
    for step in range(STEPS):
        last = step + 1 == STEPS
        payload, arriving = chip_sum(payload, arriving)
        held = held + (arriving,)
        moved, coupling, scale = in_vmem(
            functools.partial(lower_kernel, blocks, last),
            [((rows, width) if last else (2 * rows, half), F32), ((width, width), F32), ((8, 128), F32)],
            damps[step : step + 1],
            payload,
            swapped(payload, 1, 1),
            *held,
        )
        if last:
            break
        moved = shifted(moved, "cols", 1)
        gram_left, norm_upper, upper = in_vmem(
            functools.partial(upper_kernel, blocks),
            [((width, 6 * rows), jnp.bfloat16), ((1, half), F32), (whole, F32)],
            weight,
            coupling,
            scale,
            *held,
        )
        blocks, held, arriving = later_blocks, (upper, moved), swapped(moved, 1, 1)
        (payload,) = in_vmem(gram_kernel, [((width + 8, half), F32)], gram_left, norm_upper, weight, moved)
    moved = shifted(moved, "cols", 1 - STEPS)
    out_shape = jax.ShapeDtypeStruct((rows, columns), F32)
    rotated = pl.pallas_call(
        functools.partial(last_upper_kernel, blocks),
        out_shape=out_shape,
        in_specs=[ON_CHIP] * (2 + len(held)),
        out_specs=ANYWHERE,
        scratch_shapes=[pltpu.VMEM((rows, width), F32), pltpu.SemaphoreType.DMA(())],
        compiler_params=GRANT,
    )(coupling, scale, *held)
    return pl.pallas_call(
        last_lower_kernel,
        out_shape=out_shape,
        in_specs=[ON_CHIP, ANYWHERE],
        out_specs=ANYWHERE,
        scratch_shapes=[pltpu.SemaphoreType.DMA(())],
        input_output_aliases={1: 0},
        compiler_params=GRANT,
    )(moved, rotated)


def solution(mesh):
    placed = (P("pts", "cols"), P("pts"), P())
    return jax.shard_map(
        body, mesh=mesh, in_specs=placed, out_specs=P("pts", "cols"), check_vma=False
    )
```

```python
import functools

import jax
import jax.numpy as jnp
from jax import lax
from jax.experimental import pallas as pl
from jax.experimental.pallas import tpu as pltpu
from jax.sharding import PartitionSpec as P

STEPS = 3
EPSILON = 1e-06
F32 = jnp.float32


def shifted(value, axis, steps):
    count = lax.axis_size(axis)
    pairs = [(source, (source + steps) % count) for source in range(count)]
    return lax.ppermute(value, axis, pairs)


def swapped(value, even_bits, odd_bits):
    count = lax.axis_size("pts")
    pairs = [(source, source ^ (odd_bits if source % 2 else even_bits)) for source in range(count)]
    return lax.ppermute(value, "pts", pairs)


def chip_sum(value, beside=None):
    count = lax.axis_size("pts")
    bit = 2
    while bit < count:
        if 2 * bit < count:
            rounds = [(bit, 2 * bit), (2 * bit, bit)]
        else:
            rounds = [(bit, bit)]
        for even_bits, odd_bits in rounds:
            value = value + swapped(value, even_bits, odd_bits)
            if beside is not None:
                value, beside = lax.optimization_barrier((value, beside))
        bit *= 2 ** len(rounds)
    return value, beside


def two_parts(value):
    high = value.astype(jnp.bfloat16)
    return high, (value - high.astype(F32)).astype(jnp.bfloat16)


def as_left(value):
    high, low = two_parts(value)
    return jnp.concatenate([high, high, low], axis=1)


def as_right(value):
    high, low = two_parts(value)
    return jnp.concatenate([high, low, high], axis=0)


def product(left, right):
    return jnp.dot(left, right, preferred_element_type=F32)


def product_tl(left, right):
    high, low = two_parts(left)
    return lax.dot_general(
        jnp.concatenate([high, high, low], axis=0),
        right,
        (((0,), (0,)), ((), ())),
        preferred_element_type=F32,
    )


def product_bt(left, right):
    high, low = two_parts(right)
    return lax.dot_general(
        as_left(left),
        jnp.concatenate([high, low, high], axis=1),
        (((1,), (1,)), ((), ())),
        preferred_element_type=F32,
    )


def halves_swapped(value):
    half = value.shape[0] // 2
    return jnp.concatenate([value[half:], value[:half]], axis=0)


def unit(width):
    rows = lax.broadcasted_iota(jnp.int32, (width, width), 0)
    columns = lax.broadcasted_iota(jnp.int32, (width, width), 1)
    return jnp.where(rows == columns, 1.0, 0.0).astype(F32)


def times_inverse_root(left, square, scale, columns):
    identity = unit(square.shape[0])
    base = (identity + square) * (1.0 / scale)
    base_right = as_right(base)
    left_parts = as_left(left)
    second = product(as_left(base), base_right)
    left_base = product(left_parts, base_right)
    first_square = 2.25 * identity - 1.5 * base + 0.25 * second
    both = 2.25 * identity - 0.75 * base
    both = both - 0.5 * product(as_left(1.5 * base - 0.5 * second), as_right(first_square))
    both_right = as_right(both)
    both_square = product(as_left(both), both_right[:, :columns])
    left_both = product(left_parts, both_right[:, :columns])
    left_cubic = product(as_left(product(as_left(left_base), both_right)), as_right(both_square))
    return (1.5 * left_both - 0.5 * left_cubic) * lax.rsqrt(scale)


def joined(own, other):
    return jnp.concatenate([own, halves_swapped(other)], axis=1)


def own_half(half):
    own = (lax.axis_index("pts") % 2) * half
    return pl.multiple_of(own, half), pl.multiple_of(half - own, half)


def start_blocks(near, far):
    width = near.shape[1] // 2
    own, other = own_half(width // 2)

    def taken(start):
        piece = (slice(None), pl.ds(start, width // 2))
        return jnp.concatenate([near[piece], far[piece]], axis=0)

    upper = jnp.concatenate([taken(own), taken(other)], axis=1)
    return upper, jnp.concatenate([taken(width + own), taken(width + other)], axis=1)


def later_blocks(upper, own, other):
    return upper[...], joined(own[...], other[...])


def stored(ref, value):
    half = ref.shape[1] // 2
    own, other = own_half(half)
    ref[:, pl.ds(own, half)] = value[:, :half]
    ref[:, pl.ds(other, half)] = value[:, half:]


def start_kernel(near_ref, weight_ref, own_part, other_part, near, weight, near_sent, weight_sent):
    copies = [
        pltpu.make_async_copy(near_ref, near, near_sent),
        pltpu.make_async_copy(weight_ref, weight, weight_sent),
    ]
    for copy in copies:
        copy.start()
    for copy in copies:
        copy.wait()
    width = near.shape[1] // 2
    half = width // 2
    own, other = own_half(half)
    point_weight = jnp.broadcast_to(weight[...], (8, weight.shape[1])).T[:, 0:1]
    upper_own, upper_other = near[:, pl.ds(own, half)], near[:, pl.ds(other, half)]
    upper = jnp.concatenate([upper_own, upper_other], axis=1)
    rows = lax.broadcasted_iota(jnp.int32, (8, half), 0)
    for start, norm_of, out in ((own, upper_own, own_part), (other, upper_other, other_part)):
        lower = near[:, pl.ds(width + start, half)]
        weighted = point_weight * lower
        gram = product_tl(upper, as_right(weighted))
        out[:width] = gram if out is own_part else halves_swapped(gram)
        norm_lower = jnp.sum(weighted * lower, axis=0, keepdims=True)
        norm_upper = jnp.sum(point_weight * norm_of * norm_of, axis=0, keepdims=True)
        out[width:] = jnp.where(rows == 0, norm_lower, jnp.where(rows == 1, norm_upper, 0.0))


def lower_kernel(blocks, step, last, damps, own_sum, other_sum, *refs):
    *block_refs, moved, coupling_out, scale_out = refs
    width = coupling_out.shape[0]
    upper, lower = blocks(*block_refs)
    gram = joined(own_sum[:width], other_sum[:width])
    norms = jnp.concatenate([own_sum[width:], other_sum[width:]], axis=1)
    inverse = lax.rsqrt(norms + EPSILON)
    coupling = gram * (damps[step : step + 1, 0:1] * inverse.T[:, 1:2]) * inverse[0:1]
    scale = 1.0 + jnp.sum(coupling * coupling, keepdims=True)
    coupling_out[...] = coupling
    scale_out[...] = jnp.broadcast_to(scale, scale_out.shape)
    coupling_right = as_right(coupling)
    square = product_tl(coupling, coupling_right)
    rows, columns = moved.shape
    mixed = lower[:rows] + product(as_left(upper[:rows]), coupling_right)
    result = times_inverse_root(mixed, square, scale, columns)
    if last:
        stored(moved, result)
    else:
        moved[...] = result


def rotated_upper(blocks, rows, coupling_ref, scale_ref, *block_refs):
    coupling = coupling_ref[...]
    upper, lower = blocks(*block_refs)
    mixed = upper[:rows] - product_bt(lower[:rows], coupling)
    square = product_bt(coupling, coupling)
    return times_inverse_root(mixed, square, scale_ref[0:1, 0:1], coupling.shape[1])


def upper_kernel(blocks, weight, *refs):
    *ins, gram_left, norm_out, upper_out = refs
    upper = rotated_upper(blocks, upper_out.shape[0], *ins)
    upper_out[...] = upper
    weighted = weight[...] * upper
    norm_out[...] = jnp.sum(weighted * upper, axis=0, keepdims=True)[:, : norm_out.shape[1]]
    gram_left[...] = as_left(weighted.T)


def last_upper_kernel(blocks, *refs):
    *ins, out, held, sent = refs
    stored(held, rotated_upper(blocks, held.shape[0], *ins))
    copy = pltpu.make_async_copy(held, out.at[:, pl.ds(0, held.shape[1])], sent)
    copy.start()
    copy.wait()


def last_lower_kernel(lower, filled, out, sent):
    del filled
    width = lower.shape[1]
    copy = pltpu.make_async_copy(lower, out.at[:, pl.ds(width, width)], sent)
    copy.start()
    copy.wait()


def gram_kernel(gram_left, norm_upper, weight, own_ref, payload):
    width = gram_left.shape[0]
    own = own_ref[...]
    payload[:width] = product(gram_left[...], as_right(own))
    norm_lower = jnp.sum(weight[...] * own * own, axis=0, keepdims=True)
    rows = lax.broadcasted_iota(jnp.int32, (8, own.shape[1]), 0)
    payload[width:] = jnp.where(rows == 0, norm_lower, jnp.where(rows == 1, norm_upper[...], 0.0))


ON_CHIP = pl.BlockSpec(memory_space=pltpu.VMEM)
ANYWHERE = pl.BlockSpec(memory_space=pl.ANY)
GRANT = pltpu.CompilerParams(vmem_limit_bytes=24 << 20)


def in_vmem(kernel, outs, *args):
    return pl.pallas_call(
        kernel,
        out_shape=[jax.ShapeDtypeStruct(shape, dtype) for shape, dtype in outs],
        in_specs=[ON_CHIP] * len(args),
        out_specs=[ON_CHIP] * len(outs),
        compiler_params=GRANT,
    )(*args)


def body(snapshot, weights, damping):
    rows, columns = snapshot.shape
    width = columns // 2
    half = width // 2
    whole = (2 * rows, width)
    own_part, other_part = pl.pallas_call(
        start_kernel,
        out_shape=[jax.ShapeDtypeStruct((width + 8, half), F32)] * 2,
        in_specs=[ANYWHERE] * 2,
        out_specs=[ON_CHIP] * 2,
        scratch_shapes=[
            pltpu.VMEM((rows, columns), F32),
            pltpu.VMEM((1, rows), F32),
            pltpu.SemaphoreType.DMA(()),
            pltpu.SemaphoreType.DMA(()),
        ],
        compiler_params=GRANT,
    )(snapshot, weights[None])
    payload = own_part + swapped(other_part, 1, 1)
    weight = jnp.concatenate([weights, swapped(weights, 1, 1)])[:, None]
    blocks, held, arriving = start_blocks, (snapshot,), swapped(snapshot, 1, 1)
    damps = damping[:, 0].astype(F32) / (damping[:, 0] + damping[:, 1]).astype(F32)
    damps = lax.optimization_barrier(jnp.broadcast_to(damps[:, None], (STEPS, 128)))
    for step in range(STEPS):
        last = step + 1 == STEPS
        payload, arriving = chip_sum(payload, arriving)
        held = held + (arriving,)
        moved, coupling, scale = in_vmem(
            functools.partial(lower_kernel, blocks, step, last),
            [((rows, width) if last else (2 * rows, half), F32), ((width, width), F32), ((8, 128), F32)],
            damps,
            payload,
            swapped(payload, 1, 1),
            *held,
        )
        if last:
            break
        moved = shifted(moved, "cols", 1)
        gram_left, norm_upper, upper = in_vmem(
            functools.partial(upper_kernel, blocks),
            [((width, 6 * rows), jnp.bfloat16), ((1, half), F32), (whole, F32)],
            weight,
            coupling,
            scale,
            *held,
        )
        blocks, held, arriving = later_blocks, (upper, moved), swapped(moved, 1, 1)
        (payload,) = in_vmem(gram_kernel, [((width + 8, half), F32)], gram_left, norm_upper, weight, moved)
    moved = shifted(moved, "cols", 1 - STEPS)
    out_shape = jax.ShapeDtypeStruct((rows, columns), F32)
    rotated = pl.pallas_call(
        functools.partial(last_upper_kernel, blocks),
        out_shape=out_shape,
        in_specs=[ON_CHIP] * (2 + len(held)),
        out_specs=ANYWHERE,
        scratch_shapes=[pltpu.VMEM((rows, width), F32), pltpu.SemaphoreType.DMA(())],
        compiler_params=GRANT,
    )(coupling, scale, *held)
    return pl.pallas_call(
        last_lower_kernel,
        out_shape=out_shape,
        in_specs=[ON_CHIP, ANYWHERE],
        out_specs=ANYWHERE,
        scratch_shapes=[pltpu.SemaphoreType.DMA(())],
        input_output_aliases={1: 0},
        compiler_params=GRANT,
    )(moved, rotated)


def solution(mesh):
    placed = (P("pts", "cols"), P("pts"), P())
    return jax.shard_map(
        body, mesh=mesh, in_specs=placed, out_specs=P("pts", "cols"), check_vma=False
    )
```

```python
import functools

import jax
import jax.numpy as jnp
from jax import lax
from jax.experimental import pallas as pl
from jax.experimental.pallas import tpu as pltpu
from jax.sharding import PartitionSpec as P

STEPS = 3
EPSILON = 1e-06
F32 = jnp.float32


def shifted(value, axis, steps):
    count = lax.axis_size(axis)
    pairs = [(source, (source + steps) % count) for source in range(count)]
    return lax.ppermute(value, axis, pairs)


def swapped(value, even_bits, odd_bits):
    count = lax.axis_size("pts")
    pairs = [(source, source ^ (odd_bits if source % 2 else even_bits)) for source in range(count)]
    return lax.ppermute(value, "pts", pairs)


def chip_sum(value, beside=None):
    count = lax.axis_size("pts")
    bit = 2
    while bit < count:
        if 2 * bit < count:
            rounds = [(bit, 2 * bit), (2 * bit, bit)]
        else:
            rounds = [(bit, bit)]
        for even_bits, odd_bits in rounds:
            value = value + swapped(value, even_bits, odd_bits)
            if beside is not None:
                value, beside = lax.optimization_barrier((value, beside))
        bit *= 2 ** len(rounds)
    return value, beside


def two_parts(value):
    high = value.astype(jnp.bfloat16)
    return high, (value - high.astype(F32)).astype(jnp.bfloat16)


def as_left(value):
    high, low = two_parts(value)
    return jnp.concatenate([high, high, low], axis=1)


def as_right(value):
    high, low = two_parts(value)
    return jnp.concatenate([high, low, high], axis=0)


def product(left, right):
    return jnp.dot(left, right, preferred_element_type=F32)


def product_tl(left, right):
    high, low = two_parts(left)
    return lax.dot_general(
        jnp.concatenate([high, high, low], axis=0),
        right,
        (((0,), (0,)), ((), ())),
        preferred_element_type=F32,
    )


def product_bt(left, right):
    high, low = two_parts(right)
    return lax.dot_general(
        as_left(left),
        jnp.concatenate([high, low, high], axis=1),
        (((1,), (1,)), ((), ())),
        preferred_element_type=F32,
    )


def halves_swapped(value):
    half = value.shape[0] // 2
    return jnp.concatenate([value[half:], value[:half]], axis=0)


def unit(width):
    rows = lax.broadcasted_iota(jnp.int32, (width, width), 0)
    columns = lax.broadcasted_iota(jnp.int32, (width, width), 1)
    return jnp.where(rows == columns, 1.0, 0.0).astype(F32)


def times_inverse_root(left, square, scale, columns):
    identity = unit(square.shape[0])
    base = (identity + square) * (1.0 / scale)
    base_right = as_right(base)
    left_parts = as_left(left)
    second = product(as_left(base), base_right)
    left_base = product(left_parts, base_right)
    first_square = 2.25 * identity - 1.5 * base + 0.25 * second
    both = 2.25 * identity - 0.75 * base
    both = both - 0.5 * product(as_left(1.5 * base - 0.5 * second), as_right(first_square))
    both_right = as_right(both)
    both_square = product(as_left(both), both_right[:, :columns])
    left_both = product(left_parts, both_right[:, :columns])
    left_cubic = product(as_left(product(as_left(left_base), both_right)), as_right(both_square))
    return (1.5 * left_both - 0.5 * left_cubic) * lax.rsqrt(scale)


def joined(own, other):
    return jnp.concatenate([own, halves_swapped(other)], axis=1)


def own_half(half):
    own = (lax.axis_index("pts") % 2) * half
    return pl.multiple_of(own, half), pl.multiple_of(half - own, half)


def start_blocks(near, far):
    width = near.shape[1] // 2
    own, other = own_half(width // 2)

    def taken(start):
        piece = (slice(None), pl.ds(start, width // 2))
        return jnp.concatenate([near[piece], far[piece]], axis=0)

    upper = jnp.concatenate([taken(own), taken(other)], axis=1)
    return upper, jnp.concatenate([taken(width + own), taken(width + other)], axis=1)


def later_blocks(upper, own, other):
    return upper[...], joined(own[...], other[...])


def stored(ref, value):
    half = ref.shape[1] // 2
    own, other = own_half(half)
    ref[:, pl.ds(own, half)] = value[:, :half]
    ref[:, pl.ds(other, half)] = value[:, half:]


def start_kernel(near_ref, weight_ref, own_part, other_part, near, weight, near_sent, weight_sent):
    copies = [
        pltpu.make_async_copy(near_ref, near, near_sent),
        pltpu.make_async_copy(weight_ref, weight, weight_sent),
    ]
    for copy in copies:
        copy.start()
    for copy in copies:
        copy.wait()
    width = near.shape[1] // 2
    half = width // 2
    own, other = own_half(half)
    point_weight = jnp.broadcast_to(weight[...], (8, weight.shape[1])).T[:, 0:1]
    upper_own, upper_other = near[:, pl.ds(own, half)], near[:, pl.ds(other, half)]
    upper = jnp.concatenate([upper_own, upper_other], axis=1)
    rows = lax.broadcasted_iota(jnp.int32, (8, half), 0)
    for start, norm_of, out in ((own, upper_own, own_part), (other, upper_other, other_part)):
        lower = near[:, pl.ds(width + start, half)]
        weighted = point_weight * lower
        gram = product_tl(upper, as_right(weighted))
        out[:width] = gram if out is own_part else halves_swapped(gram)
        norm_lower = jnp.sum(weighted * lower, axis=0, keepdims=True)
        norm_upper = jnp.sum(point_weight * norm_of * norm_of, axis=0, keepdims=True)
        out[width:] = jnp.where(rows == 0, norm_lower, jnp.where(rows == 1, norm_upper, 0.0))


def lower_kernel(blocks, step, last, damps, own_sum, other_sum, *refs):
    *block_refs, moved, coupling_out, scale_out = refs
    width = coupling_out.shape[0]
    upper, lower = blocks(*block_refs)
    gram = joined(own_sum[:width], other_sum[:width])
    norms = jnp.concatenate([own_sum[width:], other_sum[width:]], axis=1)
    inverse = lax.rsqrt(norms + EPSILON)
    coupling = gram * (damps[step : step + 1, 0:1] * inverse.T[:, 1:2]) * inverse[0:1]
    scale = 1.0 + jnp.sum(coupling * coupling, keepdims=True)
    coupling_out[...] = coupling
    scale_out[...] = jnp.broadcast_to(scale, scale_out.shape)
    coupling_right = as_right(coupling)
    square = product_tl(coupling, coupling_right)
    rows, columns = moved.shape
    mixed = lower[:rows] + product(as_left(upper[:rows]), coupling_right)
    result = times_inverse_root(mixed, square, scale, columns)
    if last:
        stored(moved, result)
    else:
        moved[...] = result


def rotated_upper(blocks, rows, coupling_ref, scale_ref, *block_refs):
    coupling = coupling_ref[...]
    upper, lower = blocks(*block_refs)
    mixed = upper[:rows] - product_bt(lower[:rows], coupling)
    square = product_bt(coupling, coupling)
    return times_inverse_root(mixed, square, scale_ref[0:1, 0:1], coupling.shape[1])


def upper_kernel(blocks, weight, *refs):
    *ins, gram_left, norm_out, upper_out = refs
    upper = rotated_upper(blocks, upper_out.shape[0], *ins)
    upper_out[...] = upper
    weighted = weight[...] * upper
    norm_out[...] = jnp.sum(weighted * upper, axis=0, keepdims=True)[:, : norm_out.shape[1]]
    gram_left[...] = as_left(weighted.T)


def last_upper_kernel(blocks, *refs):
    *ins, out, held, sent = refs
    stored(held, rotated_upper(blocks, held.shape[0], *ins))
    copy = pltpu.make_async_copy(held, out.at[:, pl.ds(0, held.shape[1])], sent)
    copy.start()
    copy.wait()


def last_lower_kernel(lower, filled, out, sent):
    del filled
    width = lower.shape[1]
    copy = pltpu.make_async_copy(lower, out.at[:, pl.ds(width, width)], sent)
    copy.start()
    copy.wait()


def gram_kernel(gram_left, norm_upper, weight, own_ref, payload):
    width = gram_left.shape[0]
    own = own_ref[...]
    payload[:width] = product(gram_left[...], as_right(own))
    norm_lower = jnp.sum(weight[...] * own * own, axis=0, keepdims=True)
    rows = lax.broadcasted_iota(jnp.int32, (8, own.shape[1]), 0)
    payload[width:] = jnp.where(rows == 0, norm_lower, jnp.where(rows == 1, norm_upper[...], 0.0))


ON_CHIP = pl.BlockSpec(memory_space=pltpu.VMEM)
ANYWHERE = pl.BlockSpec(memory_space=pl.ANY)
GRANT = pltpu.CompilerParams(vmem_limit_bytes=24 << 20)


def in_vmem(kernel, outs, *args):
    return pl.pallas_call(
        kernel,
        out_shape=[jax.ShapeDtypeStruct(shape, dtype) for shape, dtype in outs],
        in_specs=[ON_CHIP] * len(args),
        out_specs=[ON_CHIP] * len(outs),
        compiler_params=GRANT,
    )(*args)


def body(snapshot, weights, damping):
    rows, columns = snapshot.shape
    width = columns // 2
    half = width // 2
    whole = (2 * rows, width)
    own_part, other_part = pl.pallas_call(
        start_kernel,
        out_shape=[jax.ShapeDtypeStruct((width + 8, half), F32)] * 2,
        in_specs=[pl.BlockSpec(memory_space=pltpu.HBM)] * 2,
        out_specs=[ON_CHIP] * 2,
        scratch_shapes=[
            pltpu.VMEM((rows, columns), F32),
            pltpu.VMEM((1, rows), F32),
            pltpu.SemaphoreType.DMA(()),
            pltpu.SemaphoreType.DMA(()),
        ],
        compiler_params=pltpu.CompilerParams(vmem_limit_bytes=(64 << 20) - (10752 << 10)),
    )(snapshot, weights[None])
    payload = own_part + swapped(other_part, 1, 1)
    weight = jnp.concatenate([weights, swapped(weights, 1, 1)])[:, None]
    blocks, held, arriving = start_blocks, (snapshot,), swapped(snapshot, 1, 1)
    damps = damping[:, 0].astype(F32) / (damping[:, 0] + damping[:, 1]).astype(F32)
    damps = lax.optimization_barrier(jnp.broadcast_to(damps[:, None], (STEPS, 128)))
    for step in range(STEPS):
        last = step + 1 == STEPS
        payload, arriving = chip_sum(payload, arriving)
        held = held + (arriving,)
        moved, coupling, scale = in_vmem(
            functools.partial(lower_kernel, blocks, step, last),
            [((rows, width) if last else (2 * rows, half), F32), ((width, width), F32), ((8, 128), F32)],
            damps,
            payload,
            swapped(payload, 1, 1),
            *held,
        )
        if last:
            break
        moved = shifted(moved, "cols", 1)
        gram_left, norm_upper, upper = in_vmem(
            functools.partial(upper_kernel, blocks),
            [((width, 6 * rows), jnp.bfloat16), ((1, half), F32), (whole, F32)],
            weight,
            coupling,
            scale,
            *held,
        )
        blocks, held, arriving = later_blocks, (upper, moved), swapped(moved, 1, 1)
        (payload,) = in_vmem(gram_kernel, [((width + 8, half), F32)], gram_left, norm_upper, weight, moved)
    moved = shifted(moved, "cols", 1 - STEPS)
    out_shape = jax.ShapeDtypeStruct((rows, columns), F32)
    rotated = pl.pallas_call(
        functools.partial(last_upper_kernel, blocks),
        out_shape=out_shape,
        in_specs=[ON_CHIP] * (2 + len(held)),
        out_specs=ANYWHERE,
        scratch_shapes=[pltpu.VMEM((rows, width), F32), pltpu.SemaphoreType.DMA(())],
        compiler_params=GRANT,
    )(coupling, scale, *held)
    return pl.pallas_call(
        last_lower_kernel,
        out_shape=out_shape,
        in_specs=[ON_CHIP, ANYWHERE],
        out_specs=ANYWHERE,
        scratch_shapes=[pltpu.SemaphoreType.DMA(())],
        input_output_aliases={1: 0},
        compiler_params=GRANT,
    )(moved, rotated)


def solution(mesh):
    placed = (P("pts", "cols"), P("pts"), P())
    return jax.shard_map(
        body, mesh=mesh, in_specs=placed, out_specs=P("pts", "cols"), check_vma=False
    )
```

```python
import functools

import jax
import jax.numpy as jnp
from jax import lax
from jax.experimental import pallas as pl
from jax.experimental.pallas import tpu as pltpu
from jax.sharding import PartitionSpec as P

STEPS = 3
EPSILON = 1e-06
F32 = jnp.float32


def shifted(value, axis, steps):
    count = lax.axis_size(axis)
    pairs = [(source, (source + steps) % count) for source in range(count)]
    return lax.ppermute(value, axis, pairs)


def swapped(value, even_bits, odd_bits):
    count = lax.axis_size("pts")
    pairs = [(source, source ^ (odd_bits if source % 2 else even_bits)) for source in range(count)]
    return lax.ppermute(value, "pts", pairs)


def chip_sum(value, beside=None):
    count = lax.axis_size("pts")
    bit = 2
    while bit < count:
        if 2 * bit < count:
            rounds = [(bit, 2 * bit), (2 * bit, bit)]
        else:
            rounds = [(bit, bit)]
        for even_bits, odd_bits in rounds:
            value = value + swapped(value, even_bits, odd_bits)
            if beside is not None:
                value, beside = lax.optimization_barrier((value, beside))
        bit *= 2 ** len(rounds)
    return value, beside


def two_parts(value):
    high = value.astype(jnp.bfloat16)
    return high, (value - high.astype(F32)).astype(jnp.bfloat16)


def first_columns(parts, columns):
    return parts[0][:, :columns], parts[1][:, :columns]


def product(left, right, left_axis=1, right_axis=0):
    return lax.dot_general(
        jnp.concatenate([left[0], left[0], left[1]], axis=left_axis),
        jnp.concatenate([right[0], right[1], right[0]], axis=right_axis),
        (((left_axis,), (right_axis,)), ((), ())),
        preferred_element_type=F32,
    )


def halves_swapped(value):
    half = value.shape[0] // 2
    return jnp.concatenate([value[half:], value[:half]], axis=0)


def times_inverse_root(left, square, scale, columns):
    rows = lax.broadcasted_iota(jnp.int32, square.shape, 0)
    identity = jnp.where(rows == lax.broadcasted_iota(jnp.int32, square.shape, 1), 1.0, 0.0)
    base = (identity + square) * (1.0 / scale)
    base_parts = two_parts(base)
    left_parts = two_parts(left)
    second = product(base_parts, base_parts)
    left_base = product(left_parts, base_parts)
    first_square = two_parts(2.25 * identity - 1.5 * base + 0.25 * second)
    cubic = product(two_parts(1.5 * base - 0.5 * second), first_square)
    both = two_parts(2.25 * identity - 0.75 * base - 0.5 * cubic)
    both_first = first_columns(both, columns)
    both_square = product(both, both_first)
    left_cubic = product(two_parts(left_base), both)
    left_both = product(left_parts, both_first)
    left_last = product(two_parts(left_cubic), two_parts(both_square))
    return (1.5 * left_both - 0.5 * left_last) * lax.rsqrt(scale)


def joined(own, other):
    return jnp.concatenate([own, halves_swapped(other)], axis=1)


def own_half(half):
    own = (lax.axis_index("pts") % 2) * half
    return pl.multiple_of(own, half), pl.multiple_of(half - own, half)


def start_blocks(near, far):
    width = near.shape[1] // 2
    own, other = own_half(width // 2)

    def taken(start):
        piece = (slice(None), pl.ds(start, width // 2))
        return jnp.concatenate([near[piece], far[piece]], axis=0)

    upper = jnp.concatenate([taken(own), taken(other)], axis=1)
    return upper, jnp.concatenate([taken(width + own), taken(width + other)], axis=1)


def later_blocks(upper, own, other):
    return upper[...], joined(own[...], other[...])


def stored(ref, value):
    half = ref.shape[1] // 2
    own, other = own_half(half)
    ref[:, pl.ds(own, half)] = value[:, :half]
    ref[:, pl.ds(other, half)] = value[:, half:]


def start_kernel(near_ref, weight_ref, own_part, other_part, near, weight, near_sent, weight_sent):
    copies = [
        pltpu.make_async_copy(near_ref, near, near_sent),
        pltpu.make_async_copy(weight_ref, weight, weight_sent),
    ]
    for copy in copies:
        copy.start()
    for copy in copies:
        copy.wait()
    width = near.shape[1] // 2
    half = width // 2
    own, other = own_half(half)
    point_weight = jnp.broadcast_to(weight[...], (8, weight.shape[1])).T[:, 0:1]
    upper_own, upper_other = near[:, pl.ds(own, half)], near[:, pl.ds(other, half)]
    upper_parts = two_parts(jnp.concatenate([upper_own, upper_other], axis=1))
    rows = lax.broadcasted_iota(jnp.int32, (8, half), 0)
    for start, norm_of, out in ((own, upper_own, own_part), (other, upper_other, other_part)):
        lower = near[:, pl.ds(width + start, half)]
        weighted = point_weight * lower
        gram = product(upper_parts, two_parts(weighted), 0, 0)
        out[:width] = gram if out is own_part else halves_swapped(gram)
        norm_lower = jnp.sum(weighted * lower, axis=0, keepdims=True)
        norm_upper = jnp.sum(point_weight * norm_of * norm_of, axis=0, keepdims=True)
        out[width:] = jnp.where(rows == 0, norm_lower, jnp.where(rows == 1, norm_upper, 0.0))


def lower_kernel(blocks, step, last, damps, own_sum, other_sum, *refs):
    *block_refs, moved, coupling_out, scale_out = refs
    width = coupling_out.shape[0]
    upper, lower = blocks(*block_refs)
    gram = joined(own_sum[:width], other_sum[:width])
    norms = jnp.concatenate([own_sum[width:], other_sum[width:]], axis=1)
    inverse = lax.rsqrt(norms + EPSILON)
    coupling = gram * (damps[step : step + 1, 0:1] * inverse.T[:, 1:2]) * inverse[0:1]
    scale = 1.0 + jnp.sum(coupling * coupling, keepdims=True)
    coupling_out[...] = coupling
    scale_out[...] = jnp.broadcast_to(scale, scale_out.shape)
    parts = two_parts(coupling)
    square = product(parts, parts, 0, 0)
    rows, columns = moved.shape
    mixed = lower[:rows] + product(two_parts(upper[:rows]), parts)
    result = times_inverse_root(mixed, square, scale, columns)
    if last:
        stored(moved, result)
    else:
        moved[...] = result


def rotated_upper(blocks, rows, coupling_ref, scale_ref, *block_refs):
    coupling = coupling_ref[...]
    upper, lower = blocks(*block_refs)
    parts = two_parts(coupling)
    mixed = upper[:rows] - product(two_parts(lower[:rows]), parts, 1, 1)
    square = product(parts, parts, 1, 1)
    return times_inverse_root(mixed, square, scale_ref[0:1, 0:1], coupling.shape[1])


def upper_kernel(blocks, weight, *refs):
    *ins, gram_left, norm_out, upper_out = refs
    upper = rotated_upper(blocks, upper_out.shape[0], *ins)
    upper_out[...] = upper
    weighted = weight[...] * upper
    norm_out[...] = jnp.sum(weighted * upper, axis=0, keepdims=True)[:, : norm_out.shape[1]]
    high, low = two_parts(weighted.T)
    gram_left[...] = jnp.concatenate([high, high, low], axis=1)


def last_upper_kernel(blocks, *refs):
    *ins, out, held, sent = refs
    stored(held, rotated_upper(blocks, held.shape[0], *ins))
    copy = pltpu.make_async_copy(held, out.at[:, pl.ds(0, held.shape[1])], sent)
    copy.start()
    copy.wait()


def last_lower_kernel(lower, filled, out, sent):
    del filled
    width = lower.shape[1]
    copy = pltpu.make_async_copy(lower, out.at[:, pl.ds(width, width)], sent)
    copy.start()
    copy.wait()


def gram_kernel(gram_left, norm_upper, weight, own_ref, payload):
    width = gram_left.shape[0]
    own = own_ref[...]
    high, low = two_parts(own)
    right = jnp.concatenate([high, low, high], axis=0)
    payload[:width] = jnp.dot(gram_left[...], right, preferred_element_type=F32)
    norm_lower = jnp.sum(weight[...] * own * own, axis=0, keepdims=True)
    rows = lax.broadcasted_iota(jnp.int32, (8, own.shape[1]), 0)
    payload[width:] = jnp.where(rows == 0, norm_lower, jnp.where(rows == 1, norm_upper[...], 0.0))


ON_CHIP = pl.BlockSpec(memory_space=pltpu.VMEM)
ANYWHERE = pl.BlockSpec(memory_space=pl.ANY)
GRANT = pltpu.CompilerParams(vmem_limit_bytes=24 << 20)


def in_vmem(kernel, outs, *args):
    return pl.pallas_call(
        kernel,
        out_shape=[jax.ShapeDtypeStruct(shape, dtype) for shape, dtype in outs],
        in_specs=[ON_CHIP] * len(args),
        out_specs=[ON_CHIP] * len(outs),
        compiler_params=GRANT,
    )(*args)


def body(snapshot, weights, damping):
    rows, columns = snapshot.shape
    width = columns // 2
    half = width // 2
    whole = (2 * rows, width)
    own_part, other_part = pl.pallas_call(
        start_kernel,
        out_shape=[jax.ShapeDtypeStruct((width + 8, half), F32)] * 2,
        in_specs=[pl.BlockSpec(memory_space=pltpu.HBM)] * 2,
        out_specs=[ON_CHIP] * 2,
        scratch_shapes=[
            pltpu.VMEM((rows, columns), F32),
            pltpu.VMEM((1, rows), F32),
            pltpu.SemaphoreType.DMA(()),
            pltpu.SemaphoreType.DMA(()),
        ],
        compiler_params=pltpu.CompilerParams(vmem_limit_bytes=(64 << 20) - (10752 << 10)),
    )(snapshot, weights[None])
    own_part, other_part, damping = lax.optimization_barrier((own_part, other_part, damping))
    payload = own_part + swapped(other_part, 1, 1)
    weight = jnp.concatenate([weights, swapped(weights, 1, 1)])[:, None]
    blocks, held, arriving = start_blocks, (snapshot,), swapped(snapshot, 1, 1)
    damps = damping[:, 0].astype(F32) / (damping[:, 0] + damping[:, 1]).astype(F32)
    damps = lax.optimization_barrier(jnp.broadcast_to(damps[:, None], (STEPS, 128)))
    for step in range(STEPS):
        last = step + 1 == STEPS
        payload, arriving = chip_sum(payload, arriving)
        held = held + (arriving,)
        moved, coupling, scale = in_vmem(
            functools.partial(lower_kernel, blocks, step, last),
            [((rows, width) if last else (2 * rows, half), F32), ((width, width), F32), ((8, 128), F32)],
            damps,
            payload,
            swapped(payload, 1, 1),
            *held,
        )
        if last:
            break
        moved = shifted(moved, "cols", 1)
        gram_left, norm_upper, upper = in_vmem(
            functools.partial(upper_kernel, blocks),
            [((width, 6 * rows), jnp.bfloat16), ((1, half), F32), (whole, F32)],
            weight,
            coupling,
            scale,
            *held,
        )
        blocks, held, arriving = later_blocks, (upper, moved), swapped(moved, 1, 1)
        (payload,) = in_vmem(gram_kernel, [((width + 8, half), F32)], gram_left, norm_upper, weight, moved)
    moved = shifted(moved, "cols", 1 - STEPS)
    out_shape = jax.ShapeDtypeStruct((rows, columns), F32)
    rotated = pl.pallas_call(
        functools.partial(last_upper_kernel, blocks),
        out_shape=out_shape,
        in_specs=[ON_CHIP] * (2 + len(held)),
        out_specs=ANYWHERE,
        scratch_shapes=[pltpu.VMEM((rows, width), F32), pltpu.SemaphoreType.DMA(())],
        compiler_params=GRANT,
    )(coupling, scale, *held)
    return pl.pallas_call(
        last_lower_kernel,
        out_shape=out_shape,
        in_specs=[ON_CHIP, ANYWHERE],
        out_specs=ANYWHERE,
        scratch_shapes=[pltpu.SemaphoreType.DMA(())],
        input_output_aliases={1: 0},
        compiler_params=GRANT,
    )(moved, rotated)


def solution(mesh):
    placed = (P("pts", "cols"), P("pts"), P())
    return jax.shard_map(
        body, mesh=mesh, in_specs=placed, out_specs=P("pts", "cols"), check_vma=False
    )
```

```python
import functools

import jax
import jax.numpy as jnp
from jax import lax
from jax.experimental import pallas as pl
from jax.experimental.pallas import tpu as pltpu
from jax.sharding import PartitionSpec as P

STEPS = 3
EPSILON = 1e-06
F32 = jnp.float32


def shifted(value, axis, steps):
    count = lax.axis_size(axis)
    pairs = [(source, (source + steps) % count) for source in range(count)]
    return lax.ppermute(value, axis, pairs)


def swapped(value, even_bits, odd_bits):
    count = lax.axis_size("pts")
    pairs = [(source, source ^ (odd_bits if source % 2 else even_bits)) for source in range(count)]
    return lax.ppermute(value, "pts", pairs)


def chip_sum(value, bit, beside):
    count = lax.axis_size("pts")
    while bit < count:
        if 2 * bit < count:
            rounds = [(bit, 2 * bit), (2 * bit, bit)]
        else:
            rounds = [(bit, bit)]
        for even_bits, odd_bits in rounds:
            value = value + swapped(value, even_bits, odd_bits)
            value, beside = lax.optimization_barrier((value, beside))
        bit *= 2 ** len(rounds)
    return value, beside


def two_parts(value):
    high = value.astype(jnp.bfloat16)
    return high, (value - high.astype(F32)).astype(jnp.bfloat16)


def first_columns(parts, columns):
    return parts[0][:, :columns], parts[1][:, :columns]


def product(left, right, left_axis=1, right_axis=0):
    return lax.dot_general(
        jnp.concatenate([left[0], left[0], left[1]], axis=left_axis),
        jnp.concatenate([right[0], right[1], right[0]], axis=right_axis),
        (((left_axis,), (right_axis,)), ((), ())),
        preferred_element_type=F32,
    )


def neighbours_swapped(value, block):
    count = value.shape[0] // block
    return jnp.concatenate([value[(i ^ 1) * block : ((i ^ 1) + 1) * block] for i in range(count)], axis=0)


def times_inverse_root(left, square, scale, columns):
    rows = lax.broadcasted_iota(jnp.int32, square.shape, 0)
    identity = jnp.where(rows == lax.broadcasted_iota(jnp.int32, square.shape, 1), 1.0, 0.0)
    base = (identity + square) * (1.0 / scale)
    base_parts = two_parts(base)
    left_parts = two_parts(left)
    second = product(base_parts, base_parts)
    left_base = product(left_parts, base_parts)
    first_square = two_parts(2.25 * identity - 1.5 * base + 0.25 * second)
    cubic = product(two_parts(1.5 * base - 0.5 * second), first_square)
    both = two_parts(2.25 * identity - 0.75 * base - 0.5 * cubic)
    both_first = first_columns(both, columns)
    both_square = product(both, both_first)
    left_cubic = product(two_parts(left_base), both)
    left_both = product(left_parts, both_first)
    left_last = product(two_parts(left_cubic), two_parts(both_square))
    return (1.5 * left_both - 0.5 * left_last) * lax.rsqrt(scale)


def joined(own, other, block):
    return jnp.concatenate([own, neighbours_swapped(other, block)], axis=1)


def own_half(half):
    own = (lax.axis_index("pts") % 2) * half
    return pl.multiple_of(own, half), pl.multiple_of(half - own, half)


def start_blocks(*pieces):
    width = pieces[0].shape[1] // 2
    own, other = own_half(width // 2)

    def taken(start):
        piece = (slice(None), pl.ds(start, width // 2))
        return jnp.concatenate([ref[piece] for ref in pieces], axis=0)

    upper = jnp.concatenate([taken(own), taken(other)], axis=1)
    return upper, jnp.concatenate([taken(width + own), taken(width + other)], axis=1)


def later_blocks(block, upper, own, other):
    return upper[...], joined(own[...], other[...], block)


def stored(ref, value):
    half = ref.shape[1] // 2
    own, other = own_half(half)
    ref[:, pl.ds(own, half)] = value[:, :half]
    ref[:, pl.ds(other, half)] = value[:, half:]


def start_kernel(near_ref, weight_ref, own_part, other_part, near, weight, near_sent, weight_sent):
    copies = [
        pltpu.make_async_copy(near_ref, near, near_sent),
        pltpu.make_async_copy(weight_ref, weight, weight_sent),
    ]
    for copy in copies:
        copy.start()
    for copy in copies:
        copy.wait()
    width = near.shape[1] // 2
    half = width // 2
    own, other = own_half(half)
    point_weight = jnp.broadcast_to(weight[...], (8, weight.shape[1])).T[:, 0:1]
    upper_own, upper_other = near[:, pl.ds(own, half)], near[:, pl.ds(other, half)]
    upper_parts = two_parts(jnp.concatenate([upper_own, upper_other], axis=1))
    rows = lax.broadcasted_iota(jnp.int32, (8, half), 0)
    for start, norm_of, out in ((own, upper_own, own_part), (other, upper_other, other_part)):
        lower = near[:, pl.ds(width + start, half)]
        weighted = point_weight * lower
        gram = product(upper_parts, two_parts(weighted), 0, 0)
        out[:width] = gram if out is own_part else neighbours_swapped(gram, half)
        norm_lower = jnp.sum(weighted * lower, axis=0, keepdims=True)
        norm_upper = jnp.sum(point_weight * norm_of * norm_of, axis=0, keepdims=True)
        out[width:] = jnp.where(rows == 0, norm_lower, jnp.where(rows == 1, norm_upper, 0.0))


def lower_kernel(blocks, step, last, damps, own_sum, other_sum, *refs):
    *block_refs, moved, coupling_out, scale_out = refs
    width = coupling_out.shape[0]
    upper, lower = blocks(*block_refs)
    gram = joined(own_sum[:width], other_sum[:width], width // 2)
    norms = jnp.concatenate([own_sum[width:], other_sum[width:]], axis=1)
    inverse = lax.rsqrt(norms + EPSILON)
    coupling = gram * (damps[step : step + 1, 0:1] * inverse.T[:, 1:2]) * inverse[0:1]
    scale = 1.0 + jnp.sum(coupling * coupling, keepdims=True)
    coupling_out[...] = coupling
    scale_out[...] = jnp.broadcast_to(scale, scale_out.shape)
    parts = two_parts(coupling)
    square = product(parts, parts, 0, 0)
    rows, columns = moved.shape
    mixed = lower[:rows] + product(two_parts(upper[:rows]), parts)
    result = times_inverse_root(mixed, square, scale, columns)
    if last:
        stored(moved, result)
    else:
        moved[...] = result


def rotated_upper(blocks, rows, coupling_ref, scale_ref, *block_refs):
    coupling = coupling_ref[...]
    upper, lower = blocks(*block_refs)
    parts = two_parts(coupling)
    mixed = upper[:rows] - product(two_parts(lower[:rows]), parts, 1, 1)
    square = product(parts, parts, 1, 1)
    return times_inverse_root(mixed, square, scale_ref[0:1, 0:1], coupling.shape[1])


def upper_kernel(blocks, weight, *refs):
    *ins, gram_left, norm_out, upper_out = refs
    upper = rotated_upper(blocks, upper_out.shape[0], *ins)
    upper_out[...] = upper
    weighted = weight[...] * upper
    norm_out[...] = jnp.sum(weighted * upper, axis=0, keepdims=True)[:, : norm_out.shape[1]]
    high, low = two_parts(weighted.T)
    gram_left[...] = jnp.concatenate([high, high, low], axis=1)


def last_upper_kernel(blocks, *refs):
    *ins, out, held, sent = refs
    stored(held, rotated_upper(blocks, held.shape[0], *ins))
    copy = pltpu.make_async_copy(held, out.at[:, pl.ds(0, held.shape[1])], sent)
    copy.start()
    copy.wait()


def last_lower_kernel(lower, filled, out, sent):
    del filled
    width = lower.shape[1]
    copy = pltpu.make_async_copy(lower, out.at[:, pl.ds(width, width)], sent)
    copy.start()
    copy.wait()


def gram_kernel(gram_left, norm_upper, weight, own_ref, payload):
    width = gram_left.shape[0]
    own = own_ref[...]
    high, low = two_parts(own)
    right = jnp.concatenate([high, low, high], axis=0)
    payload[:width] = jnp.dot(gram_left[...], right, preferred_element_type=F32)
    norm_lower = jnp.sum(weight[...] * own * own, axis=0, keepdims=True)
    rows = lax.broadcasted_iota(jnp.int32, (8, own.shape[1]), 0)
    payload[width:] = jnp.where(rows == 0, norm_lower, jnp.where(rows == 1, norm_upper[...], 0.0))


ON_CHIP = pl.BlockSpec(memory_space=pltpu.VMEM)
ANYWHERE = pl.BlockSpec(memory_space=pl.ANY)
GRANT = pltpu.CompilerParams(vmem_limit_bytes=24 << 20)


def in_vmem(kernel, outs, *args):
    return pl.pallas_call(
        kernel,
        out_shape=[jax.ShapeDtypeStruct(shape, dtype) for shape, dtype in outs],
        in_specs=[ON_CHIP] * len(args),
        out_specs=[ON_CHIP] * len(outs),
        compiler_params=GRANT,
    )(*args)


def body(snapshot, weights, damping):
    rows, columns = snapshot.shape
    width = columns // 2
    half = width // 2
    held_rows = 4 * rows
    own_part, other_part = pl.pallas_call(
        start_kernel,
        out_shape=[jax.ShapeDtypeStruct((width + 8, half), F32)] * 2,
        in_specs=[pl.BlockSpec(memory_space=pltpu.HBM)] * 2,
        out_specs=[ON_CHIP] * 2,
        scratch_shapes=[
            pltpu.VMEM((rows, columns), F32),
            pltpu.VMEM((1, rows), F32),
            pltpu.SemaphoreType.DMA(()),
            pltpu.SemaphoreType.DMA(()),
        ],
        compiler_params=pltpu.CompilerParams(vmem_limit_bytes=(64 << 20) - (10752 << 10)),
    )(snapshot, weights[None])
    own_part, other_part, damping = lax.optimization_barrier((own_part, other_part, damping))
    payload = own_part + swapped(other_part, 1, 1)
    weight = jnp.concatenate([weights, swapped(weights, 1, 1)])
    weight = jnp.concatenate([weight, swapped(weight, 2, 2)])[:, None]
    across = swapped(snapshot, 2, 2)
    blocks, held, arriving = start_blocks, (snapshot,), (swapped(snapshot, 1, 1), across, swapped(across, 1, 1))
    damps = damping[:, 0].astype(F32) / (damping[:, 0] + damping[:, 1]).astype(F32)
    damps = lax.optimization_barrier(jnp.broadcast_to(damps[:, None], (STEPS, 128)))
    for step in range(STEPS):
        last = step + 1 == STEPS
        if step == 0:
            payload, first = chip_sum(payload, 2, arriving[:1])
            held = held + first + arriving[1:]
        else:
            payload, arriving = chip_sum(payload, 4, arriving)
            held = held + arriving
        moved, coupling, scale = in_vmem(
            functools.partial(lower_kernel, blocks, step, last),
            [((rows, width) if last else (held_rows, half), F32), ((width, width), F32), ((8, 128), F32)],
            damps,
            payload,
            swapped(payload, 1, 1),
            *held,
        )
        if last:
            break
        moved = shifted(moved, "cols", 1)
        gram_left, norm_upper, upper = in_vmem(
            functools.partial(upper_kernel, blocks),
            [((width, 3 * held_rows), jnp.bfloat16), ((1, half), F32), ((held_rows, width), F32)],
            weight,
            coupling,
            scale,
            *held,
        )
        gram_left, norm_upper, upper, moved = lax.optimization_barrier((gram_left, norm_upper, upper, moved))
        blocks = functools.partial(later_blocks, rows)
        held, arriving = (upper, moved), (swapped(moved, 1, 1),)
        (payload,) = in_vmem(gram_kernel, [((width + 8, half), F32)], gram_left, norm_upper, weight, moved)
    moved = shifted(moved, "cols", 1 - STEPS)
    out_shape = jax.ShapeDtypeStruct((rows, columns), F32)
    rotated = pl.pallas_call(
        functools.partial(last_upper_kernel, blocks),
        out_shape=out_shape,
        in_specs=[ON_CHIP] * (2 + len(held)),
        out_specs=ANYWHERE,
        scratch_shapes=[pltpu.VMEM((rows, width), F32), pltpu.SemaphoreType.DMA(())],
        compiler_params=GRANT,
    )(coupling, scale, *held)
    return pl.pallas_call(
        last_lower_kernel,
        out_shape=out_shape,
        in_specs=[ON_CHIP, ANYWHERE],
        out_specs=ANYWHERE,
        scratch_shapes=[pltpu.SemaphoreType.DMA(())],
        input_output_aliases={1: 0},
        compiler_params=GRANT,
    )(moved, rotated)


def solution(mesh):
    placed = (P("pts", "cols"), P("pts"), P())
    return jax.shard_map(
        body, mesh=mesh, in_specs=placed, out_specs=P("pts", "cols"), check_vma=False
    )
```

```python
import functools

import jax
import jax.numpy as jnp
from jax import lax
from jax.experimental import pallas as pl
from jax.experimental.pallas import tpu as pltpu
from jax.sharding import PartitionSpec as P

STEPS = 3
EPSILON = 1e-06
F32 = jnp.float32


def shifted(value, axis, steps):
    count = lax.axis_size(axis)
    pairs = [(source, (source + steps) % count) for source in range(count)]
    return lax.ppermute(value, axis, pairs)


def swapped(value, even_bits, odd_bits):
    count = lax.axis_size("pts")
    pairs = [(source, source ^ (odd_bits if source % 2 else even_bits)) for source in range(count)]
    return lax.ppermute(value, "pts", pairs)


def chip_sum(value, beside=None):
    count = lax.axis_size("pts")
    bit = 2
    while bit < count:
        if 2 * bit < count:
            rounds = [(bit, 2 * bit), (2 * bit, bit)]
        else:
            rounds = [(bit, bit)]
        for even_bits, odd_bits in rounds:
            value = value + swapped(value, even_bits, odd_bits)
            if beside is not None:
                value, beside = lax.optimization_barrier((value, beside))
        bit *= 2 ** len(rounds)
    return value, beside


def chip_sum_at_once(value, copies):
    count = lax.axis_size("pts")
    groups = [list(range(core, count, 2)) for core in range(2)]
    parts = lax.all_to_all(value, "pts", 0, 0, axis_index_groups=groups, tiled=True)
    return jnp.sum(parts.reshape(copies, -1, value.shape[1]), axis=0)


def two_parts(value):
    high = value.astype(jnp.bfloat16)
    return high, (value - high.astype(F32)).astype(jnp.bfloat16)


def first_columns(parts, columns):
    return parts[0][:, :columns], parts[1][:, :columns]


def product(left, right, left_axis=1, right_axis=0):
    return lax.dot_general(
        jnp.concatenate([left[0], left[0], left[1]], axis=left_axis),
        jnp.concatenate([right[0], right[1], right[0]], axis=right_axis),
        (((left_axis,), (right_axis,)), ((), ())),
        preferred_element_type=F32,
    )


def halves_swapped(value):
    half = value.shape[0] // 2
    return jnp.concatenate([value[half:], value[:half]], axis=0)


def times_inverse_root(left, square, scale, columns):
    rows = lax.broadcasted_iota(jnp.int32, square.shape, 0)
    identity = jnp.where(rows == lax.broadcasted_iota(jnp.int32, square.shape, 1), 1.0, 0.0)
    base = (identity + square) * (1.0 / scale)
    base_parts = two_parts(base)
    left_parts = two_parts(left)
    second = product(base_parts, base_parts)
    left_base = product(left_parts, base_parts)
    first_square = two_parts(2.25 * identity - 1.5 * base + 0.25 * second)
    cubic = product(two_parts(1.5 * base - 0.5 * second), first_square)
    both = two_parts(2.25 * identity - 0.75 * base - 0.5 * cubic)
    both_first = first_columns(both, columns)
    both_square = product(both, both_first)
    left_cubic = product(two_parts(left_base), both)
    left_both = product(left_parts, both_first)
    left_last = product(two_parts(left_cubic), two_parts(both_square))
    return (1.5 * left_both - 0.5 * left_last) * lax.rsqrt(scale)


def joined(own, other):
    return jnp.concatenate([own, halves_swapped(other)], axis=1)


def own_half(half):
    own = (lax.axis_index("pts") % 2) * half
    return pl.multiple_of(own, half), pl.multiple_of(half - own, half)


def start_blocks(near, far):
    width = near.shape[1] // 2
    own, other = own_half(width // 2)

    def taken(start):
        piece = (slice(None), pl.ds(start, width // 2))
        return jnp.concatenate([near[piece], far[piece]], axis=0)

    upper = jnp.concatenate([taken(own), taken(other)], axis=1)
    return upper, jnp.concatenate([taken(width + own), taken(width + other)], axis=1)


def later_blocks(upper, own, other):
    return upper[...], joined(own[...], other[...])


def stored(ref, value):
    half = ref.shape[1] // 2
    own, other = own_half(half)
    ref[:, pl.ds(own, half)] = value[:, :half]
    ref[:, pl.ds(other, half)] = value[:, half:]


def start_kernel(near_ref, weight_ref, own_part, other_part, near, weight, near_sent, weight_sent):
    copies = [
        pltpu.make_async_copy(near_ref, near, near_sent),
        pltpu.make_async_copy(weight_ref, weight, weight_sent),
    ]
    for copy in copies:
        copy.start()
    for copy in copies:
        copy.wait()
    width = near.shape[1] // 2
    half = width // 2
    own, other = own_half(half)
    point_weight = jnp.broadcast_to(weight[...], (8, weight.shape[1])).T[:, 0:1]
    upper_own, upper_other = near[:, pl.ds(own, half)], near[:, pl.ds(other, half)]
    upper_parts = two_parts(jnp.concatenate([upper_own, upper_other], axis=1))
    rows = lax.broadcasted_iota(jnp.int32, (8, half), 0)
    for start, norm_of, out in ((own, upper_own, own_part), (other, upper_other, other_part)):
        lower = near[:, pl.ds(width + start, half)]
        weighted = point_weight * lower
        gram = product(upper_parts, two_parts(weighted), 0, 0)
        out[:width] = gram if out is own_part else halves_swapped(gram)
        norm_lower = jnp.sum(weighted * lower, axis=0, keepdims=True)
        norm_upper = jnp.sum(point_weight * norm_of * norm_of, axis=0, keepdims=True)
        out[width:] = jnp.where(rows == 0, norm_lower, jnp.where(rows == 1, norm_upper, 0.0))


def lower_kernel(blocks, step, last, damps, own_sum, other_sum, *refs):
    *block_refs, moved, coupling_out, scale_out = refs
    width = coupling_out.shape[0]
    upper, lower = blocks(*block_refs)
    gram = joined(own_sum[:width], other_sum[:width])
    norms = jnp.concatenate([own_sum[width:], other_sum[width:]], axis=1)
    inverse = lax.rsqrt(norms + EPSILON)
    coupling = gram * (damps[step : step + 1, 0:1] * inverse.T[:, 1:2]) * inverse[0:1]
    scale = 1.0 + jnp.sum(coupling * coupling, keepdims=True)
    coupling_out[...] = coupling
    scale_out[...] = jnp.broadcast_to(scale, scale_out.shape)
    parts = two_parts(coupling)
    square = product(parts, parts, 0, 0)
    rows, columns = moved.shape
    mixed = lower[:rows] + product(two_parts(upper[:rows]), parts)
    result = times_inverse_root(mixed, square, scale, columns)
    if last:
        stored(moved, result)
    else:
        moved[...] = result


def rotated_upper(blocks, rows, coupling_ref, scale_ref, *block_refs):
    coupling = coupling_ref[...]
    upper, lower = blocks(*block_refs)
    parts = two_parts(coupling)
    mixed = upper[:rows] - product(two_parts(lower[:rows]), parts, 1, 1)
    square = product(parts, parts, 1, 1)
    return times_inverse_root(mixed, square, scale_ref[0:1, 0:1], coupling.shape[1])


def upper_kernel(blocks, weight, *refs):
    *ins, gram_left, norm_out, upper_out = refs
    upper = rotated_upper(blocks, upper_out.shape[0], *ins)
    upper_out[...] = upper
    weighted = weight[...] * upper
    norm_out[...] = jnp.sum(weighted * upper, axis=0, keepdims=True)[:, : norm_out.shape[1]]
    high, low = two_parts(weighted.T)
    gram_left[...] = jnp.concatenate([high, high, low], axis=1)


def last_upper_kernel(blocks, *refs):
    *ins, out, held, sent = refs
    stored(held, rotated_upper(blocks, held.shape[0], *ins))
    copy = pltpu.make_async_copy(held, out.at[:, pl.ds(0, held.shape[1])], sent)
    copy.start()
    copy.wait()


def last_lower_kernel(lower, filled, out, sent):
    del filled
    width = lower.shape[1]
    copy = pltpu.make_async_copy(lower, out.at[:, pl.ds(width, width)], sent)
    copy.start()
    copy.wait()


def gram_kernel(copies, gram_left, norm_upper, weight, own_ref, payload):
    width = gram_left.shape[0]
    own = own_ref[...]
    high, low = two_parts(own)
    right = jnp.concatenate([high, low, high], axis=0)
    gram = jnp.dot(gram_left[...], right, preferred_element_type=F32)
    norm_lower = jnp.sum(weight[...] * own * own, axis=0, keepdims=True)
    rows = lax.broadcasted_iota(jnp.int32, (8, own.shape[1]), 0)
    norms = jnp.where(rows == 0, norm_lower, jnp.where(rows == 1, norm_upper[...], 0.0))
    for copy in range(copies):
        start = copy * (width + 8)
        payload[start : start + width] = gram
        payload[start + width : start + width + 8] = norms


ON_CHIP = pl.BlockSpec(memory_space=pltpu.VMEM)
ANYWHERE = pl.BlockSpec(memory_space=pl.ANY)
GRANT = pltpu.CompilerParams(vmem_limit_bytes=24 << 20)


def in_vmem(kernel, outs, *args):
    return pl.pallas_call(
        kernel,
        out_shape=[jax.ShapeDtypeStruct(shape, dtype) for shape, dtype in outs],
        in_specs=[ON_CHIP] * len(args),
        out_specs=[ON_CHIP] * len(outs),
        compiler_params=GRANT,
    )(*args)


def body(snapshot, weights, damping):
    rows, columns = snapshot.shape
    width = columns // 2
    half = width // 2
    copies = lax.axis_size("pts") // 2
    whole = (2 * rows, width)
    own_part, other_part = pl.pallas_call(
        start_kernel,
        out_shape=[jax.ShapeDtypeStruct((width + 8, half), F32)] * 2,
        in_specs=[pl.BlockSpec(memory_space=pltpu.HBM)] * 2,
        out_specs=[ON_CHIP] * 2,
        scratch_shapes=[
            pltpu.VMEM((rows, columns), F32),
            pltpu.VMEM((1, rows), F32),
            pltpu.SemaphoreType.DMA(()),
            pltpu.SemaphoreType.DMA(()),
        ],
        compiler_params=pltpu.CompilerParams(vmem_limit_bytes=(64 << 20) - (10752 << 10)),
    )(snapshot, weights[None])
    own_part, other_part, damping = lax.optimization_barrier((own_part, other_part, damping))
    payload = own_part + swapped(other_part, 1, 1)
    weight = jnp.concatenate([weights, swapped(weights, 1, 1)])[:, None]
    blocks, held, arriving = start_blocks, (snapshot,), swapped(snapshot, 1, 1)
    damps = damping[:, 0].astype(F32) / (damping[:, 0] + damping[:, 1]).astype(F32)
    damps = lax.optimization_barrier(jnp.broadcast_to(damps[:, None], (STEPS, 128)))
    for step in range(STEPS):
        last = step + 1 == STEPS
        if step == 0:
            payload, arriving = chip_sum(payload, arriving)
        else:
            payload = chip_sum_at_once(payload, copies)
        held = held + (arriving,)
        moved, coupling, scale = in_vmem(
            functools.partial(lower_kernel, blocks, step, last),
            [((rows, width) if last else (2 * rows, half), F32), ((width, width), F32), ((8, 128), F32)],
            damps,
            payload,
            swapped(payload, 1, 1),
            *held,
        )
        if last:
            break
        moved = shifted(moved, "cols", 1)
        gram_left, norm_upper, upper = in_vmem(
            functools.partial(upper_kernel, blocks),
            [((width, 6 * rows), jnp.bfloat16), ((1, half), F32), (whole, F32)],
            weight,
            coupling,
            scale,
            *held,
        )
        blocks, held, arriving = later_blocks, (upper, moved), swapped(moved, 1, 1)
        (payload,) = in_vmem(
            functools.partial(gram_kernel, copies), [((copies * (width + 8), half), F32)], gram_left, norm_upper, weight, moved)
    moved = shifted(moved, "cols", 1 - STEPS)
    out_shape = jax.ShapeDtypeStruct((rows, columns), F32)
    rotated = pl.pallas_call(
        functools.partial(last_upper_kernel, blocks),
        out_shape=out_shape,
        in_specs=[ON_CHIP] * (2 + len(held)),
        out_specs=ANYWHERE,
        scratch_shapes=[pltpu.VMEM((rows, width), F32), pltpu.SemaphoreType.DMA(())],
        compiler_params=GRANT,
    )(coupling, scale, *held)
    return pl.pallas_call(
        last_lower_kernel,
        out_shape=out_shape,
        in_specs=[ON_CHIP, ANYWHERE],
        out_specs=ANYWHERE,
        scratch_shapes=[pltpu.SemaphoreType.DMA(())],
        input_output_aliases={1: 0},
        compiler_params=GRANT,
    )(moved, rotated)


def solution(mesh):
    placed = (P("pts", "cols"), P("pts"), P())
    return jax.shard_map(
        body, mesh=mesh, in_specs=placed, out_specs=P("pts", "cols"), check_vma=False
    )
```

```python
import functools

import jax
import jax.numpy as jnp
from jax import lax
from jax.experimental import pallas as pl
from jax.experimental.pallas import tpu as pltpu
from jax.sharding import PartitionSpec as P

STEPS = 3
EPSILON = 1e-06
F32 = jnp.float32


def shifted(value, axis, steps):
    count = lax.axis_size(axis)
    pairs = [(source, (source + steps) % count) for source in range(count)]
    return lax.ppermute(value, axis, pairs)


def swapped(value, even_bits, odd_bits):
    count = lax.axis_size("pts")
    pairs = [(source, source ^ (odd_bits if source % 2 else even_bits)) for source in range(count)]
    return lax.ppermute(value, "pts", pairs)


def chip_sum(value, beside=None):
    count = lax.axis_size("pts")
    bit = 2
    while bit < count:
        if 2 * bit < count:
            rounds = [(bit, 2 * bit), (2 * bit, bit)]
        else:
            rounds = [(bit, bit)]
        for even_bits, odd_bits in rounds:
            value = value + swapped(value, even_bits, odd_bits)
            if beside is not None:
                value, beside = lax.optimization_barrier((value, beside))
        bit *= 2 ** len(rounds)
    return value, beside


def two_parts(value):
    high = value.astype(jnp.bfloat16)
    return high, (value - high.astype(F32)).astype(jnp.bfloat16)


def first_columns(parts, columns):
    return parts[0][:, :columns], parts[1][:, :columns]


def product(left, right, left_axis=1, right_axis=0):
    return lax.dot_general(
        jnp.concatenate([left[0], left[0], left[1]], axis=left_axis),
        jnp.concatenate([right[0], right[1], right[0]], axis=right_axis),
        (((left_axis,), (right_axis,)), ((), ())),
        preferred_element_type=F32,
    )


def halves_swapped(value):
    half = value.shape[0] // 2
    return jnp.concatenate([value[half:], value[:half]], axis=0)


def times_inverse_root(left, square, scale, columns):
    rows = lax.broadcasted_iota(jnp.int32, square.shape, 0)
    identity = jnp.where(rows == lax.broadcasted_iota(jnp.int32, square.shape, 1), 1.0, 0.0)
    base = (identity + square) * (1.0 / scale)
    base_parts = two_parts(base)
    left_parts = two_parts(left)
    second = product(base_parts, base_parts)
    left_base = product(left_parts, base_parts)
    first_square = two_parts(2.25 * identity - 1.5 * base + 0.25 * second)
    cubic = product(two_parts(1.5 * base - 0.5 * second), first_square)
    both = two_parts(2.25 * identity - 0.75 * base - 0.5 * cubic)
    both_first = first_columns(both, columns)
    both_square = product(both, both_first)
    left_cubic = product(two_parts(left_base), both)
    left_both = product(left_parts, both_first)
    left_last = product(two_parts(left_cubic), two_parts(both_square))
    return (1.5 * left_both - 0.5 * left_last) * lax.rsqrt(scale)


def joined(own, other):
    return jnp.concatenate([own, halves_swapped(other)], axis=1)


def own_half(half):
    own = (lax.axis_index("pts") % 2) * half
    return pl.multiple_of(own, half), pl.multiple_of(half - own, half)


def start_blocks(near, far):
    width = near.shape[1] // 2
    own, other = own_half(width // 2)

    def taken(start):
        piece = (slice(None), pl.ds(start, width // 2))
        return jnp.concatenate([near[piece], far[piece]], axis=0)

    upper = jnp.concatenate([taken(own), taken(other)], axis=1)
    return upper, jnp.concatenate([taken(width + own), taken(width + other)], axis=1)


def later_blocks(upper, own, other):
    return upper[...], joined(own[...], other[...])


def stored(ref, value):
    half = ref.shape[1] // 2
    own, other = own_half(half)
    ref[:, pl.ds(own, half)] = value[:, :half]
    ref[:, pl.ds(other, half)] = value[:, half:]


def start_kernel(near_ref, weight_ref, own_part, other_part, near, weight, near_sent, weight_sent):
    copies = [
        pltpu.make_async_copy(near_ref, near, near_sent),
        pltpu.make_async_copy(weight_ref, weight, weight_sent),
    ]
    for copy in copies:
        copy.start()
    for copy in copies:
        copy.wait()
    width = near.shape[1] // 2
    half = width // 2
    own, other = own_half(half)
    point_weight = jnp.broadcast_to(weight[...], (8, weight.shape[1])).T[:, 0:1]
    upper_own, upper_other = near[:, pl.ds(own, half)], near[:, pl.ds(other, half)]
    upper_parts = two_parts(jnp.concatenate([upper_own, upper_other], axis=1))
    rows = lax.broadcasted_iota(jnp.int32, (8, half), 0)
    for start, norm_of, out in ((own, upper_own, own_part), (other, upper_other, other_part)):
        lower = near[:, pl.ds(width + start, half)]
        weighted = point_weight * lower
        gram = product(upper_parts, two_parts(weighted), 0, 0)
        out[:width] = gram if out is own_part else halves_swapped(gram)
        norm_lower = jnp.sum(weighted * lower, axis=0, keepdims=True)
        norm_upper = jnp.sum(point_weight * norm_of * norm_of, axis=0, keepdims=True)
        out[width:] = jnp.where(rows == 0, norm_lower, jnp.where(rows == 1, norm_upper, 0.0))


def lower_kernel(blocks, step, last, damps, own_sum, other_sum, *refs):
    *block_refs, moved, coupling_out, scale_out = refs
    width = coupling_out.shape[0]
    upper, lower = blocks(*block_refs)
    gram = joined(own_sum[:width], other_sum[:width])
    norms = jnp.concatenate([own_sum[width:], other_sum[width:]], axis=1)
    inverse = lax.rsqrt(norms + EPSILON)
    coupling = gram * (damps[step : step + 1, 0:1] * inverse.T[:, 1:2]) * inverse[0:1]
    scale = 1.0 + jnp.sum(coupling * coupling, keepdims=True)
    coupling_out[...] = coupling
    scale_out[...] = jnp.broadcast_to(scale, scale_out.shape)
    parts = two_parts(coupling)
    square = product(parts, parts, 0, 0)
    rows, columns = moved.shape
    mixed = lower[:rows] + product(two_parts(upper[:rows]), parts)
    result = times_inverse_root(mixed, square, scale, columns)
    if last:
        stored(moved, result)
    else:
        moved[...] = result


def rotated_upper(blocks, rows, coupling_ref, scale_ref, *block_refs):
    coupling = coupling_ref[...]
    upper, lower = blocks(*block_refs)
    parts = two_parts(coupling)
    mixed = upper[:rows] - product(two_parts(lower[:rows]), parts, 1, 1)
    square = product(parts, parts, 1, 1)
    return times_inverse_root(mixed, square, scale_ref[0:1, 0:1], coupling.shape[1])


def upper_kernel(blocks, weight, *refs):
    *ins, gram_left, norm_out, upper_out = refs
    upper = rotated_upper(blocks, upper_out.shape[0], *ins)
    upper_out[...] = upper
    weighted = weight[...] * upper
    norm_out[...] = jnp.sum(weighted * upper, axis=0, keepdims=True)[:, : norm_out.shape[1]]
    high, low = two_parts(weighted.T)
    gram_left[...] = jnp.concatenate([high, high, low], axis=1)


def last_upper_kernel(blocks, *refs):
    *ins, out, held, sent = refs
    stored(held, rotated_upper(blocks, held.shape[0], *ins))
    copy = pltpu.make_async_copy(held, out.at[:, pl.ds(0, held.shape[1])], sent)
    copy.start()
    copy.wait()


def last_lower_kernel(lower, filled, out, sent):
    del filled
    width = lower.shape[1]
    copy = pltpu.make_async_copy(lower, out.at[:, pl.ds(width, width)], sent)
    copy.start()
    copy.wait()


def gram_kernel(gram_left, norm_upper, weight, own_ref, payload):
    width = gram_left.shape[0]
    own = own_ref[...]
    high, low = two_parts(own)
    right = jnp.concatenate([high, low, high], axis=0)
    payload[:width] = jnp.dot(gram_left[...], right, preferred_element_type=F32)
    norm_lower = jnp.sum(weight[...] * own * own, axis=0, keepdims=True)
    rows = lax.broadcasted_iota(jnp.int32, (8, own.shape[1]), 0)
    payload[width:] = jnp.where(rows == 0, norm_lower, jnp.where(rows == 1, norm_upper[...], 0.0))


ON_CHIP = pl.BlockSpec(memory_space=pltpu.VMEM)
ANYWHERE = pl.BlockSpec(memory_space=pl.ANY)
GRANT = pltpu.CompilerParams(vmem_limit_bytes=24 << 20)


def in_vmem(kernel, outs, *args):
    return pl.pallas_call(
        kernel,
        out_shape=[jax.ShapeDtypeStruct(shape, dtype) for shape, dtype in outs],
        in_specs=[ON_CHIP] * len(args),
        out_specs=[ON_CHIP] * len(outs),
        compiler_params=GRANT,
    )(*args)


def body(snapshot, weights, damping):
    rows, columns = snapshot.shape
    width = columns // 2
    half = width // 2
    whole = (2 * rows, width)
    own_part, other_part = pl.pallas_call(
        start_kernel,
        out_shape=[jax.ShapeDtypeStruct((width + 8, half), F32)] * 2,
        in_specs=[pl.BlockSpec(memory_space=pltpu.HBM)] * 2,
        out_specs=[ON_CHIP] * 2,
        scratch_shapes=[
            pltpu.VMEM((rows, columns), F32),
            pltpu.VMEM((1, rows), F32),
            pltpu.SemaphoreType.DMA(()),
            pltpu.SemaphoreType.DMA(()),
        ],
        compiler_params=GRANT,
    )(*(pltpu.with_memory_space_constraint(value, pltpu.HBM) for value in (snapshot, weights[None])))
    own_part, other_part, damping = lax.optimization_barrier((own_part, other_part, damping))
    payload = own_part + swapped(other_part, 1, 1)
    weight = jnp.concatenate([weights, swapped(weights, 1, 1)])[:, None]
    blocks, held, arriving = start_blocks, (snapshot,), swapped(snapshot, 1, 1)
    damps = damping[:, 0].astype(F32) / (damping[:, 0] + damping[:, 1]).astype(F32)
    damps = lax.optimization_barrier(jnp.broadcast_to(damps[:, None], (STEPS, 128)))
    for step in range(STEPS):
        last = step + 1 == STEPS
        payload, arriving = chip_sum(payload, arriving)
        held = held + (arriving,)
        moved, coupling, scale = in_vmem(
            functools.partial(lower_kernel, blocks, step, last),
            [((rows, width) if last else (2 * rows, half), F32), ((width, width), F32), ((8, 128), F32)],
            damps,
            payload,
            swapped(payload, 1, 1),
            *held,
        )
        if last:
            break
        moved = shifted(moved, "cols", 1)
        gram_left, norm_upper, upper = in_vmem(
            functools.partial(upper_kernel, blocks),
            [((width, 6 * rows), jnp.bfloat16), ((1, half), F32), (whole, F32)],
            weight,
            coupling,
            scale,
            *held,
        )
        blocks, held, arriving = later_blocks, (upper, moved), swapped(moved, 1, 1)
        (payload,) = in_vmem(gram_kernel, [((width + 8, half), F32)], gram_left, norm_upper, weight, moved)
    moved = shifted(moved, "cols", 1 - STEPS)
    out_shape = jax.ShapeDtypeStruct((rows, columns), F32)
    rotated = pl.pallas_call(
        functools.partial(last_upper_kernel, blocks),
        out_shape=out_shape,
        in_specs=[ON_CHIP] * (2 + len(held)),
        out_specs=ANYWHERE,
        scratch_shapes=[pltpu.VMEM((rows, width), F32), pltpu.SemaphoreType.DMA(())],
        compiler_params=GRANT,
    )(coupling, scale, *held)
    return pl.pallas_call(
        last_lower_kernel,
        out_shape=out_shape,
        in_specs=[ON_CHIP, ANYWHERE],
        out_specs=ANYWHERE,
        scratch_shapes=[pltpu.SemaphoreType.DMA(())],
        input_output_aliases={1: 0},
        compiler_params=GRANT,
    )(moved, rotated)


def solution(mesh):
    placed = (P("pts", "cols"), P("pts"), P())
    return jax.shard_map(
        body, mesh=mesh, in_specs=placed, out_specs=P("pts", "cols"), check_vma=False
    )
```

```python
import functools

import jax
import jax.numpy as jnp
from jax import lax
from jax.experimental import pallas as pl
from jax.experimental.pallas import tpu as pltpu
from jax.sharding import PartitionSpec as P

STEPS = 3
EPSILON = 1e-06
F32 = jnp.float32


def permuted(value, target):
    points, columns = lax.axis_size("pts"), lax.axis_size("cols")
    pairs = []
    for source in range(points * columns):
        point, column = target(source // columns, source % columns)
        pairs.append((source, point * columns + column % columns))
    return lax.ppermute(value, ("pts", "cols"), pairs)


def core_exchange(value):
    return permuted(value, lambda point, column: (point ^ 1, column))


def chip_exchange(value, bit):
    return permuted(value, lambda p, c: (p ^ bit, c) if p % 2 else (p, c ^ 1))


def column_shift(value, steps):
    return permuted(value, lambda p, c: (p, c + steps) if p % 2 else (p ^ 2, c))


def chip_sums(values, beside):
    count = lax.axis_size("pts")
    bit = 2
    while bit < count:
        rounds = [(bit, 2 * bit), (2 * bit, bit)] if 2 * bit < count else [(bit, bit)]
        for bits in rounds:
            values = tuple(value + chip_exchange(value, b) for value, b in zip(values, bits))
            values, beside = lax.optimization_barrier((values, beside))
        bit *= 2 ** len(rounds)
    return values, beside


def two_parts(value):
    high = value.astype(jnp.bfloat16)
    return high, (value - high.astype(F32)).astype(jnp.bfloat16)


def first_columns(parts, columns):
    return parts[0][:, :columns], parts[1][:, :columns]


def product(left, right, left_axis=1, right_axis=0):
    return lax.dot_general(
        jnp.concatenate([left[0], left[0], left[1]], axis=left_axis),
        jnp.concatenate([right[0], right[1], right[0]], axis=right_axis),
        (((left_axis,), (right_axis,)), ((), ())),
        preferred_element_type=F32,
    )


def times_inverse_root(left, square, scale, columns):
    rows = lax.broadcasted_iota(jnp.int32, square.shape, 0)
    identity = jnp.where(rows == lax.broadcasted_iota(jnp.int32, square.shape, 1), 1.0, 0.0)
    base = (identity + square) * (1.0 / scale)
    base_parts = two_parts(base)
    left_parts = two_parts(left)
    second = product(base_parts, base_parts)
    left_base = product(left_parts, base_parts)
    first_square = two_parts(2.25 * identity - 1.5 * base + 0.25 * second)
    cubic = product(two_parts(1.5 * base - 0.5 * second), first_square)
    both = two_parts(2.25 * identity - 0.75 * base - 0.5 * cubic)
    both_first = first_columns(both, columns)
    both_square = product(both, both_first)
    left_cubic = product(two_parts(left_base), both)
    left_both = product(left_parts, both_first)
    left_last = product(two_parts(left_cubic), two_parts(both_square))
    return (1.5 * left_both - 0.5 * left_last) * lax.rsqrt(scale)


def start_blocks(far, near):
    width = near.shape[1] // 2
    whole = jnp.concatenate([far[...], near[...]], axis=0)
    return whole[:, :width], whole[:, width:]


def later_blocks(upper, lower):
    return upper[...], lower[...]


def put_sums(outs, gram, norm_lower, norm_upper):
    width = gram.shape[0]
    rows = lax.broadcasted_iota(jnp.int32, (8, width), 0)
    norms = jnp.where(rows == 0, norm_lower, jnp.where(rows == 1, norm_upper, 0.0))
    for index, out in enumerate(outs):
        columns = slice(index * (width // 2), (index + 1) * (width // 2))
        out[:width] = gram[:, columns]
        out[width:] = norms[:, columns]


def start_kernel(near_ref, weight_ref, first, second, near, weight, near_sent, weight_sent):
    copies = [
        pltpu.make_async_copy(near_ref, near, near_sent),
        pltpu.make_async_copy(weight_ref, weight, weight_sent),
    ]
    for copy in copies:
        copy.start()
    for copy in copies:
        copy.wait()
    width = near.shape[1] // 2
    point_weight = jnp.broadcast_to(weight[...], (8, weight.shape[1])).T[:, 0:1]
    upper, lower = near[:, :width], near[:, width:]
    weighted = point_weight * lower
    gram = product(two_parts(upper), two_parts(weighted), 0, 0)
    norm_lower = jnp.sum(weighted * lower, axis=0, keepdims=True)
    norm_upper = jnp.sum(point_weight * upper * upper, axis=0, keepdims=True)
    put_sums((first, second), gram, norm_lower, norm_upper)


def lower_kernel(blocks, step, damps, first_sum, second_sum, *refs):
    *block_refs, coupling_out, scale_out = refs[: len(refs) - (2 if step + 1 == STEPS else 1)]
    moved = refs[len(block_refs) + 2 :]
    width = coupling_out.shape[0]
    upper, lower = blocks(*block_refs)
    gram = jnp.concatenate([first_sum[:width], second_sum[:width]], axis=1)
    norms = jnp.concatenate([first_sum[width:], second_sum[width:]], axis=1)
    inverse = lax.rsqrt(norms + EPSILON)
    coupling = gram * (damps[step : step + 1, 0:1] * inverse.T[:, 1:2]) * inverse[0:1]
    scale = 1.0 + jnp.sum(coupling * coupling, keepdims=True)
    coupling_out[...] = coupling
    scale_out[...] = jnp.broadcast_to(scale, scale_out.shape)
    parts = two_parts(coupling)
    square = product(parts, parts, 0, 0)
    mixed = lower + product(two_parts(upper), parts)
    put_rows(moved, times_inverse_root(mixed, square, scale, width))


def put_rows(outs, value):
    rows = outs[0].shape[0]
    for index, out in enumerate(outs):
        out[...] = value[index * rows : (index + 1) * rows]


def rotated_upper(blocks, coupling_ref, scale_ref, *block_refs):
    coupling = coupling_ref[...]
    upper, lower = blocks(*block_refs)
    parts = two_parts(coupling)
    mixed = upper - product(two_parts(lower), parts, 1, 1)
    square = product(parts, parts, 1, 1)
    return times_inverse_root(mixed, square, scale_ref[0:1, 0:1], coupling.shape[1])


def upper_kernel(blocks, weight, *refs):
    *ins, gram_left, norm_out, upper_out = refs
    upper = rotated_upper(blocks, *ins)
    upper_out[...] = upper
    weighted = weight[...] * upper
    norm_out[...] = jnp.sum(weighted * upper, axis=0, keepdims=True)
    high, low = two_parts(weighted.T)
    gram_left[...] = jnp.concatenate([high, high, low], axis=1)


def last_upper_kernel(blocks, *refs):
    *ins, first, second = refs
    put_rows((first, second), rotated_upper(blocks, *ins))


def gram_kernel(gram_left, norm_upper, weight, lower_ref, first, second):
    lower = lower_ref[...]
    high, low = two_parts(lower)
    right = jnp.concatenate([high, low, high], axis=0)
    gram = jnp.dot(gram_left[...], right, preferred_element_type=F32)
    norm_lower = jnp.sum(weight[...] * lower * lower, axis=0, keepdims=True)
    put_sums((first, second), gram, norm_lower, norm_upper[...])


def put_columns(start, own, given, out, sent):
    core = lax.axis_index("pts") % 2
    for index, ref in enumerate((given, own)):

        @pl.when(core == index)
        def _(ref=ref):
            copy = pltpu.make_async_copy(ref, out.at[:, pl.ds(start, ref.shape[1])], sent)
            copy.start()
            copy.wait()


def first_columns_kernel(own, given, out, sent):
    put_columns(0, own, given, out, sent)


def last_columns_kernel(own, given, filled, out, sent):
    del filled
    put_columns(own.shape[1], own, given, out, sent)


ON_CHIP = pl.BlockSpec(memory_space=pltpu.VMEM)
ANYWHERE = pl.BlockSpec(memory_space=pl.ANY)
GRANT = pltpu.CompilerParams(vmem_limit_bytes=24 << 20)


def in_vmem(kernel, outs, *args, flops=None):
    cost = None if flops is None else pl.CostEstimate(flops=flops, bytes_accessed=0, transcendentals=0)
    return pl.pallas_call(
        kernel,
        out_shape=[jax.ShapeDtypeStruct(shape, dtype) for shape, dtype in outs],
        in_specs=[ON_CHIP] * len(args),
        out_specs=[ON_CHIP] * len(outs),
        compiler_params=GRANT,
        cost_estimate=cost,
    )(*args)


def body(snapshot, weights, damping):
    rows, columns = snapshot.shape
    width = columns // 2
    sums = [((width + 8, width // 2), F32)] * 2
    whole = ((2 * rows, width), F32)
    parts = pl.pallas_call(
        start_kernel,
        out_shape=[jax.ShapeDtypeStruct(*one) for one in sums],
        in_specs=[pl.BlockSpec(memory_space=pltpu.HBM)] * 2,
        out_specs=[ON_CHIP] * 2,
        scratch_shapes=[
            pltpu.VMEM((rows, columns), F32),
            pltpu.VMEM((1, rows), F32),
            pltpu.SemaphoreType.DMA(()),
            pltpu.SemaphoreType.DMA(()),
        ],
        compiler_params=GRANT,
    )(*(pltpu.with_memory_space_constraint(value, pltpu.HBM) for value in (snapshot, weights[None])))
    *parts, damping = lax.optimization_barrier((*parts, damping))
    parts = tuple(part + core_exchange(part) for part in parts)
    weight = jnp.concatenate([core_exchange(weights), weights])[:, None]
    far = core_exchange(snapshot)
    damps = damping[:, 0].astype(F32) / (damping[:, 0] + damping[:, 1]).astype(F32)
    damps = lax.optimization_barrier(jnp.broadcast_to(damps[:, None], (STEPS, 128)))
    blocks, held = start_blocks, (far, snapshot)
    for step in range(STEPS):
        last = step + 1 == STEPS
        if step == 0:
            parts, far = chip_sums(parts, far)
            held = (far, snapshot)
        else:
            parts, _ = chip_sums(parts, ())
        halves = [((rows, width), F32)] * 2
        coupling, scale, *moved = in_vmem(
            functools.partial(lower_kernel, blocks, step),
            [((width, width), F32), ((8, 128), F32)] + (halves if last else [whole]),
            damps,
            *parts,
            *held,
        )
        if last:
            break
        moved = column_shift(moved[0], 1)
        gram_left, norm_upper, upper = in_vmem(
            functools.partial(upper_kernel, blocks),
            [((width, 6 * rows), jnp.bfloat16), ((1, width), F32), whole],
            weight,
            coupling,
            scale,
            *held,
        )
        gram_left, norm_upper, upper, moved = lax.optimization_barrier((gram_left, norm_upper, upper, moved))
        blocks, held = later_blocks, (upper, moved)
        parts = in_vmem(gram_kernel, sums, gram_left, norm_upper, weight, moved)
        parts = tuple(parts)
    back = 1 - STEPS
    given = permuted(moved[0], lambda p, c: (p ^ 1, c + back) if p % 2 else (p ^ 1, c))
    own = column_shift(moved[1], back)
    upper_given, upper_own = in_vmem(
        functools.partial(last_upper_kernel, blocks), halves, coupling, scale, *held, flops=48 * width**3
    )
    upper_given = core_exchange(upper_given)
    result = dict(
        out_shape=jax.ShapeDtypeStruct((rows, columns), F32),
        out_specs=ANYWHERE,
        scratch_shapes=[pltpu.SemaphoreType.DMA(())],
        compiler_params=GRANT,
    )
    rotated = pl.pallas_call(first_columns_kernel, in_specs=[ON_CHIP] * 2, **result)(upper_own, upper_given)
    return pl.pallas_call(
        last_columns_kernel,
        in_specs=[ON_CHIP, ON_CHIP, ANYWHERE],
        input_output_aliases={2: 0},
        **result,
    )(own, given, rotated)


def solution(mesh):
    placed = (P("pts", "cols"), P("pts"), P())
    return jax.shard_map(
        body, mesh=mesh, in_specs=placed, out_specs=P("pts", "cols"), check_vma=False
    )
```

```python
import functools

import jax
import jax.numpy as jnp
from jax import lax
from jax.experimental import pallas as pl
from jax.experimental.pallas import tpu as pltpu
from jax.sharding import PartitionSpec as P

STEPS = 3
EPSILON = 1e-06
F32 = jnp.float32


def column_shift(value, steps):
    points, columns = lax.axis_size("pts"), lax.axis_size("cols")
    pairs = [
        (point * columns + column, (point ^ 1) * columns + (column + steps) % columns)
        for point in range(points)
        for column in range(columns)
    ]
    return lax.ppermute(value, ("pts", "cols"), pairs)


def swapped(value, even_bits, odd_bits):
    count = lax.axis_size("pts")
    pairs = [(source, source ^ (odd_bits if source % 2 else even_bits)) for source in range(count)]
    return lax.ppermute(value, "pts", pairs)


def chip_sum(value, beside):
    count = lax.axis_size("pts")
    bit = 2
    while bit < count:
        if 2 * bit < count:
            for _ in range(2):
                value = swapped(value, bit ^ 1, 2 * bit ^ 1) + swapped(value, 1, 1)
                value, beside = lax.optimization_barrier((value, beside))
        else:
            value = value + swapped(value, bit, bit)
        bit *= 4
    return value, beside


def two_parts(value):
    high = value.astype(jnp.bfloat16)
    return high, (value - high.astype(F32)).astype(jnp.bfloat16)


def first_columns(parts, columns):
    return parts[0][:, :columns], parts[1][:, :columns]


def product(left, right, left_axis=1, right_axis=0):
    return lax.dot_general(
        jnp.concatenate([left[0], left[0], left[1]], axis=left_axis),
        jnp.concatenate([right[0], right[1], right[0]], axis=right_axis),
        (((left_axis,), (right_axis,)), ((), ())),
        preferred_element_type=F32,
    )


def halves_swapped(value):
    half = value.shape[0] // 2
    return jnp.concatenate([value[half:], value[:half]], axis=0)


def times_inverse_root(left, square, scale, columns):
    rows = lax.broadcasted_iota(jnp.int32, square.shape, 0)
    identity = jnp.where(rows == lax.broadcasted_iota(jnp.int32, square.shape, 1), 1.0, 0.0)
    base = (identity + square) * (1.0 / scale)
    base_parts = two_parts(base)
    left_parts = two_parts(left)
    second = product(base_parts, base_parts)
    left_base = product(left_parts, base_parts)
    first_square = two_parts(2.25 * identity - 1.5 * base + 0.25 * second)
    cubic = product(two_parts(1.5 * base - 0.5 * second), first_square)
    both = two_parts(2.25 * identity - 0.75 * base - 0.5 * cubic)
    both_first = first_columns(both, columns)
    both_square = product(both, both_first)
    left_cubic = product(two_parts(left_base), both)
    left_both = product(left_parts, both_first)
    left_last = product(two_parts(left_cubic), two_parts(both_square))
    return (1.5 * left_both - 0.5 * left_last) * lax.rsqrt(scale)


def joined(own, other):
    return jnp.concatenate([own, halves_swapped(other)], axis=1)


def own_half(half):
    own = (lax.axis_index("pts") % 2) * half
    return pl.multiple_of(own, half), pl.multiple_of(half - own, half)


def start_blocks(near, far):
    width = near.shape[1] // 2
    own, other = own_half(width // 2)

    def taken(start):
        piece = (slice(None), pl.ds(start, width // 2))
        return jnp.concatenate([near[piece], far[piece]], axis=0)

    upper = jnp.concatenate([taken(own), taken(other)], axis=1)
    return upper, jnp.concatenate([taken(width + own), taken(width + other)], axis=1)


def later_blocks(upper, own, other):
    return upper[...], jnp.concatenate([halves_swapped(own[...]), other[...]], axis=1)


def stored(ref, value):
    half = ref.shape[1] // 2
    own, other = own_half(half)
    ref[:, pl.ds(own, half)] = value[:, :half]
    ref[:, pl.ds(other, half)] = value[:, half:]


def start_kernel(near_ref, weight_ref, own_part, other_part, near, weight, near_sent, weight_sent):
    copies = [
        pltpu.make_async_copy(near_ref, near, near_sent),
        pltpu.make_async_copy(weight_ref, weight, weight_sent),
    ]
    for copy in copies:
        copy.start()
    for copy in copies:
        copy.wait()
    width = near.shape[1] // 2
    half = width // 2
    own, other = own_half(half)
    point_weight = jnp.broadcast_to(weight[...], (8, weight.shape[1])).T[:, 0:1]
    upper_own, upper_other = near[:, pl.ds(own, half)], near[:, pl.ds(other, half)]
    upper_parts = two_parts(jnp.concatenate([upper_own, upper_other], axis=1))
    rows = lax.broadcasted_iota(jnp.int32, (8, half), 0)
    for start, norm_of, out in ((own, upper_own, own_part), (other, upper_other, other_part)):
        lower = near[:, pl.ds(width + start, half)]
        weighted = point_weight * lower
        gram = product(upper_parts, two_parts(weighted), 0, 0)
        out[:width] = gram if out is own_part else halves_swapped(gram)
        norm_lower = jnp.sum(weighted * lower, axis=0, keepdims=True)
        norm_upper = jnp.sum(point_weight * norm_of * norm_of, axis=0, keepdims=True)
        out[width:] = jnp.where(rows == 0, norm_lower, jnp.where(rows == 1, norm_upper, 0.0))


def lower_kernel(blocks, step, last, damps, own_sum, other_sum, *refs):
    *block_refs, moved, coupling_out, scale_out = refs
    width = coupling_out.shape[0]
    upper, lower = blocks(*block_refs)
    gram = joined(own_sum[:width], other_sum[:width])
    norms = jnp.concatenate([own_sum[width:], other_sum[width:]], axis=1)
    inverse = lax.rsqrt(norms + EPSILON)
    coupling = gram * (damps[step : step + 1, 0:1] * inverse.T[:, 1:2]) * inverse[0:1]
    scale = 1.0 + jnp.sum(coupling * coupling, keepdims=True)
    coupling_out[...] = coupling
    scale_out[...] = jnp.broadcast_to(scale, scale_out.shape)
    parts = two_parts(coupling)
    square = product(parts, parts, 0, 0)
    rows, columns = moved.shape
    taken = slice(rows, 2 * rows) if last else slice(0, rows)
    mixed = lower[taken] + product(two_parts(upper[taken]), parts)
    result = times_inverse_root(mixed, square, scale, columns)
    if last:
        stored(moved, result)
    else:
        moved[...] = result


def rotated_upper(blocks, rows, coupling_ref, scale_ref, *block_refs):
    coupling = coupling_ref[...]
    upper, lower = blocks(*block_refs)
    parts = two_parts(coupling)
    mixed = upper[:rows] - product(two_parts(lower[:rows]), parts, 1, 1)
    square = product(parts, parts, 1, 1)
    return times_inverse_root(mixed, square, scale_ref[0:1, 0:1], coupling.shape[1])


def upper_kernel(blocks, weight, *refs):
    *ins, gram_left, norm_out, upper_out = refs
    upper = rotated_upper(blocks, upper_out.shape[0], *ins)
    upper_out[...] = upper
    weighted = weight[...] * upper
    norm_out[...] = jnp.sum(weighted * upper, axis=0, keepdims=True)[:, : norm_out.shape[1]]
    high, low = two_parts(weighted.T)
    gram_left[...] = jnp.concatenate([high, high, low], axis=1)


def last_upper_kernel(blocks, *refs):
    *ins, out, held, sent = refs
    stored(held, rotated_upper(blocks, held.shape[0], *ins))
    copy = pltpu.make_async_copy(held, out.at[:, pl.ds(0, held.shape[1])], sent)
    copy.start()
    copy.wait()


def last_lower_kernel(lower, filled, out, sent):
    del filled
    width = lower.shape[1]
    copy = pltpu.make_async_copy(lower, out.at[:, pl.ds(width, width)], sent)
    copy.start()
    copy.wait()


def gram_kernel(gram_left, norm_upper, weight, own_ref, payload):
    width = gram_left.shape[0]
    own = halves_swapped(own_ref[...])
    high, low = two_parts(own)
    right = jnp.concatenate([high, low, high], axis=0)
    payload[:width] = jnp.dot(gram_left[...], right, preferred_element_type=F32)
    norm_lower = jnp.sum(weight[...] * own * own, axis=0, keepdims=True)
    rows = lax.broadcasted_iota(jnp.int32, (8, own.shape[1]), 0)
    payload[width:] = jnp.where(rows == 0, norm_lower, jnp.where(rows == 1, norm_upper[...], 0.0))


ON_CHIP = pl.BlockSpec(memory_space=pltpu.VMEM)
ANYWHERE = pl.BlockSpec(memory_space=pl.ANY)
GRANT = pltpu.CompilerParams(vmem_limit_bytes=24 << 20)


def in_vmem(kernel, outs, *args):
    return pl.pallas_call(
        kernel,
        out_shape=[jax.ShapeDtypeStruct(shape, dtype) for shape, dtype in outs],
        in_specs=[ON_CHIP] * len(args),
        out_specs=[ON_CHIP] * len(outs),
        compiler_params=GRANT,
    )(*args)


def body(snapshot, weights, damping):
    rows, columns = snapshot.shape
    width = columns // 2
    half = width // 2
    whole = (2 * rows, width)
    own_part, other_part = pl.pallas_call(
        start_kernel,
        out_shape=[jax.ShapeDtypeStruct((width + 8, half), F32)] * 2,
        in_specs=[pl.BlockSpec(memory_space=pltpu.HBM)] * 2,
        out_specs=[ON_CHIP] * 2,
        scratch_shapes=[
            pltpu.VMEM((rows, columns), F32),
            pltpu.VMEM((1, rows), F32),
            pltpu.SemaphoreType.DMA(()),
            pltpu.SemaphoreType.DMA(()),
        ],
        compiler_params=GRANT,
    )(*(pltpu.with_memory_space_constraint(value, pltpu.HBM) for value in (snapshot, weights[None])))
    own_part, other_part, damping = lax.optimization_barrier((own_part, other_part, damping))
    payload = own_part + swapped(other_part, 1, 1)
    weight = jnp.concatenate([weights, swapped(weights, 1, 1)])[:, None]
    blocks, held, arriving = start_blocks, (snapshot,), swapped(snapshot, 1, 1)
    damps = damping[:, 0].astype(F32) / (damping[:, 0] + damping[:, 1]).astype(F32)
    damps = lax.optimization_barrier(jnp.broadcast_to(damps[:, None], (STEPS, 128)))
    for step in range(STEPS):
        last = step + 1 == STEPS
        payload, arriving = chip_sum(payload, arriving)
        held = held + (arriving,)
        moved, coupling, scale = in_vmem(
            functools.partial(lower_kernel, blocks, step, last),
            [((rows, width) if last else (2 * rows, half), F32), ((width, width), F32), ((8, 128), F32)],
            damps,
            payload,
            swapped(payload, 1, 1),
            *held,
        )
        if last:
            break
        moved = column_shift(moved, 1)
        gram_left, norm_upper, upper = in_vmem(
            functools.partial(upper_kernel, blocks),
            [((width, 6 * rows), jnp.bfloat16), ((1, half), F32), (whole, F32)],
            weight,
            coupling,
            scale,
            *held,
        )
        blocks, held, arriving = later_blocks, (upper, moved), swapped(moved, 1, 1)
        (payload,) = in_vmem(gram_kernel, [((width + 8, half), F32)], gram_left, norm_upper, weight, moved)
    moved = column_shift(moved, 1 - STEPS)
    out_shape = jax.ShapeDtypeStruct((rows, columns), F32)
    rotated = pl.pallas_call(
        functools.partial(last_upper_kernel, blocks),
        out_shape=out_shape,
        in_specs=[ON_CHIP] * (2 + len(held)),
        out_specs=ANYWHERE,
        scratch_shapes=[pltpu.VMEM((rows, width), F32), pltpu.SemaphoreType.DMA(())],
        compiler_params=GRANT,
    )(coupling, scale, *held)
    return pl.pallas_call(
        last_lower_kernel,
        out_shape=out_shape,
        in_specs=[ON_CHIP, ANYWHERE],
        out_specs=ANYWHERE,
        scratch_shapes=[pltpu.SemaphoreType.DMA(())],
        input_output_aliases={1: 0},
        compiler_params=GRANT,
    )(moved, rotated)


def solution(mesh):
    placed = (P("pts", "cols"), P("pts"), P())
    return jax.shard_map(
        body, mesh=mesh, in_specs=placed, out_specs=P("pts", "cols"), check_vma=False
    )
```

```python
import functools

import jax
import jax.numpy as jnp
from jax import lax
from jax.experimental import pallas as pl
from jax.experimental.pallas import tpu as pltpu
from jax.sharding import PartitionSpec as P

STEPS = 3
EPSILON = 1e-06
F32 = jnp.float32


def column_shift(value, steps):
    points, columns = lax.axis_size("pts"), lax.axis_size("cols")
    pairs = [
        (point * columns + column, (point ^ 1) * columns + (column + steps) % columns)
        for point in range(points)
        for column in range(columns)
    ]
    return lax.ppermute(value, ("pts", "cols"), pairs)


def swapped(value, even_bits, odd_bits):
    count = lax.axis_size("pts")
    pairs = [(source, source ^ (odd_bits if source % 2 else even_bits)) for source in range(count)]
    return lax.ppermute(value, "pts", pairs)


def chip_sum(value, beside):
    count = lax.axis_size("pts")
    bit = 2
    while bit < count:
        if 2 * bit < count:
            for _ in range(2):
                near = swapped(value, 1, 1)
                value = near + swapped(value, bit ^ 1, 2 * bit ^ 1)
                value, beside = lax.optimization_barrier((value, beside))
        else:
            value = value + swapped(value, bit, bit)
        bit *= 4
    return value, beside


def two_parts(value):
    high = value.astype(jnp.bfloat16)
    return high, (value - high.astype(F32)).astype(jnp.bfloat16)


def first_columns(parts, columns):
    return parts[0][:, :columns], parts[1][:, :columns]


def product(left, right, left_axis=1, right_axis=0):
    return lax.dot_general(
        jnp.concatenate([left[0], left[0], left[1]], axis=left_axis),
        jnp.concatenate([right[0], right[1], right[0]], axis=right_axis),
        (((left_axis,), (right_axis,)), ((), ())),
        preferred_element_type=F32,
    )


def halves_swapped(value):
    half = value.shape[0] // 2
    return jnp.concatenate([value[half:], value[:half]], axis=0)


def times_inverse_root(left, square, scale, columns):
    rows = lax.broadcasted_iota(jnp.int32, square.shape, 0)
    identity = jnp.where(rows == lax.broadcasted_iota(jnp.int32, square.shape, 1), 1.0, 0.0)
    base = (identity + square) * (1.0 / scale)
    base_parts = two_parts(base)
    left_parts = two_parts(left)
    second = product(base_parts, base_parts)
    left_base = product(left_parts, base_parts)
    first_square = two_parts(2.25 * identity - 1.5 * base + 0.25 * second)
    cubic = product(two_parts(1.5 * base - 0.5 * second), first_square)
    both = two_parts(2.25 * identity - 0.75 * base - 0.5 * cubic)
    both_first = first_columns(both, columns)
    both_square = product(both, both_first)
    left_cubic = product(two_parts(left_base), both)
    left_both = product(left_parts, both_first)
    left_last = product(two_parts(left_cubic), two_parts(both_square))
    return (1.5 * left_both - 0.5 * left_last) * lax.rsqrt(scale)


def joined(own, other):
    return jnp.concatenate([own, halves_swapped(other)], axis=1)


def own_half(half):
    own = (lax.axis_index("pts") % 2) * half
    return pl.multiple_of(own, half), pl.multiple_of(half - own, half)


def start_blocks(near, far):
    width = near.shape[1] // 2
    own, other = own_half(width // 2)

    def taken(start):
        piece = (slice(None), pl.ds(start, width // 2))
        return jnp.concatenate([near[piece], far[piece]], axis=0)

    upper = jnp.concatenate([taken(own), taken(other)], axis=1)
    return upper, jnp.concatenate([taken(width + own), taken(width + other)], axis=1)


def later_blocks(upper, own, other):
    return upper[...], jnp.concatenate([halves_swapped(own[...]), other[...]], axis=1)


def stored(ref, value):
    half = ref.shape[1] // 2
    own, other = own_half(half)
    ref[:, pl.ds(own, half)] = value[:, :half]
    ref[:, pl.ds(other, half)] = value[:, half:]


def start_kernel(near_ref, weight_ref, own_part, other_part, near, weight, near_sent, weight_sent):
    copies = [
        pltpu.make_async_copy(near_ref, near, near_sent),
        pltpu.make_async_copy(weight_ref, weight, weight_sent),
    ]
    for copy in copies:
        copy.start()
    for copy in copies:
        copy.wait()
    width = near.shape[1] // 2
    half = width // 2
    own, other = own_half(half)
    point_weight = jnp.broadcast_to(weight[...], (8, weight.shape[1])).T[:, 0:1]
    upper_own, upper_other = near[:, pl.ds(own, half)], near[:, pl.ds(other, half)]
    upper_parts = two_parts(jnp.concatenate([upper_own, upper_other], axis=1))
    rows = lax.broadcasted_iota(jnp.int32, (8, half), 0)
    for start, norm_of, out in ((own, upper_own, own_part), (other, upper_other, other_part)):
        lower = near[:, pl.ds(width + start, half)]
        weighted = point_weight * lower
        gram = product(upper_parts, two_parts(weighted), 0, 0)
        out[:width] = gram if out is own_part else halves_swapped(gram)
        norm_lower = jnp.sum(weighted * lower, axis=0, keepdims=True)
        norm_upper = jnp.sum(point_weight * norm_of * norm_of, axis=0, keepdims=True)
        out[width:] = jnp.where(rows == 0, norm_lower, jnp.where(rows == 1, norm_upper, 0.0))


def lower_kernel(blocks, step, last, damps, own_sum, other_sum, *refs):
    *block_refs, moved, coupling_out, scale_out = refs
    width = coupling_out.shape[0]
    upper, lower = blocks(*block_refs)
    gram = joined(own_sum[:width], other_sum[:width])
    norms = jnp.concatenate([own_sum[width:], other_sum[width:]], axis=1)
    inverse = lax.rsqrt(norms + EPSILON)
    coupling = gram * (damps[step : step + 1, 0:1] * inverse.T[:, 1:2]) * inverse[0:1]
    scale = 1.0 + jnp.sum(coupling * coupling, keepdims=True)
    coupling_out[...] = coupling
    scale_out[...] = jnp.broadcast_to(scale, scale_out.shape)
    parts = two_parts(coupling)
    square = product(parts, parts, 0, 0)
    rows, columns = moved.shape
    taken = slice(rows, 2 * rows) if last else slice(0, rows)
    mixed = lower[taken] + product(two_parts(upper[taken]), parts)
    result = times_inverse_root(mixed, square, scale, columns)
    if last:
        stored(moved, result)
    else:
        moved[...] = result


def rotated_upper(blocks, rows, coupling_ref, scale_ref, *block_refs):
    coupling = coupling_ref[...]
    upper, lower = blocks(*block_refs)
    parts = two_parts(coupling)
    mixed = upper[:rows] - product(two_parts(lower[:rows]), parts, 1, 1)
    square = product(parts, parts, 1, 1)
    return times_inverse_root(mixed, square, scale_ref[0:1, 0:1], coupling.shape[1])


def upper_kernel(blocks, weight, *refs):
    *ins, gram_left, norm_out, upper_out = refs
    upper = rotated_upper(blocks, upper_out.shape[0], *ins)
    upper_out[...] = upper
    weighted = weight[...] * upper
    norm_out[...] = jnp.sum(weighted * upper, axis=0, keepdims=True)[:, : norm_out.shape[1]]
    high, low = two_parts(weighted.T)
    gram_left[...] = jnp.concatenate([high, high, low], axis=1)


def last_upper_kernel(blocks, *refs):
    *ins, out, held, sent = refs
    stored(held, rotated_upper(blocks, held.shape[0], *ins))
    copy = pltpu.make_async_copy(held, out.at[:, pl.ds(0, held.shape[1])], sent)
    copy.start()
    copy.wait()


def last_lower_kernel(lower, filled, out, sent):
    del filled
    width = lower.shape[1]
    copy = pltpu.make_async_copy(lower, out.at[:, pl.ds(width, width)], sent)
    copy.start()
    copy.wait()


def gram_kernel(gram_left, norm_upper, weight, own_ref, payload):
    width = gram_left.shape[0]
    own = halves_swapped(own_ref[...])
    high, low = two_parts(own)
    right = jnp.concatenate([high, low, high], axis=0)
    payload[:width] = jnp.dot(gram_left[...], right, preferred_element_type=F32)
    norm_lower = jnp.sum(weight[...] * own * own, axis=0, keepdims=True)
    rows = lax.broadcasted_iota(jnp.int32, (8, own.shape[1]), 0)
    payload[width:] = jnp.where(rows == 0, norm_lower, jnp.where(rows == 1, norm_upper[...], 0.0))


ON_CHIP = pl.BlockSpec(memory_space=pltpu.VMEM)
ANYWHERE = pl.BlockSpec(memory_space=pl.ANY)
GRANT = pltpu.CompilerParams(vmem_limit_bytes=24 << 20)


def in_vmem(kernel, outs, *args):
    return pl.pallas_call(
        kernel,
        out_shape=[jax.ShapeDtypeStruct(shape, dtype) for shape, dtype in outs],
        in_specs=[ON_CHIP] * len(args),
        out_specs=[ON_CHIP] * len(outs),
        compiler_params=GRANT,
    )(*args)


def body(snapshot, weights, damping):
    rows, columns = snapshot.shape
    width = columns // 2
    half = width // 2
    whole = (2 * rows, width)
    own_part, other_part = pl.pallas_call(
        start_kernel,
        out_shape=[jax.ShapeDtypeStruct((width + 8, half), F32)] * 2,
        in_specs=[pl.BlockSpec(memory_space=pltpu.HBM)] * 2,
        out_specs=[ON_CHIP] * 2,
        scratch_shapes=[
            pltpu.VMEM((rows, columns), F32),
            pltpu.VMEM((1, rows), F32),
            pltpu.SemaphoreType.DMA(()),
            pltpu.SemaphoreType.DMA(()),
        ],
        compiler_params=GRANT,
    )(*(pltpu.with_memory_space_constraint(value, pltpu.HBM) for value in (snapshot, weights[None])))
    own_part, other_part, damping = lax.optimization_barrier((own_part, other_part, damping))
    payload = own_part + swapped(other_part, 1, 1)
    weight = jnp.concatenate([weights, swapped(weights, 1, 1)])[:, None]
    blocks, held, arriving = start_blocks, (snapshot,), swapped(snapshot, 1, 1)
    damps = damping[:, 0].astype(F32) / (damping[:, 0] + damping[:, 1]).astype(F32)
    damps = lax.optimization_barrier(jnp.broadcast_to(damps[:, None], (STEPS, 128)))
    for step in range(STEPS):
        last = step + 1 == STEPS
        payload, arriving = chip_sum(payload, arriving)
        held = held + (arriving,)
        moved, coupling, scale = in_vmem(
            functools.partial(lower_kernel, blocks, step, last),
            [((rows, width) if last else (2 * rows, half), F32), ((width, width), F32), ((8, 128), F32)],
            damps,
            payload,
            swapped(payload, 1, 1),
            *held,
        )
        if last:
            break
        moved = column_shift(moved, 1)
        gram_left, norm_upper, upper = in_vmem(
            functools.partial(upper_kernel, blocks),
            [((width, 6 * rows), jnp.bfloat16), ((1, half), F32), (whole, F32)],
            weight,
            coupling,
            scale,
            *held,
        )
        blocks, held, arriving = later_blocks, (upper, moved), swapped(moved, 1, 1)
        (payload,) = in_vmem(gram_kernel, [((width + 8, half), F32)], gram_left, norm_upper, weight, moved)
    moved = column_shift(moved, 1 - STEPS)
    out_shape = jax.ShapeDtypeStruct((rows, columns), F32)
    rotated = pl.pallas_call(
        functools.partial(last_upper_kernel, blocks),
        out_shape=out_shape,
        in_specs=[ON_CHIP] * (2 + len(held)),
        out_specs=ANYWHERE,
        scratch_shapes=[pltpu.VMEM((rows, width), F32), pltpu.SemaphoreType.DMA(())],
        compiler_params=GRANT,
    )(coupling, scale, *held)
    return pl.pallas_call(
        last_lower_kernel,
        out_shape=out_shape,
        in_specs=[ON_CHIP, ANYWHERE],
        out_specs=ANYWHERE,
        scratch_shapes=[pltpu.SemaphoreType.DMA(())],
        input_output_aliases={1: 0},
        compiler_params=GRANT,
    )(moved, rotated)


def solution(mesh):
    placed = (P("pts", "cols"), P("pts"), P())
    return jax.shard_map(
        body, mesh=mesh, in_specs=placed, out_specs=P("pts", "cols"), check_vma=False
    )
```

```python
import functools

import jax
import jax.numpy as jnp
from jax import lax
from jax.experimental import pallas as pl
from jax.experimental.pallas import tpu as pltpu
from jax.sharding import PartitionSpec as P

STEPS = 3
EPSILON = 1e-06
F32 = jnp.float32


def column_shift(value, steps):
    points, columns = lax.axis_size("pts"), lax.axis_size("cols")
    pairs = [
        (point * columns + column, (point ^ 1) * columns + (column + steps) % columns)
        for point in range(points)
        for column in range(columns)
    ]
    return lax.ppermute(value, ("pts", "cols"), pairs)


def swapped(value, even_bits, odd_bits):
    count = lax.axis_size("pts")
    pairs = [(source, source ^ (odd_bits if source % 2 else even_bits)) for source in range(count)]
    return lax.ppermute(value, "pts", pairs)


def chip_sum(value, beside):
    count = lax.axis_size("pts")
    bit = 2
    while bit < count:
        if 2 * bit < count:
            for _ in range(2):
                near = swapped(value, 1, 1)
                value = near + swapped(value, bit ^ 1, 2 * bit ^ 1)
                value, beside = lax.optimization_barrier((value, beside))
        else:
            value = value + swapped(value, bit, bit)
        bit *= 4
    return value, beside


def two_parts(value):
    high = value.astype(jnp.bfloat16)
    return high, (value - high.astype(F32)).astype(jnp.bfloat16)


def first_columns(parts, columns):
    return parts[0][:, :columns], parts[1][:, :columns]


def product(left, right, left_axis=1, right_axis=0):
    return lax.dot_general(
        jnp.concatenate([left[0], left[0], left[1]], axis=left_axis),
        jnp.concatenate([right[0], right[1], right[0]], axis=right_axis),
        (((left_axis,), (right_axis,)), ((), ())),
        preferred_element_type=F32,
    )


def halves_swapped(value):
    half = value.shape[0] // 2
    return jnp.concatenate([value[half:], value[:half]], axis=0)


def times_inverse_root(left, square, scale, columns):
    rows = lax.broadcasted_iota(jnp.int32, square.shape, 0)
    identity = jnp.where(rows == lax.broadcasted_iota(jnp.int32, square.shape, 1), 1.0, 0.0)
    base = (identity + square) * (1.0 / scale)
    base_parts = two_parts(base)
    left_parts = two_parts(left)
    second = product(base_parts, base_parts)
    left_base = product(left_parts, base_parts)
    first_square = two_parts(2.25 * identity - 1.5 * base + 0.25 * second)
    cubic = product(two_parts(1.5 * base - 0.5 * second), first_square)
    both = two_parts(2.25 * identity - 0.75 * base - 0.5 * cubic)
    both_first = first_columns(both, columns)
    both_square = product(both, both_first)
    left_cubic = product(two_parts(left_base), both)
    left_both = product(left_parts, both_first)
    left_last = product(two_parts(left_cubic), two_parts(both_square))
    return (1.5 * left_both - 0.5 * left_last) * lax.rsqrt(scale)


def joined(own, other):
    return jnp.concatenate([own, halves_swapped(other)], axis=1)


def own_half(half):
    own = (lax.axis_index("pts") % 2) * half
    return pl.multiple_of(own, half), pl.multiple_of(half - own, half)


def start_blocks(near, far):
    width = near.shape[1] // 2
    own, other = own_half(width // 2)

    def taken(start):
        piece = (slice(None), pl.ds(start, width // 2))
        return jnp.concatenate([near[piece], far[piece]], axis=0)

    upper = jnp.concatenate([taken(own), taken(other)], axis=1)
    return upper, jnp.concatenate([taken(width + own), taken(width + other)], axis=1)


def later_blocks(upper, own, other):
    return upper[...], jnp.concatenate([halves_swapped(own[...]), other[...]], axis=1)


def stored(ref, value):
    half = ref.shape[1] // 2
    own, other = own_half(half)
    ref[:, pl.ds(own, half)] = value[:, :half]
    ref[:, pl.ds(other, half)] = value[:, half:]


def norm_rows(norm_lower, norm_upper, norm_upper_other):
    rows = lax.broadcasted_iota(jnp.int32, (8, norm_lower.shape[1]), 0)
    uppers = jnp.where(rows == 1, norm_upper, jnp.where(rows == 2, norm_upper_other, 0.0))
    return jnp.where(rows == 0, norm_lower, uppers)


def start_kernel(near_ref, weight_ref, own_part, other_part, near, weight, near_sent, weight_sent):
    copies = [
        pltpu.make_async_copy(near_ref, near, near_sent),
        pltpu.make_async_copy(weight_ref, weight, weight_sent),
    ]
    for copy in copies:
        copy.start()
    for copy in copies:
        copy.wait()
    width = near.shape[1] // 2
    half = width // 2
    own, other = own_half(half)
    point_weight = jnp.broadcast_to(weight[...], (8, weight.shape[1])).T[:, 0:1]
    upper_own, upper_other = near[:, pl.ds(own, half)], near[:, pl.ds(other, half)]
    upper_parts = two_parts(jnp.concatenate([upper_own, upper_other], axis=1))
    orders = ((upper_own, upper_other), (upper_other, upper_own))
    for start, order, out in zip((own, other), orders, (own_part, other_part)):
        lower = near[:, pl.ds(width + start, half)]
        weighted = point_weight * lower
        gram = product(upper_parts, two_parts(weighted), 0, 0)
        out[:width] = gram if out is own_part else halves_swapped(gram)
        norm_lower = jnp.sum(weighted * lower, axis=0, keepdims=True)
        uppers = [jnp.sum(point_weight * value * value, axis=0, keepdims=True) for value in order]
        out[width:] = norm_rows(norm_lower, *uppers)


def taken_rows(last, rows):
    return slice(rows, 2 * rows) if last else slice(0, rows)


def half_kernel(blocks, step, last, damps, own_sum, *refs):
    *block_refs, own_coupling, left_scale, own_mixed = refs
    width, half = own_coupling.shape
    upper, lower = blocks(*block_refs)
    inverse = lax.rsqrt(own_sum[width:] + EPSILON)
    uppers = jnp.broadcast_to(jnp.concatenate([inverse[1:2], inverse[2:3]], axis=1), (8, width))
    scaled = damps[step : step + 1, 0:1] * uppers.T[:, 0:1]
    left_scale[...] = jnp.broadcast_to(scaled, left_scale.shape)
    coupling = own_sum[:width] * scaled * inverse[0:1]
    own_coupling[...] = coupling
    taken = taken_rows(last, own_mixed.shape[0])
    own_mixed[...] = lower[taken, :half] + product(two_parts(upper[taken]), two_parts(coupling))


def lower_kernel(blocks, last, own_coupling, left_scale, own_mixed, other_sum, *refs):
    *block_refs, moved, other_coupling, scale_out = refs
    width, half = own_coupling.shape
    upper, lower = blocks(*block_refs)
    inverse = lax.rsqrt(other_sum[width : width + 1] + EPSILON)
    coupling = halves_swapped(other_sum[:width]) * left_scale[...] * inverse
    other_coupling[...] = coupling
    other_parts = two_parts(coupling)
    parts = [jnp.concatenate(pair, axis=1) for pair in zip(two_parts(own_coupling[...]), other_parts)]
    square = product(parts, parts, 0, 0)
    both = own_coupling[...] ** 2 + coupling**2
    scale = 1.0 + jnp.sum(both, keepdims=True)
    scale_out[...] = jnp.broadcast_to(scale, scale_out.shape)
    rows, columns = moved.shape
    taken = taken_rows(last, rows)
    other_mixed = lower[taken, half:] + product(two_parts(upper[taken]), other_parts)
    mixed = jnp.concatenate([own_mixed[...], other_mixed], axis=1)
    result = times_inverse_root(mixed, square, scale, columns)
    if last:
        stored(moved, result)
    else:
        moved[...] = result


def rotated_upper(blocks, rows, own_coupling, other_coupling, scale_ref, *block_refs):
    coupling = jnp.concatenate([own_coupling[...], other_coupling[...]], axis=1)
    upper, lower = blocks(*block_refs)
    parts = two_parts(coupling)
    mixed = upper[:rows] - product(two_parts(lower[:rows]), parts, 1, 1)
    square = product(parts, parts, 1, 1)
    return times_inverse_root(mixed, square, scale_ref[0:1, 0:1], coupling.shape[1])


def upper_kernel(blocks, weight, *refs):
    *ins, gram_left, norm_out, upper_out = refs
    upper = rotated_upper(blocks, upper_out.shape[0], *ins)
    upper_out[...] = upper
    weighted = weight[...] * upper
    norm_out[...] = jnp.sum(weighted * upper, axis=0, keepdims=True)
    high, low = two_parts(weighted.T)
    gram_left[...] = jnp.concatenate([high, high, low], axis=1)


def last_upper_kernel(blocks, *refs):
    *ins, out, held, sent = refs
    stored(held, rotated_upper(blocks, held.shape[0], *ins))
    copy = pltpu.make_async_copy(held, out.at[:, pl.ds(0, held.shape[1])], sent)
    copy.start()
    copy.wait()


def last_lower_kernel(lower, filled, out, sent):
    del filled
    width = lower.shape[1]
    copy = pltpu.make_async_copy(lower, out.at[:, pl.ds(width, width)], sent)
    copy.start()
    copy.wait()


def gram_kernel(gram_left, norm_upper, weight, own_ref, payload):
    width = gram_left.shape[0]
    own = halves_swapped(own_ref[...])
    high, low = two_parts(own)
    right = jnp.concatenate([high, low, high], axis=0)
    payload[:width] = jnp.dot(gram_left[...], right, preferred_element_type=F32)
    norm_lower = jnp.sum(weight[...] * own * own, axis=0, keepdims=True)
    half = own.shape[1]
    payload[width:] = norm_rows(norm_lower, norm_upper[:, :half], norm_upper[:, half:])


ON_CHIP = pl.BlockSpec(memory_space=pltpu.VMEM)
ANYWHERE = pl.BlockSpec(memory_space=pl.ANY)
GRANT = pltpu.CompilerParams(vmem_limit_bytes=24 << 20)


def in_vmem(kernel, outs, *args):
    return pl.pallas_call(
        kernel,
        out_shape=[jax.ShapeDtypeStruct(shape, dtype) for shape, dtype in outs],
        in_specs=[ON_CHIP] * len(args),
        out_specs=[ON_CHIP] * len(outs),
        compiler_params=GRANT,
    )(*args)


def body(snapshot, weights, damping):
    rows, columns = snapshot.shape
    width = columns // 2
    half = width // 2
    whole = (2 * rows, width)
    own_part, other_part = pl.pallas_call(
        start_kernel,
        out_shape=[jax.ShapeDtypeStruct((width + 8, half), F32)] * 2,
        in_specs=[pl.BlockSpec(memory_space=pltpu.HBM)] * 2,
        out_specs=[ON_CHIP] * 2,
        scratch_shapes=[
            pltpu.VMEM((rows, columns), F32),
            pltpu.VMEM((1, rows), F32),
            pltpu.SemaphoreType.DMA(()),
            pltpu.SemaphoreType.DMA(()),
        ],
        compiler_params=GRANT,
    )(*(pltpu.with_memory_space_constraint(value, pltpu.HBM) for value in (snapshot, weights[None])))
    own_part, other_part, damping = lax.optimization_barrier((own_part, other_part, damping))
    payload = own_part + swapped(other_part, 1, 1)
    weight = jnp.concatenate([weights, swapped(weights, 1, 1)])[:, None]
    blocks, held, arriving = start_blocks, (snapshot,), swapped(snapshot, 1, 1)
    damps = damping[:, 0].astype(F32) / (damping[:, 0] + damping[:, 1]).astype(F32)
    damps = lax.optimization_barrier(jnp.broadcast_to(damps[:, None], (STEPS, 128)))
    for step in range(STEPS):
        last = step + 1 == STEPS
        payload, arriving = chip_sum(payload, arriving)
        held = held + (arriving,)
        remote = swapped(payload, 1, 1)
        shape = (rows, width) if last else (2 * rows, half)
        pieces = in_vmem(
            functools.partial(half_kernel, blocks, step, last),
            [((width, half), F32), ((width, half), F32), ((shape[0], half), F32)],
            damps,
            payload,
            *held,
        )
        moved, other_coupling, scale = in_vmem(
            functools.partial(lower_kernel, blocks, last),
            [(shape, F32), ((width, half), F32), ((8, 128), F32)],
            *pieces,
            remote,
            *held,
        )
        coupling = (pieces[0], other_coupling)
        if last:
            break
        moved = column_shift(moved, 1)
        gram_left, norm_upper, upper = in_vmem(
            functools.partial(upper_kernel, blocks),
            [((width, 6 * rows), jnp.bfloat16), ((1, width), F32), (whole, F32)],
            weight,
            *coupling,
            scale,
            *held,
        )
        blocks, held, arriving = later_blocks, (upper, moved), swapped(moved, 1, 1)
        (payload,) = in_vmem(gram_kernel, [((width + 8, half), F32)], gram_left, norm_upper, weight, moved)
    moved = column_shift(moved, 1 - STEPS)
    out_shape = jax.ShapeDtypeStruct((rows, columns), F32)
    rotated = pl.pallas_call(
        functools.partial(last_upper_kernel, blocks),
        out_shape=out_shape,
        in_specs=[ON_CHIP] * (3 + len(held)),
        out_specs=ANYWHERE,
        scratch_shapes=[pltpu.VMEM((rows, width), F32), pltpu.SemaphoreType.DMA(())],
        compiler_params=GRANT,
    )(*coupling, scale, *held)
    return pl.pallas_call(
        last_lower_kernel,
        out_shape=out_shape,
        in_specs=[ON_CHIP, ANYWHERE],
        out_specs=ANYWHERE,
        scratch_shapes=[pltpu.SemaphoreType.DMA(())],
        input_output_aliases={1: 0},
        compiler_params=GRANT,
    )(moved, rotated)


def solution(mesh):
    placed = (P("pts", "cols"), P("pts"), P())
    return jax.shard_map(
        body, mesh=mesh, in_specs=placed, out_specs=P("pts", "cols"), check_vma=False
    )
```

```python
import functools

import jax
import jax.numpy as jnp
from jax import lax
from jax.experimental import pallas as pl
from jax.experimental.pallas import tpu as pltpu
from jax.sharding import PartitionSpec as P

STEPS = 3
EPSILON = 1e-06
F32 = jnp.float32


def column_shift(value, steps):
    points, columns = lax.axis_size("pts"), lax.axis_size("cols")
    pairs = [
        (point * columns + column, (point ^ 1) * columns + (column + steps) % columns)
        for point in range(points)
        for column in range(columns)
    ]
    return lax.ppermute(value, ("pts", "cols"), pairs)


def swapped(value, even_bits, odd_bits):
    count = lax.axis_size("pts")
    pairs = [(source, source ^ (odd_bits if source % 2 else even_bits)) for source in range(count)]
    return lax.ppermute(value, "pts", pairs)


def chip_sum(value, beside):
    count = lax.axis_size("pts")
    bit = 2
    while bit < count:
        if 2 * bit < count:
            for _ in range(2):
                near = swapped(value, 1, 1)
                value = near + swapped(value, bit ^ 1, 2 * bit ^ 1)
                value, beside = lax.optimization_barrier((value, beside))
        else:
            value = value + swapped(value, bit, bit)
        bit *= 4
    return value, beside


def two_parts(value):
    high = value.astype(jnp.bfloat16)
    return high, (value - high.astype(F32)).astype(jnp.bfloat16)


def first_columns(parts, columns):
    return parts[0][:, :columns], parts[1][:, :columns]


def product(left, right, left_axis=1, right_axis=0):
    return lax.dot_general(
        jnp.concatenate([left[0], left[0], left[1]], axis=left_axis),
        jnp.concatenate([right[0], right[1], right[0]], axis=right_axis),
        (((left_axis,), (right_axis,)), ((), ())),
        preferred_element_type=F32,
    )


def halves_swapped(value):
    half = value.shape[0] // 2
    return jnp.concatenate([value[half:], value[:half]], axis=0)


def times_inverse_root(left, square, scale, columns):
    rows = lax.broadcasted_iota(jnp.int32, square.shape, 0)
    identity = jnp.where(rows == lax.broadcasted_iota(jnp.int32, square.shape, 1), 1.0, 0.0)
    base = (identity + square) * (1.0 / scale)
    base_parts = two_parts(base)
    left_parts = two_parts(left)
    second = product(base_parts, base_parts)
    left_base = product(left_parts, base_parts)
    first_square = two_parts(2.25 * identity - 1.5 * base + 0.25 * second)
    cubic = product(two_parts(1.5 * base - 0.5 * second), first_square)
    both = two_parts(2.25 * identity - 0.75 * base - 0.5 * cubic)
    both_first = first_columns(both, columns)
    both_square = product(both, both_first)
    left_cubic = product(two_parts(left_base), both)
    left_both = product(left_parts, both_first)
    left_last = product(two_parts(left_cubic), two_parts(both_square))
    return (1.5 * left_both - 0.5 * left_last) * lax.rsqrt(scale)


def joined(own, other):
    return jnp.concatenate([own, halves_swapped(other)], axis=1)


def own_half(half):
    own = (lax.axis_index("pts") % 2) * half
    return pl.multiple_of(own, half), pl.multiple_of(half - own, half)


def start_blocks(near, far):
    width = near.shape[1] // 2
    own, other = own_half(width // 2)

    def taken(start):
        piece = (slice(None), pl.ds(start, width // 2))
        return jnp.concatenate([near[piece], far[piece]], axis=0)

    upper = jnp.concatenate([taken(own), taken(other)], axis=1)
    return upper, jnp.concatenate([taken(width + own), taken(width + other)], axis=1)


def later_blocks(upper, own, other):
    return upper[...], jnp.concatenate([halves_swapped(own[...]), other[...]], axis=1)


def stored(ref, value):
    half = ref.shape[1] // 2
    own, other = own_half(half)
    ref[:, pl.ds(own, half)] = value[:, :half]
    ref[:, pl.ds(other, half)] = value[:, half:]


def norm_rows(norm_lower, norm_upper, norm_upper_other):
    rows = lax.broadcasted_iota(jnp.int32, (8, norm_lower.shape[1]), 0)
    uppers = jnp.where(rows == 1, norm_upper, jnp.where(rows == 2, norm_upper_other, 0.0))
    return jnp.where(rows == 0, norm_lower, uppers)


def start_kernel(near_ref, weight_ref, own_part, other_part, near, weight, near_sent, weight_sent):
    copies = [
        pltpu.make_async_copy(near_ref, near, near_sent),
        pltpu.make_async_copy(weight_ref, weight, weight_sent),
    ]
    for copy in copies:
        copy.start()
    for copy in copies:
        copy.wait()
    width = near.shape[1] // 2
    half = width // 2
    own, other = own_half(half)
    point_weight = jnp.broadcast_to(weight[...], (8, weight.shape[1])).T[:, 0:1]
    upper_own, upper_other = near[:, pl.ds(own, half)], near[:, pl.ds(other, half)]
    upper_parts = two_parts(jnp.concatenate([upper_own, upper_other], axis=1))
    orders = ((upper_own, upper_other), (upper_other, upper_own))
    for start, order, out in zip((own, other), orders, (own_part, other_part)):
        lower = near[:, pl.ds(width + start, half)]
        weighted = point_weight * lower
        gram = product(upper_parts, two_parts(weighted), 0, 0)
        out[:width] = gram if out is own_part else halves_swapped(gram)
        norm_lower = jnp.sum(weighted * lower, axis=0, keepdims=True)
        uppers = [jnp.sum(point_weight * value * value, axis=0, keepdims=True) for value in order]
        out[width:] = norm_rows(norm_lower, *uppers)


def taken_rows(last, rows):
    return slice(rows, 2 * rows) if last else slice(0, rows)


def half_kernel(blocks, step, last, damps, own_sum, *refs):
    *block_refs, own_coupling, own_high, own_low, upper_high, upper_low, left_scale, square, norm, own_mixed = refs
    width, half = own_coupling.shape
    upper, lower = blocks(*block_refs)
    inverse = lax.rsqrt(own_sum[width:] + EPSILON)
    uppers = jnp.broadcast_to(jnp.concatenate([inverse[1:2], inverse[2:3]], axis=1), (8, width))
    scaled = damps[step : step + 1, 0:1] * uppers.T[:, 0:1]
    left_scale[...] = jnp.broadcast_to(scaled, left_scale.shape)
    coupling = own_sum[:width] * scaled * inverse[0:1]
    own_coupling[...] = coupling
    norm[...] = jnp.sum(coupling * coupling, axis=0, keepdims=True)
    parts = own_high[...], own_low[...] = two_parts(coupling)
    square[...] = product(parts, parts, 0, 0)
    taken = taken_rows(last, own_mixed.shape[0])
    upper_parts = upper_high[...], upper_low[...] = two_parts(upper[taken])
    own_mixed[...] = lower[taken, :half] + product(upper_parts, parts)


def lower_kernel(
    blocks, last, own_high, own_low, upper_high, upper_low, left_scale, own_square, norm, own_mixed, other_sum, *refs
):
    *block_refs, moved, other_coupling, scale_out = refs
    width, half = own_high.shape
    _, lower = blocks(*block_refs)
    inverse = lax.rsqrt(other_sum[width : width + 1] + EPSILON)
    coupling = halves_swapped(other_sum[:width]) * left_scale[...] * inverse
    other_coupling[...] = coupling
    other_parts = two_parts(coupling)
    own_parts = own_high[...], own_low[...]
    parts = [jnp.concatenate(pair, axis=1) for pair in zip(own_parts, other_parts)]
    crossed = product(other_parts, own_parts, 0, 0)
    square = jnp.concatenate(
        [jnp.concatenate([own_square[...], crossed], axis=0), product(parts, other_parts, 0, 0)], axis=1
    )
    norms = norm[...] + jnp.sum(coupling * coupling, axis=0, keepdims=True)
    scale = 1.0 + jnp.sum(norms, keepdims=True)
    scale_out[...] = jnp.broadcast_to(scale, scale_out.shape)
    rows, columns = moved.shape
    taken = taken_rows(last, rows)
    other_mixed = lower[taken, half:] + product((upper_high[...], upper_low[...]), other_parts)
    mixed = jnp.concatenate([own_mixed[...], other_mixed], axis=1)
    result = times_inverse_root(mixed, square, scale, columns)
    if last:
        stored(moved, result)
    else:
        moved[...] = result


def rotated_upper(blocks, rows, own_coupling, other_coupling, scale_ref, *block_refs):
    coupling = jnp.concatenate([own_coupling[...], other_coupling[...]], axis=1)
    upper, lower = blocks(*block_refs)
    parts = two_parts(coupling)
    mixed = upper[:rows] - product(two_parts(lower[:rows]), parts, 1, 1)
    square = product(parts, parts, 1, 1)
    return times_inverse_root(mixed, square, scale_ref[0:1, 0:1], coupling.shape[1])


def upper_kernel(blocks, weight, *refs):
    *ins, gram_left, norm_out, upper_out = refs
    upper = rotated_upper(blocks, upper_out.shape[0], *ins)
    upper_out[...] = upper
    weighted = weight[...] * upper
    norm_out[...] = jnp.sum(weighted * upper, axis=0, keepdims=True)
    high, low = two_parts(weighted.T)
    gram_left[...] = jnp.concatenate([high, high, low], axis=1)


def last_upper_kernel(blocks, *refs):
    *ins, out, held, sent = refs
    stored(held, rotated_upper(blocks, held.shape[0], *ins))
    copy = pltpu.make_async_copy(held, out.at[:, pl.ds(0, held.shape[1])], sent)
    copy.start()
    copy.wait()


def last_lower_kernel(lower, filled, out, sent):
    del filled
    width = lower.shape[1]
    copy = pltpu.make_async_copy(lower, out.at[:, pl.ds(width, width)], sent)
    copy.start()
    copy.wait()


def gram_kernel(gram_left, norm_upper, weight, own_ref, payload):
    width = gram_left.shape[0]
    own = halves_swapped(own_ref[...])
    high, low = two_parts(own)
    right = jnp.concatenate([high, low, high], axis=0)
    payload[:width] = jnp.dot(gram_left[...], right, preferred_element_type=F32)
    norm_lower = jnp.sum(weight[...] * own * own, axis=0, keepdims=True)
    half = own.shape[1]
    payload[width:] = norm_rows(norm_lower, norm_upper[:, :half], norm_upper[:, half:])


ON_CHIP = pl.BlockSpec(memory_space=pltpu.VMEM)
ANYWHERE = pl.BlockSpec(memory_space=pl.ANY)
GRANT = pltpu.CompilerParams(vmem_limit_bytes=24 << 20)


def in_vmem(kernel, outs, *args):
    return pl.pallas_call(
        kernel,
        out_shape=[jax.ShapeDtypeStruct(shape, dtype) for shape, dtype in outs],
        in_specs=[ON_CHIP] * len(args),
        out_specs=[ON_CHIP] * len(outs),
        compiler_params=GRANT,
    )(*args)


def body(snapshot, weights, damping):
    rows, columns = snapshot.shape
    width = columns // 2
    half = width // 2
    whole = (2 * rows, width)
    own_part, other_part = pl.pallas_call(
        start_kernel,
        out_shape=[jax.ShapeDtypeStruct((width + 8, half), F32)] * 2,
        in_specs=[pl.BlockSpec(memory_space=pltpu.HBM)] * 2,
        out_specs=[ON_CHIP] * 2,
        scratch_shapes=[
            pltpu.VMEM((rows, columns), F32),
            pltpu.VMEM((1, rows), F32),
            pltpu.SemaphoreType.DMA(()),
            pltpu.SemaphoreType.DMA(()),
        ],
        compiler_params=GRANT,
    )(*(pltpu.with_memory_space_constraint(value, pltpu.HBM) for value in (snapshot, weights[None])))
    own_part, other_part, damping = lax.optimization_barrier((own_part, other_part, damping))
    payload = own_part + swapped(other_part, 1, 1)
    weight = jnp.concatenate([weights, swapped(weights, 1, 1)])[:, None]
    blocks, held, arriving = start_blocks, (snapshot,), swapped(snapshot, 1, 1)
    damps = damping[:, 0].astype(F32) / (damping[:, 0] + damping[:, 1]).astype(F32)
    damps = lax.optimization_barrier(jnp.broadcast_to(damps[:, None], (STEPS, 128)))
    for step in range(STEPS):
        last = step + 1 == STEPS
        payload, arriving = chip_sum(payload, arriving)
        held = held + (arriving,)
        remote = swapped(payload, 1, 1)
        shape = (rows, width) if last else (2 * rows, half)
        pieces = in_vmem(
            functools.partial(half_kernel, blocks, step, last),
            [((width, half), F32)]
            + [((width, half), jnp.bfloat16)] * 2
            + [((shape[0], width), jnp.bfloat16)] * 2
            + [((width, half), F32), ((half, half), F32), ((1, half), F32), ((shape[0], half), F32)],
            damps,
            payload,
            *held,
        )
        moved, other_coupling, scale = in_vmem(
            functools.partial(lower_kernel, blocks, last),
            [(shape, F32), ((width, half), F32), ((8, 128), F32)],
            *pieces[1:],
            remote,
            *held,
        )
        coupling = (pieces[0], other_coupling)
        if last:
            break
        moved = column_shift(moved, 1)
        gram_left, norm_upper, upper = in_vmem(
            functools.partial(upper_kernel, blocks),
            [((width, 6 * rows), jnp.bfloat16), ((1, width), F32), (whole, F32)],
            weight,
            *coupling,
            scale,
            *held,
        )
        blocks, held, arriving = later_blocks, (upper, moved), swapped(moved, 1, 1)
        (payload,) = in_vmem(gram_kernel, [((width + 8, half), F32)], gram_left, norm_upper, weight, moved)
    moved = column_shift(moved, 1 - STEPS)
    out_shape = jax.ShapeDtypeStruct((rows, columns), F32)
    rotated = pl.pallas_call(
        functools.partial(last_upper_kernel, blocks),
        out_shape=out_shape,
        in_specs=[ON_CHIP] * (3 + len(held)),
        out_specs=ANYWHERE,
        scratch_shapes=[pltpu.VMEM((rows, width), F32), pltpu.SemaphoreType.DMA(())],
        compiler_params=GRANT,
    )(*coupling, scale, *held)
    return pl.pallas_call(
        last_lower_kernel,
        out_shape=out_shape,
        in_specs=[ON_CHIP, ANYWHERE],
        out_specs=ANYWHERE,
        scratch_shapes=[pltpu.SemaphoreType.DMA(())],
        input_output_aliases={1: 0},
        compiler_params=GRANT,
    )(moved, rotated)


def solution(mesh):
    placed = (P("pts", "cols"), P("pts"), P())
    return jax.shard_map(
        body, mesh=mesh, in_specs=placed, out_specs=P("pts", "cols"), check_vma=False
    )
```

```python
import functools

import jax
import jax.numpy as jnp
from jax import lax
from jax.experimental import pallas as pl
from jax.experimental.pallas import tpu as pltpu
from jax.sharding import PartitionSpec as P

STEPS = 3
EPSILON = 1e-06
F32 = jnp.float32


def column_shift(value, steps):
    points, columns = lax.axis_size("pts"), lax.axis_size("cols")
    pairs = [
        (point * columns + column, (point ^ 1) * columns + (column + steps) % columns)
        for point in range(points)
        for column in range(columns)
    ]
    return lax.ppermute(value, ("pts", "cols"), pairs)


def swapped(value, even_bits, odd_bits):
    count = lax.axis_size("pts")
    pairs = [(source, source ^ (odd_bits if source % 2 else even_bits)) for source in range(count)]
    return lax.ppermute(value, "pts", pairs)


def chip_sum(value, beside):
    count = lax.axis_size("pts")
    bit = 2
    own, known, needed = (value,), (), value
    while bit < count:
        if 2 * bit < count:
            for _ in range(2):
                near = swapped(value, 1, 1)
                far = swapped(value, bit ^ 1, 2 * bit ^ 1)
                own, known, needed = (near, far), (value,), far
                value = near + far
                value, beside = lax.optimization_barrier((value, beside))
        else:
            value = value + swapped(value, bit, bit)
            own, known, needed = (value,), (), value
        bit *= 4
    return own, known, needed, beside


def two_parts(value):
    high = value.astype(jnp.bfloat16)
    return high, (value - high.astype(F32)).astype(jnp.bfloat16)


def first_columns(parts, columns):
    return parts[0][:, :columns], parts[1][:, :columns]


def product(left, right, left_axis=1, right_axis=0):
    return lax.dot_general(
        jnp.concatenate([left[0], left[0], left[1]], axis=left_axis),
        jnp.concatenate([right[0], right[1], right[0]], axis=right_axis),
        (((left_axis,), (right_axis,)), ((), ())),
        preferred_element_type=F32,
    )


def halves_swapped(value):
    half = value.shape[0] // 2
    return jnp.concatenate([value[half:], value[:half]], axis=0)


def times_inverse_root(left_parts, square, scale, columns):
    rows = lax.broadcasted_iota(jnp.int32, square.shape, 0)
    identity = jnp.where(rows == lax.broadcasted_iota(jnp.int32, square.shape, 1), 1.0, 0.0)
    base = (identity + square) * (1.0 / scale)
    base_parts = two_parts(base)
    second = product(base_parts, base_parts)
    left_base = product(left_parts, base_parts)
    first_square = two_parts(2.25 * identity - 1.5 * base + 0.25 * second)
    cubic = product(two_parts(1.5 * base - 0.5 * second), first_square)
    both = two_parts(2.25 * identity - 0.75 * base - 0.5 * cubic)
    both_first = first_columns(both, columns)
    both_square = product(both, both_first)
    left_cubic = product(two_parts(left_base), both)
    left_both = product(left_parts, both_first)
    left_last = product(two_parts(left_cubic), two_parts(both_square))
    return (1.5 * left_both - 0.5 * left_last) * lax.rsqrt(scale)


def joined(own, other):
    return jnp.concatenate([own, halves_swapped(other)], axis=1)


def own_half(half):
    own = (lax.axis_index("pts") % 2) * half
    return pl.multiple_of(own, half), pl.multiple_of(half - own, half)


def start_blocks(near, far):
    width = near.shape[1] // 2
    own, other = own_half(width // 2)

    def taken(start):
        piece = (slice(None), pl.ds(start, width // 2))
        return jnp.concatenate([near[piece], far[piece]], axis=0)

    upper = jnp.concatenate([taken(own), taken(other)], axis=1)
    return upper, jnp.concatenate([taken(width + own), taken(width + other)], axis=1)


def later_blocks(upper, own, other):
    return upper[...], jnp.concatenate([halves_swapped(own[...]), other[...]], axis=1)


def stored(ref, value):
    half = ref.shape[1] // 2
    own, other = own_half(half)
    ref[:, pl.ds(own, half)] = value[:, :half]
    ref[:, pl.ds(other, half)] = value[:, half:]


def norm_rows(norm_lower, norm_upper, norm_upper_other):
    rows = lax.broadcasted_iota(jnp.int32, (8, norm_lower.shape[1]), 0)
    uppers = jnp.where(rows == 1, norm_upper, jnp.where(rows == 2, norm_upper_other, 0.0))
    return jnp.where(rows == 0, norm_lower, uppers)


def start_kernel(near_ref, weight_ref, own_part, other_part, near, weight, near_sent, weight_sent):
    copies = [
        pltpu.make_async_copy(near_ref, near, near_sent),
        pltpu.make_async_copy(weight_ref, weight, weight_sent),
    ]
    for copy in copies:
        copy.start()
    for copy in copies:
        copy.wait()
    width = near.shape[1] // 2
    half = width // 2
    own, other = own_half(half)
    point_weight = jnp.broadcast_to(weight[...], (8, weight.shape[1])).T[:, 0:1]
    upper_own, upper_other = near[:, pl.ds(own, half)], near[:, pl.ds(other, half)]
    upper_parts = two_parts(jnp.concatenate([upper_own, upper_other], axis=1))
    orders = ((upper_own, upper_other), (upper_other, upper_own))
    for start, order, out in zip((own, other), orders, (own_part, other_part)):
        lower = near[:, pl.ds(width + start, half)]
        weighted = point_weight * lower
        gram = product(upper_parts, two_parts(weighted), 0, 0)
        out[:width] = gram if out is own_part else halves_swapped(gram)
        norm_lower = jnp.sum(weighted * lower, axis=0, keepdims=True)
        uppers = [jnp.sum(point_weight * value * value, axis=0, keepdims=True) for value in order]
        out[width:] = norm_rows(norm_lower, *uppers)


def taken_rows(last, rows):
    return slice(rows, 2 * rows) if last else slice(0, rows)


def total(refs):
    return sum((ref[...] for ref in refs[1:]), refs[0][...])


def half_kernel(addends, blocks, step, last, damps, *refs):
    *ins, own_coupling, own_high, own_low, upper_high, upper_low, left_scale, square, norm, high, low = refs
    own_sum, block_refs = total(ins[:addends]), ins[addends:]
    width, half = own_coupling.shape
    upper, lower = blocks(*block_refs)
    inverse = lax.rsqrt(own_sum[width:] + EPSILON)
    uppers = jnp.broadcast_to(jnp.concatenate([inverse[1:2], inverse[2:3]], axis=1), (8, width))
    scaled = damps[step : step + 1, 0:1] * uppers.T[:, 0:1]
    left_scale[...] = jnp.broadcast_to(scaled, left_scale.shape)
    coupling = own_sum[:width] * scaled * inverse[0:1]
    own_coupling[...] = coupling
    norm[...] = jnp.sum(coupling * coupling, axis=0, keepdims=True)
    parts = own_high[...], own_low[...] = two_parts(coupling)
    square[...] = product(parts, parts, 0, 0)
    taken = taken_rows(last, high.shape[0])
    upper_parts = upper_high[...], upper_low[...] = two_parts(upper[taken])
    high[...], low[...] = two_parts(lower[taken, :half] + product(upper_parts, parts))


def lower_kernel(
    addends, blocks, last, own_high, own_low, upper_high, upper_low, left_scale, own_square, norm, high, low, *refs
):
    *ins, moved, other_coupling, scale_out = refs
    other_sum, block_refs = total(ins[:addends]), ins[addends:]
    width, half = own_high.shape
    _, lower = blocks(*block_refs)
    inverse = lax.rsqrt(other_sum[width : width + 1] + EPSILON)
    coupling = halves_swapped(other_sum[:width]) * left_scale[...] * inverse
    other_coupling[...] = coupling
    other_parts = two_parts(coupling)
    own_parts = own_high[...], own_low[...]
    parts = [jnp.concatenate(pair, axis=1) for pair in zip(own_parts, other_parts)]
    crossed = product(other_parts, own_parts, 0, 0)
    square = jnp.concatenate(
        [jnp.concatenate([own_square[...], crossed], axis=0), product(parts, other_parts, 0, 0)], axis=1
    )
    norms = norm[...] + jnp.sum(coupling * coupling, axis=0, keepdims=True)
    scale = 1.0 + jnp.sum(norms, keepdims=True)
    scale_out[...] = jnp.broadcast_to(scale, scale_out.shape)
    rows, columns = moved.shape
    taken = taken_rows(last, rows)
    other_mixed = lower[taken, half:] + product((upper_high[...], upper_low[...]), other_parts)
    mixed = [jnp.concatenate(pair, axis=1) for pair in zip((high[...], low[...]), two_parts(other_mixed))]
    result = times_inverse_root(mixed, square, scale, columns)
    if last:
        stored(moved, result)
    else:
        moved[...] = result


def rotated_upper(blocks, rows, own_coupling, other_coupling, scale_ref, *block_refs):
    coupling = jnp.concatenate([own_coupling[...], other_coupling[...]], axis=1)
    upper, lower = blocks(*block_refs)
    parts = two_parts(coupling)
    mixed = upper[:rows] - product(two_parts(lower[:rows]), parts, 1, 1)
    square = product(parts, parts, 1, 1)
    return times_inverse_root(two_parts(mixed), square, scale_ref[0:1, 0:1], coupling.shape[1])


def upper_kernel(blocks, weight, *refs):
    *ins, gram_left, norm_out, upper_out = refs
    upper = rotated_upper(blocks, upper_out.shape[0], *ins)
    upper_out[...] = upper
    weighted = weight[...] * upper
    norm_out[...] = jnp.sum(weighted * upper, axis=0, keepdims=True)
    high, low = two_parts(weighted.T)
    gram_left[...] = jnp.concatenate([high, high, low], axis=1)


def last_upper_kernel(blocks, *refs):
    *ins, out, held, sent = refs
    stored(held, rotated_upper(blocks, held.shape[0], *ins))
    copy = pltpu.make_async_copy(held, out.at[:, pl.ds(0, held.shape[1])], sent)
    copy.start()
    copy.wait()


def last_lower_kernel(lower, filled, out, sent):
    del filled
    width = lower.shape[1]
    copy = pltpu.make_async_copy(lower, out.at[:, pl.ds(width, width)], sent)
    copy.start()
    copy.wait()


def gram_kernel(gram_left, norm_upper, weight, own_ref, payload):
    width = gram_left.shape[0]
    own = halves_swapped(own_ref[...])
    high, low = two_parts(own)
    right = jnp.concatenate([high, low, high], axis=0)
    payload[:width] = jnp.dot(gram_left[...], right, preferred_element_type=F32)
    norm_lower = jnp.sum(weight[...] * own * own, axis=0, keepdims=True)
    half = own.shape[1]
    payload[width:] = norm_rows(norm_lower, norm_upper[:, :half], norm_upper[:, half:])


ON_CHIP = pl.BlockSpec(memory_space=pltpu.VMEM)
ANYWHERE = pl.BlockSpec(memory_space=pl.ANY)
GRANT = pltpu.CompilerParams(vmem_limit_bytes=24 << 20)


def in_vmem(kernel, outs, *args):
    return pl.pallas_call(
        kernel,
        out_shape=[jax.ShapeDtypeStruct(shape, dtype) for shape, dtype in outs],
        in_specs=[ON_CHIP] * len(args),
        out_specs=[ON_CHIP] * len(outs),
        compiler_params=GRANT,
    )(*args)


def body(snapshot, weights, damping):
    rows, columns = snapshot.shape
    width = columns // 2
    half = width // 2
    whole = (2 * rows, width)
    own_part, other_part = pl.pallas_call(
        start_kernel,
        out_shape=[jax.ShapeDtypeStruct((width + 8, half), F32)] * 2,
        in_specs=[pl.BlockSpec(memory_space=pltpu.HBM)] * 2,
        out_specs=[ON_CHIP] * 2,
        scratch_shapes=[
            pltpu.VMEM((rows, columns), F32),
            pltpu.VMEM((1, rows), F32),
            pltpu.SemaphoreType.DMA(()),
            pltpu.SemaphoreType.DMA(()),
        ],
        compiler_params=GRANT,
    )(*(pltpu.with_memory_space_constraint(value, pltpu.HBM) for value in (snapshot, weights[None])))
    own_part, other_part, damping = lax.optimization_barrier((own_part, other_part, damping))
    payload = own_part + swapped(other_part, 1, 1)
    weight = jnp.concatenate([weights, swapped(weights, 1, 1)])[:, None]
    blocks, held, arriving = start_blocks, (snapshot,), swapped(snapshot, 1, 1)
    damps = damping[:, 0].astype(F32) / (damping[:, 0] + damping[:, 1]).astype(F32)
    damps = lax.optimization_barrier(jnp.broadcast_to(damps[:, None], (STEPS, 128)))
    for step in range(STEPS):
        last = step + 1 == STEPS
        own, known, needed, arriving = chip_sum(payload, arriving)
        held = held + (arriving,)
        remote = swapped(needed, 1, 1)
        shape = (rows, width) if last else (2 * rows, half)
        pieces = in_vmem(
            functools.partial(half_kernel, len(own), blocks, step, last),
            [((width, half), F32)]
            + [((width, half), jnp.bfloat16)] * 2
            + [((shape[0], width), jnp.bfloat16)] * 2
            + [((width, half), F32), ((half, half), F32), ((1, half), F32)]
            + [((shape[0], half), jnp.bfloat16)] * 2,
            damps,
            *own,
            *held,
        )
        moved, other_coupling, scale = in_vmem(
            functools.partial(lower_kernel, len(known) + 1, blocks, last),
            [(shape, F32), ((width, half), F32), ((8, 128), F32)],
            *pieces[1:],
            *known,
            remote,
            *held,
        )
        coupling = (pieces[0], other_coupling)
        if last:
            break
        moved = column_shift(moved, 1)
        gram_left, norm_upper, upper = in_vmem(
            functools.partial(upper_kernel, blocks),
            [((width, 6 * rows), jnp.bfloat16), ((1, width), F32), (whole, F32)],
            weight,
            *coupling,
            scale,
            *held,
        )
        blocks, held, arriving = later_blocks, (upper, moved), swapped(moved, 1, 1)
        (payload,) = in_vmem(gram_kernel, [((width + 8, half), F32)], gram_left, norm_upper, weight, moved)
    moved = column_shift(moved, 1 - STEPS)
    out_shape = jax.ShapeDtypeStruct((rows, columns), F32)
    rotated = pl.pallas_call(
        functools.partial(last_upper_kernel, blocks),
        out_shape=out_shape,
        in_specs=[ON_CHIP] * (3 + len(held)),
        out_specs=ANYWHERE,
        scratch_shapes=[pltpu.VMEM((rows, width), F32), pltpu.SemaphoreType.DMA(())],
        compiler_params=GRANT,
    )(*coupling, scale, *held)
    return pl.pallas_call(
        last_lower_kernel,
        out_shape=out_shape,
        in_specs=[ON_CHIP, ANYWHERE],
        out_specs=ANYWHERE,
        scratch_shapes=[pltpu.SemaphoreType.DMA(())],
        input_output_aliases={1: 0},
        compiler_params=GRANT,
    )(moved, rotated)


def solution(mesh):
    placed = (P("pts", "cols"), P("pts"), P())
    return jax.shard_map(
        body, mesh=mesh, in_specs=placed, out_specs=P("pts", "cols"), check_vma=False
    )
```

```python
import functools

import jax
import jax.numpy as jnp
from jax import lax
from jax.experimental import pallas as pl
from jax.experimental.pallas import tpu as pltpu
from jax.sharding import PartitionSpec as P

STEPS = 3
EPSILON = 1e-06
F32 = jnp.float32


def column_shift(value, steps):
    points, columns = lax.axis_size("pts"), lax.axis_size("cols")
    pairs = [
        (point * columns + column, (point ^ 1) * columns + (column + steps) % columns)
        for point in range(points)
        for column in range(columns)
    ]
    return lax.ppermute(value, ("pts", "cols"), pairs)


def swapped(value, even_bits, odd_bits):
    count = lax.axis_size("pts")
    pairs = [(source, source ^ (odd_bits if source % 2 else even_bits)) for source in range(count)]
    return lax.ppermute(value, "pts", pairs)


def chip_sum(value, beside):
    count = lax.axis_size("pts")
    bit = 2
    own, known, needed = (value,), (), value
    while bit < count:
        if 2 * bit < count:
            for _ in range(2):
                near = swapped(value, 1, 1)
                far = swapped(value, bit ^ 1, 2 * bit ^ 1)
                own, known, needed = (near, far), (value,), far
                value = far + near
                value, beside = lax.optimization_barrier((value, beside))
        else:
            value = value + swapped(value, bit, bit)
            own, known, needed = (value,), (), value
        bit *= 4
    return own, known, needed, beside


def two_parts(value):
    high = value.astype(jnp.bfloat16)
    return high, (value - high.astype(F32)).astype(jnp.bfloat16)


def first_columns(parts, columns):
    return parts[0][:, :columns], parts[1][:, :columns]


def product(left, right, left_axis=1, right_axis=0):
    return lax.dot_general(
        jnp.concatenate([left[0], left[0], left[1]], axis=left_axis),
        jnp.concatenate([right[0], right[1], right[0]], axis=right_axis),
        (((left_axis,), (right_axis,)), ((), ())),
        preferred_element_type=F32,
    )


def halves_swapped(value):
    half = value.shape[0] // 2
    return jnp.concatenate([value[half:], value[:half]], axis=0)


def times_inverse_root(left_parts, square, scale, columns):
    rows = lax.broadcasted_iota(jnp.int32, square.shape, 0)
    identity = jnp.where(rows == lax.broadcasted_iota(jnp.int32, square.shape, 1), 1.0, 0.0)
    base = (identity + square) * (1.0 / scale)
    base_parts = two_parts(base)
    second = product(base_parts, base_parts)
    left_base = product(left_parts, base_parts)
    first_square = two_parts(2.25 * identity - 1.5 * base + 0.25 * second)
    cubic = product(two_parts(1.5 * base - 0.5 * second), first_square)
    both = two_parts(2.25 * identity - 0.75 * base - 0.5 * cubic)
    both_first = first_columns(both, columns)
    both_square = product(both, both_first)
    left_cubic = product(two_parts(left_base), both)
    left_both = product(left_parts, both_first)
    left_last = product(two_parts(left_cubic), two_parts(both_square))
    return (1.5 * left_both - 0.5 * left_last) * lax.rsqrt(scale)


def joined(own, other):
    return jnp.concatenate([own, halves_swapped(other)], axis=1)


def own_half(half):
    own = (lax.axis_index("pts") % 2) * half
    return pl.multiple_of(own, half), pl.multiple_of(half - own, half)


def start_blocks(near, far):
    width = near.shape[1] // 2
    own, other = own_half(width // 2)

    def taken(start):
        piece = (slice(None), pl.ds(start, width // 2))
        return jnp.concatenate([near[piece], far[piece]], axis=0)

    upper = jnp.concatenate([taken(own), taken(other)], axis=1)
    return upper, jnp.concatenate([taken(width + own), taken(width + other)], axis=1)


def later_blocks(upper, own, other):
    return upper[...], jnp.concatenate([halves_swapped(own[...]), other[...]], axis=1)


def stored(ref, value):
    half = ref.shape[1] // 2
    own, other = own_half(half)
    ref[:, pl.ds(own, half)] = value[:, :half]
    ref[:, pl.ds(other, half)] = value[:, half:]


def norm_rows(norm_lower, norm_upper, norm_upper_other):
    rows = lax.broadcasted_iota(jnp.int32, (8, norm_lower.shape[1]), 0)
    uppers = jnp.where(rows == 1, norm_upper, jnp.where(rows == 2, norm_upper_other, 0.0))
    return jnp.where(rows == 0, norm_lower, uppers)


def start_kernel(near_ref, weight_ref, own_part, other_part, near, weight, near_sent, weight_sent):
    copies = [
        pltpu.make_async_copy(near_ref, near, near_sent),
        pltpu.make_async_copy(weight_ref, weight, weight_sent),
    ]
    for copy in copies:
        copy.start()
    for copy in copies:
        copy.wait()
    width = near.shape[1] // 2
    half = width // 2
    own, other = own_half(half)
    point_weight = jnp.broadcast_to(weight[...], (8, weight.shape[1])).T[:, 0:1]
    upper_own, upper_other = near[:, pl.ds(own, half)], near[:, pl.ds(other, half)]
    upper_parts = two_parts(jnp.concatenate([upper_own, upper_other], axis=1))
    orders = ((upper_own, upper_other), (upper_other, upper_own))
    for start, order, out in zip((own, other), orders, (own_part, other_part)):
        lower = near[:, pl.ds(width + start, half)]
        weighted = point_weight * lower
        gram = product(upper_parts, two_parts(weighted), 0, 0)
        out[:width] = gram if out is own_part else halves_swapped(gram)
        norm_lower = jnp.sum(weighted * lower, axis=0, keepdims=True)
        uppers = [jnp.sum(point_weight * value * value, axis=0, keepdims=True) for value in order]
        out[width:] = norm_rows(norm_lower, *uppers)


def taken_rows(last, rows):
    return slice(rows, 2 * rows) if last else slice(0, rows)


def total(refs):
    return sum((ref[...] for ref in refs[1:]), refs[0][...])


def half_kernel(addends, blocks, step, last, damps, *refs):
    *ins, own_coupling, own_high, own_low, upper_high, upper_low, left_scale, square, norm, high, low = refs
    own_sum, block_refs = total(ins[:addends]), ins[addends:]
    width, half = own_coupling.shape
    upper, lower = blocks(*block_refs)
    inverse = lax.rsqrt(own_sum[width:] + EPSILON)
    uppers = jnp.broadcast_to(jnp.concatenate([inverse[1:2], inverse[2:3]], axis=1), (8, width))
    scaled = damps[step : step + 1, 0:1] * uppers.T[:, 0:1]
    left_scale[...] = jnp.broadcast_to(scaled, left_scale.shape)
    coupling = own_sum[:width] * scaled * inverse[0:1]
    own_coupling[...] = coupling
    norm[...] = jnp.sum(coupling * coupling, axis=0, keepdims=True)
    parts = own_high[...], own_low[...] = two_parts(coupling)
    square[...] = product(parts, parts, 0, 0)
    taken = taken_rows(last, high.shape[0])
    upper_parts = upper_high[...], upper_low[...] = two_parts(upper[taken])
    high[...], low[...] = two_parts(lower[taken, :half] + product(upper_parts, parts))


def lower_kernel(
    addends, blocks, last, own_high, own_low, upper_high, upper_low, left_scale, own_square, norm, high, low, *refs
):
    *ins, moved, other_coupling, scale_out = refs
    other_sum, block_refs = total(ins[:addends]), ins[addends:]
    width, half = own_high.shape
    _, lower = blocks(*block_refs)
    inverse = lax.rsqrt(other_sum[width : width + 1] + EPSILON)
    coupling = halves_swapped(other_sum[:width]) * left_scale[...] * inverse
    other_coupling[...] = coupling
    other_parts = two_parts(coupling)
    own_parts = own_high[...], own_low[...]
    parts = [jnp.concatenate(pair, axis=1) for pair in zip(own_parts, other_parts)]
    crossed = product(other_parts, own_parts, 0, 0)
    square = jnp.concatenate(
        [jnp.concatenate([own_square[...], crossed], axis=0), product(parts, other_parts, 0, 0)], axis=1
    )
    norms = norm[...] + jnp.sum(coupling * coupling, axis=0, keepdims=True)
    scale = 1.0 + jnp.sum(norms, keepdims=True)
    scale_out[...] = jnp.broadcast_to(scale, scale_out.shape)
    rows, columns = moved.shape
    taken = taken_rows(last, rows)
    other_mixed = lower[taken, half:] + product((upper_high[...], upper_low[...]), other_parts)
    mixed = [jnp.concatenate(pair, axis=1) for pair in zip((high[...], low[...]), two_parts(other_mixed))]
    result = times_inverse_root(mixed, square, scale, columns)
    if last:
        stored(moved, result)
    else:
        moved[...] = result


def rotated_upper(blocks, rows, own_coupling, other_coupling, scale_ref, *block_refs):
    coupling = jnp.concatenate([own_coupling[...], other_coupling[...]], axis=1)
    upper, lower = blocks(*block_refs)
    parts = two_parts(coupling)
    mixed = upper[:rows] - product(two_parts(lower[:rows]), parts, 1, 1)
    square = product(parts, parts, 1, 1)
    return times_inverse_root(two_parts(mixed), square, scale_ref[0:1, 0:1], coupling.shape[1])


def upper_kernel(blocks, weight, *refs):
    *ins, gram_left, norm_out, upper_out = refs
    upper = rotated_upper(blocks, upper_out.shape[0], *ins)
    upper_out[...] = upper
    weighted = weight[...] * upper
    norm_out[...] = jnp.sum(weighted * upper, axis=0, keepdims=True)
    high, low = two_parts(weighted.T)
    gram_left[...] = jnp.concatenate([high, high, low], axis=1)


def last_upper_kernel(blocks, *refs):
    *ins, out, held, sent = refs
    stored(held, rotated_upper(blocks, held.shape[0], *ins))
    copy = pltpu.make_async_copy(held, out.at[:, pl.ds(0, held.shape[1])], sent)
    copy.start()
    copy.wait()


def last_lower_kernel(lower, filled, out, sent):
    del filled
    width = lower.shape[1]
    copy = pltpu.make_async_copy(lower, out.at[:, pl.ds(width, width)], sent)
    copy.start()
    copy.wait()


def gram_kernel(gram_left, norm_upper, weight, own_ref, payload):
    width = gram_left.shape[0]
    own = halves_swapped(own_ref[...])
    high, low = two_parts(own)
    right = jnp.concatenate([high, low, high], axis=0)
    payload[:width] = jnp.dot(gram_left[...], right, preferred_element_type=F32)
    norm_lower = jnp.sum(weight[...] * own * own, axis=0, keepdims=True)
    half = own.shape[1]
    payload[width:] = norm_rows(norm_lower, norm_upper[:, :half], norm_upper[:, half:])


ON_CHIP = pl.BlockSpec(memory_space=pltpu.VMEM)
ANYWHERE = pl.BlockSpec(memory_space=pl.ANY)
GRANT = pltpu.CompilerParams(vmem_limit_bytes=24 << 20)


def in_vmem(kernel, outs, *args):
    return pl.pallas_call(
        kernel,
        out_shape=[jax.ShapeDtypeStruct(shape, dtype) for shape, dtype in outs],
        in_specs=[ON_CHIP] * len(args),
        out_specs=[ON_CHIP] * len(outs),
        compiler_params=GRANT,
    )(*args)


def body(snapshot, weights, damping):
    rows, columns = snapshot.shape
    width = columns // 2
    half = width // 2
    whole = (2 * rows, width)
    own_part, other_part = pl.pallas_call(
        start_kernel,
        out_shape=[jax.ShapeDtypeStruct((width + 8, half), F32)] * 2,
        in_specs=[pl.BlockSpec(memory_space=pltpu.HBM)] * 2,
        out_specs=[ON_CHIP] * 2,
        scratch_shapes=[
            pltpu.VMEM((rows, columns), F32),
            pltpu.VMEM((1, rows), F32),
            pltpu.SemaphoreType.DMA(()),
            pltpu.SemaphoreType.DMA(()),
        ],
        compiler_params=GRANT,
    )(*(pltpu.with_memory_space_constraint(value, pltpu.HBM) for value in (snapshot, weights[None])))
    own_part, other_part, damping = lax.optimization_barrier((own_part, other_part, damping))
    payload = own_part + swapped(other_part, 1, 1)
    weight = jnp.concatenate([weights, swapped(weights, 1, 1)])[:, None]
    blocks, held, arriving = start_blocks, (snapshot,), swapped(snapshot, 1, 1)
    damps = damping[:, 0].astype(F32) / (damping[:, 0] + damping[:, 1]).astype(F32)
    damps = lax.optimization_barrier(jnp.broadcast_to(damps[:, None], (STEPS, 128)))
    for step in range(STEPS):
        last = step + 1 == STEPS
        own, known, needed, arriving = chip_sum(payload, arriving)
        held = held + (arriving,)
        remote = swapped(needed, 1, 1)
        shape = (rows, width) if last else (2 * rows, half)
        pieces = in_vmem(
            functools.partial(half_kernel, len(own), blocks, step, last),
            [((width, half), F32)]
            + [((width, half), jnp.bfloat16)] * 2
            + [((shape[0], width), jnp.bfloat16)] * 2
            + [((width, half), F32), ((half, half), F32), ((1, half), F32)]
            + [((shape[0], half), jnp.bfloat16)] * 2,
            damps,
            *own,
            *held,
        )
        moved, other_coupling, scale = in_vmem(
            functools.partial(lower_kernel, len(known) + 1, blocks, last),
            [(shape, F32), ((width, half), F32), ((8, 128), F32)],
            *pieces[1:],
            *known,
            remote,
            *held,
        )
        coupling = (pieces[0], other_coupling)
        if last:
            break
        moved = column_shift(moved, 1)
        gram_left, norm_upper, upper = in_vmem(
            functools.partial(upper_kernel, blocks),
            [((width, 6 * rows), jnp.bfloat16), ((1, width), F32), (whole, F32)],
            weight,
            *coupling,
            scale,
            *held,
        )
        blocks, held, arriving = later_blocks, (upper, moved), swapped(moved, 1, 1)
        (payload,) = in_vmem(gram_kernel, [((width + 8, half), F32)], gram_left, norm_upper, weight, moved)
    moved = column_shift(moved, 1 - STEPS)
    out_shape = jax.ShapeDtypeStruct((rows, columns), F32)
    rotated = pl.pallas_call(
        functools.partial(last_upper_kernel, blocks),
        out_shape=out_shape,
        in_specs=[ON_CHIP] * (3 + len(held)),
        out_specs=ANYWHERE,
        scratch_shapes=[pltpu.VMEM((rows, width), F32), pltpu.SemaphoreType.DMA(())],
        compiler_params=GRANT,
    )(*coupling, scale, *held)
    return pl.pallas_call(
        last_lower_kernel,
        out_shape=out_shape,
        in_specs=[ON_CHIP, ANYWHERE],
        out_specs=ANYWHERE,
        scratch_shapes=[pltpu.SemaphoreType.DMA(())],
        input_output_aliases={1: 0},
        compiler_params=GRANT,
    )(moved, rotated)


def solution(mesh):
    placed = (P("pts", "cols"), P("pts"), P())
    return jax.shard_map(
        body, mesh=mesh, in_specs=placed, out_specs=P("pts", "cols"), check_vma=False
    )
```

```python
import functools

import jax
import jax.numpy as jnp
from jax import lax
from jax.experimental import pallas as pl
from jax.experimental.pallas import tpu as pltpu
from jax.sharding import PartitionSpec as P

STEPS = 3
EPSILON = 1e-06
F32 = jnp.float32


def column_shift(value, steps):
    points, columns = lax.axis_size("pts"), lax.axis_size("cols")
    pairs = [
        (point * columns + column, (point ^ 1) * columns + (column + steps) % columns)
        for point in range(points)
        for column in range(columns)
    ]
    return lax.ppermute(value, ("pts", "cols"), pairs)


def swapped(value, even_bits, odd_bits):
    count = lax.axis_size("pts")
    pairs = [(source, source ^ (odd_bits if source % 2 else even_bits)) for source in range(count)]
    return lax.ppermute(value, "pts", pairs)


def chip_sum(value, beside):
    count = lax.axis_size("pts")
    bit = 2
    own, known, needed = (value,), (), value
    while bit < count:
        if 2 * bit < count:
            for _ in range(2):
                near = swapped(value, 1, 1)
                far = swapped(value, bit ^ 1, 2 * bit ^ 1)
                own, known, needed = (near, far), (value,), far
                value = far + near
                value, beside = lax.optimization_barrier((value, beside))
        else:
            value = value + swapped(value, bit, bit)
            own, known, needed = (value,), (), value
        bit *= 4
    return own, known, needed, beside


def two_parts(value):
    high = value.astype(jnp.bfloat16)
    return high, (value - high.astype(F32)).astype(jnp.bfloat16)


def first_columns(parts, columns):
    return parts[0][:, :columns], parts[1][:, :columns]


def product(left, right, left_axis=1, right_axis=0):
    return lax.dot_general(
        jnp.concatenate([left[0], left[0], left[1]], axis=left_axis),
        jnp.concatenate([right[0], right[1], right[0]], axis=right_axis),
        (((left_axis,), (right_axis,)), ((), ())),
        preferred_element_type=F32,
    )


def halves_swapped(value):
    half = value.shape[0] // 2
    return jnp.concatenate([value[half:], value[:half]], axis=0)


def times_inverse_root(left, left_parts, square, scale, columns):
    rows = lax.broadcasted_iota(jnp.int32, square.shape, 0)
    identity = jnp.where(rows == lax.broadcasted_iota(jnp.int32, square.shape, 1), 1.0, 0.0)
    square_parts = two_parts(square)
    inverse = 1.0 / scale
    base = (identity + square) * inverse
    second = (identity + 2.0 * square + product(square_parts, square_parts)) * (inverse * inverse)
    left_base = (left + product(left_parts, square_parts)) * inverse
    first_square = two_parts(2.25 * identity - 1.5 * base + 0.25 * second)
    cubic = product(two_parts(1.5 * base - 0.5 * second), first_square)
    both = two_parts(2.25 * identity - 0.75 * base - 0.5 * cubic)
    both_first = first_columns(both, columns)
    both_square = product(both, both_first)
    left_cubic = product(two_parts(left_base), both)
    left_both = product(left_parts, both_first)
    left_last = product(two_parts(left_cubic), two_parts(both_square))
    return (1.5 * left_both - 0.5 * left_last) * lax.rsqrt(scale)


def joined(own, other):
    return jnp.concatenate([own, halves_swapped(other)], axis=1)


def own_half(half):
    own = (lax.axis_index("pts") % 2) * half
    return pl.multiple_of(own, half), pl.multiple_of(half - own, half)


def start_blocks(near, far):
    width = near.shape[1] // 2
    own, other = own_half(width // 2)

    def taken(start):
        piece = (slice(None), pl.ds(start, width // 2))
        return jnp.concatenate([near[piece], far[piece]], axis=0)

    upper = jnp.concatenate([taken(own), taken(other)], axis=1)
    return upper, jnp.concatenate([taken(width + own), taken(width + other)], axis=1)


def later_blocks(upper, own, other):
    return upper[...], jnp.concatenate([halves_swapped(own[...]), other[...]], axis=1)


def stored(ref, value):
    half = ref.shape[1] // 2
    own, other = own_half(half)
    ref[:, pl.ds(own, half)] = value[:, :half]
    ref[:, pl.ds(other, half)] = value[:, half:]


def norm_rows(norm_lower, norm_upper, norm_upper_other):
    rows = lax.broadcasted_iota(jnp.int32, (8, norm_lower.shape[1]), 0)
    uppers = jnp.where(rows == 1, norm_upper, jnp.where(rows == 2, norm_upper_other, 0.0))
    return jnp.where(rows == 0, norm_lower, uppers)


def start_kernel(near_ref, weight_ref, own_part, other_part, near, weight, near_sent, weight_sent):
    copies = [
        pltpu.make_async_copy(near_ref, near, near_sent),
        pltpu.make_async_copy(weight_ref, weight, weight_sent),
    ]
    for copy in copies:
        copy.start()
    for copy in copies:
        copy.wait()
    width = near.shape[1] // 2
    half = width // 2
    own, other = own_half(half)
    point_weight = jnp.broadcast_to(weight[...], (8, weight.shape[1])).T[:, 0:1]
    upper_own, upper_other = near[:, pl.ds(own, half)], near[:, pl.ds(other, half)]
    upper_parts = two_parts(jnp.concatenate([upper_own, upper_other], axis=1))
    orders = ((upper_own, upper_other), (upper_other, upper_own))
    for start, order, out in zip((own, other), orders, (own_part, other_part)):
        lower = near[:, pl.ds(width + start, half)]
        weighted = point_weight * lower
        gram = product(upper_parts, two_parts(weighted), 0, 0)
        out[:width] = gram if out is own_part else halves_swapped(gram)
        norm_lower = jnp.sum(weighted * lower, axis=0, keepdims=True)
        uppers = [jnp.sum(point_weight * value * value, axis=0, keepdims=True) for value in order]
        out[width:] = norm_rows(norm_lower, *uppers)


def taken_rows(last, rows):
    return slice(rows, 2 * rows) if last else slice(0, rows)


def total(refs):
    return sum((ref[...] for ref in refs[1:]), refs[0][...])


def half_kernel(addends, blocks, step, last, damps, *refs):
    *ins, own_coupling, own_high, own_low, upper_high, upper_low, left_scale, square, norm, high, low = refs
    own_sum, block_refs = total(ins[:addends]), ins[addends:]
    width, half = own_coupling.shape
    upper, lower = blocks(*block_refs)
    inverse = lax.rsqrt(own_sum[width:] + EPSILON)
    uppers = jnp.broadcast_to(jnp.concatenate([inverse[1:2], inverse[2:3]], axis=1), (8, width))
    scaled = damps[step : step + 1, 0:1] * uppers.T[:, 0:1]
    left_scale[...] = jnp.broadcast_to(scaled, left_scale.shape)
    coupling = own_sum[:width] * scaled * inverse[0:1]
    own_coupling[...] = coupling
    norm[...] = jnp.sum(coupling * coupling, axis=0, keepdims=True)
    parts = own_high[...], own_low[...] = two_parts(coupling)
    square[...] = product(parts, parts, 0, 0)
    taken = taken_rows(last, high.shape[0])
    upper_parts = upper_high[...], upper_low[...] = two_parts(upper[taken])
    high[...], low[...] = two_parts(lower[taken, :half] + product(upper_parts, parts))


def lower_kernel(
    addends, blocks, last, own_high, own_low, upper_high, upper_low, left_scale, own_square, norm, high, low, *refs
):
    *ins, moved, other_coupling, scale_out = refs
    other_sum, block_refs = total(ins[:addends]), ins[addends:]
    width, half = own_high.shape
    _, lower = blocks(*block_refs)
    inverse = lax.rsqrt(other_sum[width : width + 1] + EPSILON)
    coupling = halves_swapped(other_sum[:width]) * left_scale[...] * inverse
    other_coupling[...] = coupling
    other_parts = two_parts(coupling)
    own_parts = own_high[...], own_low[...]
    parts = [jnp.concatenate(pair, axis=1) for pair in zip(own_parts, other_parts)]
    crossed = product(other_parts, own_parts, 0, 0)
    square = jnp.concatenate(
        [jnp.concatenate([own_square[...], crossed], axis=0), product(parts, other_parts, 0, 0)], axis=1
    )
    norms = norm[...] + jnp.sum(coupling * coupling, axis=0, keepdims=True)
    scale = 1.0 + jnp.sum(norms, keepdims=True)
    scale_out[...] = jnp.broadcast_to(scale, scale_out.shape)
    rows, columns = moved.shape
    taken = taken_rows(last, rows)
    other_mixed = lower[taken, half:] + product((upper_high[...], upper_low[...]), other_parts)
    mixed_parts = [jnp.concatenate(pair, axis=1) for pair in zip((high[...], low[...]), two_parts(other_mixed))]
    mixed = jnp.concatenate([high[...].astype(F32) + low[...].astype(F32), other_mixed], axis=1)
    result = times_inverse_root(mixed, mixed_parts, square, scale, columns)
    if last:
        stored(moved, result)
    else:
        moved[...] = result


def rotated_upper(blocks, rows, own_coupling, other_coupling, scale_ref, *block_refs):
    coupling = jnp.concatenate([own_coupling[...], other_coupling[...]], axis=1)
    upper, lower = blocks(*block_refs)
    parts = two_parts(coupling)
    mixed = upper[:rows] - product(two_parts(lower[:rows]), parts, 1, 1)
    square = product(parts, parts, 1, 1)
    return times_inverse_root(mixed, two_parts(mixed), square, scale_ref[0:1, 0:1], coupling.shape[1])


def upper_kernel(blocks, weight, *refs):
    *ins, gram_left, norm_out, upper_out = refs
    upper = rotated_upper(blocks, upper_out.shape[0], *ins)
    upper_out[...] = upper
    weighted = weight[...] * upper
    norm_out[...] = jnp.sum(weighted * upper, axis=0, keepdims=True)
    high, low = two_parts(weighted.T)
    gram_left[...] = jnp.concatenate([high, high, low], axis=1)


def last_upper_kernel(blocks, *refs):
    *ins, out, held, sent = refs
    stored(held, rotated_upper(blocks, held.shape[0], *ins))
    copy = pltpu.make_async_copy(held, out.at[:, pl.ds(0, held.shape[1])], sent)
    copy.start()
    copy.wait()


def last_lower_kernel(lower, filled, out, sent):
    del filled
    width = lower.shape[1]
    copy = pltpu.make_async_copy(lower, out.at[:, pl.ds(width, width)], sent)
    copy.start()
    copy.wait()


def gram_kernel(gram_left, norm_upper, weight, own_ref, payload):
    width = gram_left.shape[0]
    own = halves_swapped(own_ref[...])
    high, low = two_parts(own)
    right = jnp.concatenate([high, low, high], axis=0)
    payload[:width] = jnp.dot(gram_left[...], right, preferred_element_type=F32)
    norm_lower = jnp.sum(weight[...] * own * own, axis=0, keepdims=True)
    half = own.shape[1]
    payload[width:] = norm_rows(norm_lower, norm_upper[:, :half], norm_upper[:, half:])


ON_CHIP = pl.BlockSpec(memory_space=pltpu.VMEM)
ANYWHERE = pl.BlockSpec(memory_space=pl.ANY)
GRANT = pltpu.CompilerParams(vmem_limit_bytes=24 << 20)


def in_vmem(kernel, outs, *args):
    return pl.pallas_call(
        kernel,
        out_shape=[jax.ShapeDtypeStruct(shape, dtype) for shape, dtype in outs],
        in_specs=[ON_CHIP] * len(args),
        out_specs=[ON_CHIP] * len(outs),
        compiler_params=GRANT,
    )(*args)


def body(snapshot, weights, damping):
    rows, columns = snapshot.shape
    width = columns // 2
    half = width // 2
    whole = (2 * rows, width)
    own_part, other_part, near = pl.pallas_call(
        start_kernel,
        out_shape=[jax.ShapeDtypeStruct((width + 8, half), F32)] * 2 + [jax.ShapeDtypeStruct(snapshot.shape, F32)],
        in_specs=[pl.BlockSpec(memory_space=pltpu.HBM)] * 2,
        out_specs=[ON_CHIP] * 3,
        scratch_shapes=[
            pltpu.VMEM((1, rows), F32),
            pltpu.SemaphoreType.DMA(()),
            pltpu.SemaphoreType.DMA(()),
        ],
        compiler_params=GRANT,
    )(*(pltpu.with_memory_space_constraint(value, pltpu.HBM) for value in (snapshot, weights[None])))
    own_part, other_part, damping = lax.optimization_barrier((own_part, other_part, damping))
    payload = own_part + swapped(other_part, 1, 1)
    weight = jnp.concatenate([weights, swapped(weights, 1, 1)])[:, None]
    blocks, held, arriving = start_blocks, (near,), swapped(near, 1, 1)
    damps = damping[:, 0].astype(F32) / (damping[:, 0] + damping[:, 1]).astype(F32)
    damps = lax.optimization_barrier(jnp.broadcast_to(damps[:, None], (STEPS, 128)))
    for step in range(STEPS):
        last = step + 1 == STEPS
        own, known, needed, arriving = chip_sum(payload, arriving)
        held = held + (arriving,)
        remote = swapped(needed, 1, 1)
        shape = (rows, width) if last else (2 * rows, half)
        pieces = in_vmem(
            functools.partial(half_kernel, len(own), blocks, step, last),
            [((width, half), F32)]
            + [((width, half), jnp.bfloat16)] * 2
            + [((shape[0], width), jnp.bfloat16)] * 2
            + [((width, half), F32), ((half, half), F32), ((1, half), F32)]
            + [((shape[0], half), jnp.bfloat16)] * 2,
            damps,
            *own,
            *held,
        )
        moved, other_coupling, scale = in_vmem(
            functools.partial(lower_kernel, len(known) + 1, blocks, last),
            [(shape, F32), ((width, half), F32), ((8, 128), F32)],
            *pieces[1:],
            *known,
            remote,
            *held,
        )
        coupling = (pieces[0], other_coupling)
        if last:
            break
        moved = column_shift(moved, 1)
        gram_left, norm_upper, upper = in_vmem(
            functools.partial(upper_kernel, blocks),
            [((width, 6 * rows), jnp.bfloat16), ((1, width), F32), (whole, F32)],
            weight,
            *coupling,
            scale,
            *held,
        )
        blocks, held, arriving = later_blocks, (upper, moved), swapped(moved, 1, 1)
        (payload,) = in_vmem(gram_kernel, [((width + 8, half), F32)], gram_left, norm_upper, weight, moved)
    moved = column_shift(moved, 1 - STEPS)
    out_shape = jax.ShapeDtypeStruct((rows, columns), F32)
    rotated = pl.pallas_call(
        functools.partial(last_upper_kernel, blocks),
        out_shape=out_shape,
        in_specs=[ON_CHIP] * (3 + len(held)),
        out_specs=ANYWHERE,
        scratch_shapes=[pltpu.VMEM((rows, width), F32), pltpu.SemaphoreType.DMA(())],
        compiler_params=GRANT,
    )(*coupling, scale, *held)
    return pl.pallas_call(
        last_lower_kernel,
        out_shape=out_shape,
        in_specs=[ON_CHIP, ANYWHERE],
        out_specs=ANYWHERE,
        scratch_shapes=[pltpu.SemaphoreType.DMA(())],
        input_output_aliases={1: 0},
        compiler_params=GRANT,
    )(moved, rotated)


def solution(mesh):
    placed = (P("pts", "cols"), P("pts"), P())
    return jax.shard_map(
        body, mesh=mesh, in_specs=placed, out_specs=P("pts", "cols"), check_vma=False
    )
```

```python
import functools

import jax
import jax.numpy as jnp
from jax import lax
from jax.experimental import pallas as pl
from jax.experimental.pallas import tpu as pltpu
from jax.sharding import PartitionSpec as P

STEPS = 3
EPSILON = 1e-06
F32 = jnp.float32


def column_shift(value, steps):
    points, columns = lax.axis_size("pts"), lax.axis_size("cols")
    pairs = [
        (point * columns + column, (point ^ 1) * columns + (column + steps) % columns)
        for point in range(points)
        for column in range(columns)
    ]
    return lax.ppermute(value, ("pts", "cols"), pairs)


def swapped(value, even_bits, odd_bits):
    count = lax.axis_size("pts")
    pairs = [(source, source ^ (odd_bits if source % 2 else even_bits)) for source in range(count)]
    return lax.ppermute(value, "pts", pairs)


def chip_sum(value, beside):
    count = lax.axis_size("pts")
    bit = 2
    own, known, needed = (value,), (), value
    while bit < count:
        if 2 * bit < count:
            for _ in range(2):
                near = swapped(value, 1, 1)
                far = swapped(value, bit ^ 1, 2 * bit ^ 1)
                own, known, needed = (near, far), (value,), far
                value = far + near
                value, beside = lax.optimization_barrier((value, beside))
        else:
            value = value + swapped(value, bit, bit)
            own, known, needed = (value,), (), value
        bit *= 4
    return own, known, needed, beside


def two_parts(value):
    high = value.astype(jnp.bfloat16)
    return high, (value - high.astype(F32)).astype(jnp.bfloat16)


def first_columns(parts, columns):
    return parts[0][:, :columns], parts[1][:, :columns]


def product(left, right, left_axis=1, right_axis=0):
    return lax.dot_general(
        jnp.concatenate([left[0], left[0], left[1]], axis=left_axis),
        jnp.concatenate([right[0], right[1], right[0]], axis=right_axis),
        (((left_axis,), (right_axis,)), ((), ())),
        preferred_element_type=F32,
    )


def halves_swapped(value):
    half = value.shape[0] // 2
    return jnp.concatenate([value[half:], value[:half]], axis=0)


def times_inverse_root(left_parts, square, scale, columns):
    rows = lax.broadcasted_iota(jnp.int32, square.shape, 0)
    identity = jnp.where(rows == lax.broadcasted_iota(jnp.int32, square.shape, 1), 1.0, 0.0)
    base = (identity + square) * (1.0 / scale)
    base_parts = two_parts(base)
    second = product(base_parts, base_parts)
    left_base = product(left_parts, base_parts)
    first_square = two_parts(2.25 * identity - 1.5 * base + 0.25 * second)
    cubic = product(two_parts(1.5 * base - 0.5 * second), first_square)
    both = two_parts(2.25 * identity - 0.75 * base - 0.5 * cubic)
    both_first = first_columns(both, columns)
    both_square = product(both, both_first)
    left_cubic = product(two_parts(left_base), both)
    left_both = product(left_parts, both_first)
    left_last = product(two_parts(left_cubic), two_parts(both_square))
    return (1.5 * left_both - 0.5 * left_last) * lax.rsqrt(scale)


def joined(own, other):
    return jnp.concatenate([own, halves_swapped(other)], axis=1)


def own_half(half):
    own = (lax.axis_index("pts") % 2) * half
    return pl.multiple_of(own, half), pl.multiple_of(half - own, half)


def start_blocks(near, far):
    width = near.shape[1] // 2
    own, other = own_half(width // 2)

    def taken(start):
        piece = (slice(None), pl.ds(start, width // 2))
        return jnp.concatenate([near[piece], far[piece]], axis=0)

    upper = jnp.concatenate([taken(own), taken(other)], axis=1)
    return upper, jnp.concatenate([taken(width + own), taken(width + other)], axis=1)


def later_blocks(upper, own, other):
    return upper[...], jnp.concatenate([halves_swapped(own[...]), other[...]], axis=1)


def stored(ref, value):
    half = ref.shape[1] // 2
    own, other = own_half(half)
    ref[:, pl.ds(own, half)] = value[:, :half]
    ref[:, pl.ds(other, half)] = value[:, half:]


def norm_rows(norm_lower, norm_upper, norm_upper_other):
    rows = lax.broadcasted_iota(jnp.int32, (8, norm_lower.shape[1]), 0)
    uppers = jnp.where(rows == 1, norm_upper, jnp.where(rows == 2, norm_upper_other, 0.0))
    return jnp.where(rows == 0, norm_lower, uppers)


def start_kernel(near_ref, weight_ref, own_part, other_part, near, weight, near_sent, weight_sent):
    copies = [
        pltpu.make_async_copy(near_ref, near, near_sent),
        pltpu.make_async_copy(weight_ref, weight, weight_sent),
    ]
    for copy in copies:
        copy.start()
    for copy in copies:
        copy.wait()
    width = near.shape[1] // 2
    half = width // 2
    own, other = own_half(half)
    point_weight = jnp.broadcast_to(weight[...], (8, weight.shape[1])).T[:, 0:1]
    upper_own, upper_other = near[:, pl.ds(own, half)], near[:, pl.ds(other, half)]
    upper_parts = two_parts(jnp.concatenate([upper_own, upper_other], axis=1))
    orders = ((upper_own, upper_other), (upper_other, upper_own))
    for start, order, out in zip((own, other), orders, (own_part, other_part)):
        lower = near[:, pl.ds(width + start, half)]
        weighted = point_weight * lower
        gram = product(upper_parts, two_parts(weighted), 0, 0)
        out[:width] = gram if out is own_part else halves_swapped(gram)
        norm_lower = jnp.sum(weighted * lower, axis=0, keepdims=True)
        uppers = [jnp.sum(point_weight * value * value, axis=0, keepdims=True) for value in order]
        out[width:] = norm_rows(norm_lower, *uppers)


def taken_rows(last, rows):
    return slice(rows, 2 * rows) if last else slice(0, rows)


def total(refs):
    return sum((ref[...] for ref in refs[1:]), refs[0][...])


def half_kernel(addends, blocks, step, last, damps, *refs):
    *ins, own_coupling, own_high, own_low, upper_high, upper_low, left_scale, square, norm, high, low = refs
    own_sum, block_refs = total(ins[:addends]), ins[addends:]
    width, half = own_coupling.shape
    upper, lower = blocks(*block_refs)
    inverse = lax.rsqrt(own_sum[width:] + EPSILON)
    uppers = jnp.broadcast_to(jnp.concatenate([inverse[1:2], inverse[2:3]], axis=1), (8, width))
    scaled = damps[step : step + 1, 0:1] * uppers.T[:, 0:1]
    left_scale[...] = jnp.broadcast_to(scaled, left_scale.shape)
    coupling = own_sum[:width] * scaled * inverse[0:1]
    own_coupling[...] = coupling
    norm[...] = jnp.sum(coupling * coupling, axis=0, keepdims=True)
    parts = own_high[...], own_low[...] = two_parts(coupling)
    square[...] = product(parts, parts, 0, 0)
    taken = taken_rows(last, high.shape[0])
    upper_parts = upper_high[...], upper_low[...] = two_parts(upper[taken])
    high[...], low[...] = two_parts(lower[taken, :half] + product(upper_parts, parts))


def lower_kernel(
    addends, blocks, last, own_high, own_low, upper_high, upper_low, left_scale, own_square, norm, high, low, *refs
):
    *ins, moved, other_coupling, scale_out = refs
    other_sum, block_refs = total(ins[:addends]), ins[addends:]
    width, half = own_high.shape
    _, lower = blocks(*block_refs)
    inverse = lax.rsqrt(other_sum[width : width + 1] + EPSILON)
    coupling = halves_swapped(other_sum[:width]) * left_scale[...] * inverse
    other_coupling[...] = coupling
    other_parts = two_parts(coupling)
    own_parts = own_high[...], own_low[...]
    parts = [jnp.concatenate(pair, axis=1) for pair in zip(own_parts, other_parts)]
    crossed = product(other_parts, own_parts, 0, 0)
    square = jnp.concatenate(
        [jnp.concatenate([own_square[...], crossed], axis=0), product(parts, other_parts, 0, 0)], axis=1
    )
    norms = norm[...] + jnp.sum(coupling * coupling, axis=0, keepdims=True)
    scale = 1.0 + jnp.sum(norms, keepdims=True)
    scale_out[...] = jnp.broadcast_to(scale, scale_out.shape)
    rows, columns = moved.shape
    taken = taken_rows(last, rows)
    other_mixed = lower[taken, half:] + product((upper_high[...], upper_low[...]), other_parts)
    mixed = [jnp.concatenate(pair, axis=1) for pair in zip((high[...], low[...]), two_parts(other_mixed))]
    result = times_inverse_root(mixed, square, scale, columns)
    if last:
        stored(moved, result)
    else:
        moved[...] = result


def rotated_upper(blocks, rows, own_coupling, other_coupling, scale_ref, *block_refs):
    coupling = jnp.concatenate([own_coupling[...], other_coupling[...]], axis=1)
    upper, lower = blocks(*block_refs)
    parts = two_parts(coupling)
    mixed = upper[:rows] - product(two_parts(lower[:rows]), parts, 1, 1)
    square = product(parts, parts, 1, 1)
    return times_inverse_root(two_parts(mixed), square, scale_ref[0:1, 0:1], coupling.shape[1])


def upper_kernel(blocks, weight, *refs):
    *ins, gram_left, norm_out, upper_out = refs
    upper = rotated_upper(blocks, upper_out.shape[0], *ins)
    upper_out[...] = upper
    weighted = weight[...] * upper
    norm_out[...] = jnp.sum(weighted * upper, axis=0, keepdims=True)
    high, low = two_parts(weighted.T)
    gram_left[...] = jnp.concatenate([high, high, low], axis=1)


def last_upper_kernel(blocks, *refs):
    *ins, out, held, sent = refs
    stored(held, rotated_upper(blocks, held.shape[0], *ins))
    copy = pltpu.make_async_copy(held, out.at[:, pl.ds(0, held.shape[1])], sent)
    copy.start()
    copy.wait()


def last_lower_kernel(lower, filled, out, sent):
    del filled
    width = lower.shape[1]
    copy = pltpu.make_async_copy(lower, out.at[:, pl.ds(width, width)], sent)
    copy.start()
    copy.wait()


def gram_kernel(gram_left, norm_upper, weight, own_ref, payload):
    width = gram_left.shape[0]
    own = halves_swapped(own_ref[...])
    high, low = two_parts(own)
    right = jnp.concatenate([high, low, high], axis=0)
    payload[:width] = jnp.dot(gram_left[...], right, preferred_element_type=F32)
    norm_lower = jnp.sum(weight[...] * own * own, axis=0, keepdims=True)
    half = own.shape[1]
    payload[width:] = norm_rows(norm_lower, norm_upper[:, :half], norm_upper[:, half:])


ON_CHIP = pl.BlockSpec(memory_space=pltpu.VMEM)
ANYWHERE = pl.BlockSpec(memory_space=pl.ANY)
GRANT = pltpu.CompilerParams(vmem_limit_bytes=24 << 20)


def in_vmem(kernel, outs, *args):
    return pl.pallas_call(
        kernel,
        out_shape=[jax.ShapeDtypeStruct(shape, dtype) for shape, dtype in outs],
        in_specs=[ON_CHIP] * len(args),
        out_specs=[ON_CHIP] * len(outs),
        compiler_params=GRANT,
    )(*args)


def body(snapshot, weights, damping):
    rows, columns = snapshot.shape
    width = columns // 2
    half = width // 2
    whole = (2 * rows, width)
    own_part, other_part, near = pl.pallas_call(
        start_kernel,
        out_shape=[jax.ShapeDtypeStruct((width + 8, half), F32)] * 2 + [jax.ShapeDtypeStruct(snapshot.shape, F32)],
        in_specs=[pl.BlockSpec(memory_space=pltpu.HBM)] * 2,
        out_specs=[ON_CHIP] * 3,
        scratch_shapes=[
            pltpu.VMEM((1, rows), F32),
            pltpu.SemaphoreType.DMA(()),
            pltpu.SemaphoreType.DMA(()),
        ],
        compiler_params=GRANT,
    )(*(pltpu.with_memory_space_constraint(value, pltpu.HBM) for value in (snapshot, weights[None])))
    own_part, other_part, damping = lax.optimization_barrier((own_part, other_part, damping))
    payload = own_part + swapped(other_part, 1, 1)
    weight = jnp.concatenate([weights, swapped(weights, 1, 1)])[:, None]
    blocks, held, arriving = start_blocks, (near,), swapped(near, 1, 1)
    damps = damping[:, 0].astype(F32) / (damping[:, 0] + damping[:, 1]).astype(F32)
    damps = lax.optimization_barrier(jnp.broadcast_to(damps[:, None], (STEPS, 128)))
    for step in range(STEPS):
        last = step + 1 == STEPS
        own, known, needed, arriving = chip_sum(payload, arriving)
        held = held + (arriving,)
        remote = swapped(needed, 1, 1)
        shape = (rows, width) if last else (2 * rows, half)
        pieces = in_vmem(
            functools.partial(half_kernel, len(own), blocks, step, last),
            [((width, half), F32)]
            + [((width, half), jnp.bfloat16)] * 2
            + [((shape[0], width), jnp.bfloat16)] * 2
            + [((width, half), F32), ((half, half), F32), ((1, half), F32)]
            + [((shape[0], half), jnp.bfloat16)] * 2,
            damps,
            *own,
            *held,
        )
        moved, other_coupling, scale = in_vmem(
            functools.partial(lower_kernel, len(known) + 1, blocks, last),
            [(shape, F32), ((width, half), F32), ((8, 128), F32)],
            *pieces[1:],
            *known,
            remote,
            *held,
        )
        coupling = (pieces[0], other_coupling)
        if last:
            break
        moved = column_shift(moved, 1)
        gram_left, norm_upper, upper = in_vmem(
            functools.partial(upper_kernel, blocks),
            [((width, 6 * rows), jnp.bfloat16), ((1, width), F32), (whole, F32)],
            weight,
            *coupling,
            scale,
            *held,
        )
        blocks, held, arriving = later_blocks, (upper, moved), swapped(moved, 1, 1)
        (payload,) = in_vmem(gram_kernel, [((width + 8, half), F32)], gram_left, norm_upper, weight, moved)
    moved = column_shift(moved, 1 - STEPS)
    out_shape = jax.ShapeDtypeStruct((rows, columns), F32)
    rotated = pl.pallas_call(
        functools.partial(last_upper_kernel, blocks),
        out_shape=out_shape,
        in_specs=[ON_CHIP] * (3 + len(held)),
        out_specs=ANYWHERE,
        scratch_shapes=[pltpu.VMEM((rows, width), F32), pltpu.SemaphoreType.DMA(())],
        compiler_params=GRANT,
    )(*coupling, scale, *held)
    return pl.pallas_call(
        last_lower_kernel,
        out_shape=out_shape,
        in_specs=[ON_CHIP, ANYWHERE],
        out_specs=ANYWHERE,
        scratch_shapes=[pltpu.SemaphoreType.DMA(())],
        input_output_aliases={1: 0},
        compiler_params=GRANT,
    )(moved, rotated)


def solution(mesh):
    placed = (P("pts", "cols"), P("pts"), P())
    return jax.shard_map(
        body, mesh=mesh, in_specs=placed, out_specs=P("pts", "cols"), check_vma=False
    )
```

```python
import functools

import jax
import jax.numpy as jnp
from jax import lax
from jax.experimental import pallas as pl
from jax.experimental.pallas import tpu as pltpu
from jax.sharding import PartitionSpec as P

STEPS = 3
EPSILON = 1e-06
F32 = jnp.float32


def column_shift(value, steps):
    points, columns = lax.axis_size("pts"), lax.axis_size("cols")
    pairs = [
        (point * columns + column, (point ^ 1) * columns + (column + steps) % columns)
        for point in range(points)
        for column in range(columns)
    ]
    return lax.ppermute(value, ("pts", "cols"), pairs)


def swapped(value, even_bits, odd_bits):
    count = lax.axis_size("pts")
    pairs = [(source, source ^ (odd_bits if source % 2 else even_bits)) for source in range(count)]
    return lax.ppermute(value, "pts", pairs)


def chip_sum(value, beside):
    count = lax.axis_size("pts")
    bit = 2
    own, known, needed = (value,), (), value
    while bit < count:
        if 2 * bit < count:
            for _ in range(2):
                near = swapped(value, 1, 1)
                far = swapped(value, bit ^ 1, 2 * bit ^ 1)
                own, known, needed = (near, far), (value,), far
                value = far + near
                value, beside = lax.optimization_barrier((value, beside))
        else:
            value = value + swapped(value, bit, bit)
            own, known, needed = (value,), (), value
        bit *= 4
    return own, known, needed, beside


def two_parts(value):
    high = value.astype(jnp.bfloat16)
    return high, (value - high.astype(F32)).astype(jnp.bfloat16)


def first_columns(parts, columns):
    return parts[0][:, :columns], parts[1][:, :columns]


def product(left, right, left_axis=1, right_axis=0):
    return lax.dot_general(
        jnp.concatenate([left[0], left[0], left[1]], axis=left_axis),
        jnp.concatenate([right[0], right[1], right[0]], axis=right_axis),
        (((left_axis,), (right_axis,)), ((), ())),
        preferred_element_type=F32,
    )


def halves_swapped(value):
    half = value.shape[0] // 2
    return jnp.concatenate([value[half:], value[:half]], axis=0)


def times_inverse_root(left_parts, square, scale, columns):
    rows = lax.broadcasted_iota(jnp.int32, square.shape, 0)
    identity = jnp.where(rows == lax.broadcasted_iota(jnp.int32, square.shape, 1), 1.0, 0.0)
    base = (identity + square) * (1.0 / scale)
    base_parts = two_parts(base)
    second = product(base_parts, base_parts)
    left_base = product(left_parts, base_parts)
    first_square = two_parts(2.25 * identity - 1.5 * base + 0.25 * second)
    cubic = product(two_parts(1.5 * base - 0.5 * second), first_square)
    both = two_parts(2.25 * identity - 0.75 * base - 0.5 * cubic)
    both_first = first_columns(both, columns)
    both_square = product(both, both_first)
    left_cubic = product(two_parts(left_base), both)
    left_both = product(left_parts, both_first)
    left_last = product(two_parts(left_cubic), two_parts(both_square))
    return (1.5 * left_both - 0.5 * left_last) * lax.rsqrt(scale)


def joined(own, other):
    return jnp.concatenate([own, halves_swapped(other)], axis=1)


def own_half(half):
    own = (lax.axis_index("pts") % 2) * half
    return pl.multiple_of(own, half), pl.multiple_of(half - own, half)


def start_blocks(near, far):
    width = near.shape[1] // 2
    own, other = own_half(width // 2)

    def taken(start):
        piece = (slice(None), pl.ds(start, width // 2))
        return jnp.concatenate([near[piece], far[piece]], axis=0)

    upper = jnp.concatenate([taken(own), taken(other)], axis=1)
    return upper, jnp.concatenate([taken(width + own), taken(width + other)], axis=1)


def later_blocks(upper, own, other):
    return upper[...], jnp.concatenate([halves_swapped(own[...]), other[...]], axis=1)


def stored(ref, value):
    half = ref.shape[1] // 2
    own, other = own_half(half)
    ref[:, pl.ds(own, half)] = value[:, :half]
    ref[:, pl.ds(other, half)] = value[:, half:]


def norm_rows(norm_lower, norm_upper, norm_upper_other):
    rows = lax.broadcasted_iota(jnp.int32, (8, norm_lower.shape[1]), 0)
    uppers = jnp.where(rows == 1, norm_upper, jnp.where(rows == 2, norm_upper_other, 0.0))
    return jnp.where(rows == 0, norm_lower, uppers)


def start_kernel(near_ref, weight_ref, own_part, other_part, near, weight, weight_sent, *near_sent):
    rows = near.shape[0] // len(near_sent)
    pieces = [pl.ds(index * rows, rows) for index in range(len(near_sent))]
    weight_copy = pltpu.make_async_copy(weight_ref, weight, weight_sent)
    weight_copy.start()
    copies = [
        pltpu.make_async_copy(near_ref.at[piece], near.at[piece], sent) for piece, sent in zip(pieces, near_sent)
    ]
    for copy in copies:
        copy.start()
    weight_copy.wait()
    width = near.shape[1] // 2
    half = width // 2
    own, other = own_half(half)
    point_weights = jnp.broadcast_to(weight[...], (8, weight.shape[1])).T[:, 0:1]
    grams, norms = [0.0, 0.0], [0.0, 0.0, 0.0, 0.0]
    for index, (piece, copy) in enumerate(zip(pieces, copies)):
        copy.wait()
        point_weight = point_weights[index * rows : (index + 1) * rows]
        uppers = near[piece, pl.ds(own, half)], near[piece, pl.ds(other, half)]
        upper_parts = two_parts(jnp.concatenate(uppers, axis=1))
        for place, start in enumerate((own, other)):
            lower = near[piece, pl.ds(width + start, half)]
            weighted = point_weight * lower
            grams[place] += product(upper_parts, two_parts(weighted), 0, 0)
            norms[place] += jnp.sum(weighted * lower, axis=0, keepdims=True)
            norms[2 + place] += jnp.sum(point_weight * uppers[place] * uppers[place], axis=0, keepdims=True)
    own_part[:width] = grams[0]
    own_part[width:] = norm_rows(norms[0], norms[2], norms[3])
    other_part[:width] = halves_swapped(grams[1])
    other_part[width:] = norm_rows(norms[1], norms[3], norms[2])


def taken_rows(last, rows):
    return slice(rows, 2 * rows) if last else slice(0, rows)


def total(refs):
    return sum((ref[...] for ref in refs[1:]), refs[0][...])


def half_kernel(addends, blocks, step, last, damps, *refs):
    *ins, own_coupling, own_high, own_low, upper_high, upper_low, left_scale, square, norm, high, low = refs
    own_sum, block_refs = total(ins[:addends]), ins[addends:]
    width, half = own_coupling.shape
    upper, lower = blocks(*block_refs)
    inverse = lax.rsqrt(own_sum[width:] + EPSILON)
    uppers = jnp.broadcast_to(jnp.concatenate([inverse[1:2], inverse[2:3]], axis=1), (8, width))
    scaled = damps[step : step + 1, 0:1] * uppers.T[:, 0:1]
    left_scale[...] = jnp.broadcast_to(scaled, left_scale.shape)
    coupling = own_sum[:width] * scaled * inverse[0:1]
    own_coupling[...] = coupling
    norm[...] = jnp.sum(coupling * coupling, axis=0, keepdims=True)
    parts = own_high[...], own_low[...] = two_parts(coupling)
    square[...] = product(parts, parts, 0, 0)
    taken = taken_rows(last, high.shape[0])
    upper_parts = upper_high[...], upper_low[...] = two_parts(upper[taken])
    high[...], low[...] = two_parts(lower[taken, :half] + product(upper_parts, parts))


def lower_kernel(
    addends, blocks, last, own_high, own_low, upper_high, upper_low, left_scale, own_square, norm, high, low, *refs
):
    *ins, moved, other_coupling, scale_out = refs
    other_sum, block_refs = total(ins[:addends]), ins[addends:]
    width, half = own_high.shape
    _, lower = blocks(*block_refs)
    inverse = lax.rsqrt(other_sum[width : width + 1] + EPSILON)
    coupling = halves_swapped(other_sum[:width]) * left_scale[...] * inverse
    other_coupling[...] = coupling
    other_parts = two_parts(coupling)
    own_parts = own_high[...], own_low[...]
    parts = [jnp.concatenate(pair, axis=1) for pair in zip(own_parts, other_parts)]
    crossed = product(other_parts, own_parts, 0, 0)
    square = jnp.concatenate(
        [jnp.concatenate([own_square[...], crossed], axis=0), product(parts, other_parts, 0, 0)], axis=1
    )
    norms = norm[...] + jnp.sum(coupling * coupling, axis=0, keepdims=True)
    scale = 1.0 + jnp.sum(norms, keepdims=True)
    scale_out[...] = jnp.broadcast_to(scale, scale_out.shape)
    rows, columns = moved.shape
    taken = taken_rows(last, rows)
    other_mixed = lower[taken, half:] + product((upper_high[...], upper_low[...]), other_parts)
    mixed = [jnp.concatenate(pair, axis=1) for pair in zip((high[...], low[...]), two_parts(other_mixed))]
    result = times_inverse_root(mixed, square, scale, columns)
    if last:
        stored(moved, result)
    else:
        moved[...] = result


def rotated_upper(blocks, rows, own_coupling, other_coupling, scale_ref, *block_refs):
    coupling = jnp.concatenate([own_coupling[...], other_coupling[...]], axis=1)
    upper, lower = blocks(*block_refs)
    parts = two_parts(coupling)
    mixed = upper[:rows] - product(two_parts(lower[:rows]), parts, 1, 1)
    square = product(parts, parts, 1, 1)
    return times_inverse_root(two_parts(mixed), square, scale_ref[0:1, 0:1], coupling.shape[1])


def upper_kernel(blocks, weight, *refs):
    *ins, gram_left, norm_out, upper_out = refs
    upper = rotated_upper(blocks, upper_out.shape[0], *ins)
    upper_out[...] = upper
    weighted = weight[...] * upper
    norm_out[...] = jnp.sum(weighted * upper, axis=0, keepdims=True)
    high, low = two_parts(weighted.T)
    gram_left[...] = jnp.concatenate([high, high, low], axis=1)


def last_upper_kernel(blocks, *refs):
    *ins, out, held, sent = refs
    stored(held, rotated_upper(blocks, held.shape[0], *ins))
    copy = pltpu.make_async_copy(held, out.at[:, pl.ds(0, held.shape[1])], sent)
    copy.start()
    copy.wait()


def last_lower_kernel(lower, filled, out, sent):
    del filled
    width = lower.shape[1]
    copy = pltpu.make_async_copy(lower, out.at[:, pl.ds(width, width)], sent)
    copy.start()
    copy.wait()


def gram_kernel(gram_left, norm_upper, weight, own_ref, payload):
    width = gram_left.shape[0]
    own = halves_swapped(own_ref[...])
    high, low = two_parts(own)
    right = jnp.concatenate([high, low, high], axis=0)
    payload[:width] = jnp.dot(gram_left[...], right, preferred_element_type=F32)
    norm_lower = jnp.sum(weight[...] * own * own, axis=0, keepdims=True)
    half = own.shape[1]
    payload[width:] = norm_rows(norm_lower, norm_upper[:, :half], norm_upper[:, half:])


ON_CHIP = pl.BlockSpec(memory_space=pltpu.VMEM)
ANYWHERE = pl.BlockSpec(memory_space=pl.ANY)
GRANT = pltpu.CompilerParams(vmem_limit_bytes=24 << 20)


def in_vmem(kernel, outs, *args):
    return pl.pallas_call(
        kernel,
        out_shape=[jax.ShapeDtypeStruct(shape, dtype) for shape, dtype in outs],
        in_specs=[ON_CHIP] * len(args),
        out_specs=[ON_CHIP] * len(outs),
        compiler_params=GRANT,
    )(*args)


def body(snapshot, weights, damping):
    rows, columns = snapshot.shape
    width = columns // 2
    half = width // 2
    whole = (2 * rows, width)
    own_part, other_part, near = pl.pallas_call(
        start_kernel,
        out_shape=[jax.ShapeDtypeStruct((width + 8, half), F32)] * 2 + [jax.ShapeDtypeStruct(snapshot.shape, F32)],
        in_specs=[pl.BlockSpec(memory_space=pltpu.HBM)] * 2,
        out_specs=[ON_CHIP] * 3,
        scratch_shapes=[
            pltpu.VMEM((1, rows), F32),
            pltpu.SemaphoreType.DMA(()),
            pltpu.SemaphoreType.DMA(()),
            pltpu.SemaphoreType.DMA(()),
        ],
        compiler_params=GRANT,
    )(*(pltpu.with_memory_space_constraint(value, pltpu.HBM) for value in (snapshot, weights[None])))
    own_part, other_part, damping = lax.optimization_barrier((own_part, other_part, damping))
    payload = own_part + swapped(other_part, 1, 1)
    weight = jnp.concatenate([weights, swapped(weights, 1, 1)])[:, None]
    blocks, held, arriving = start_blocks, (near,), swapped(near, 1, 1)
    damps = damping[:, 0].astype(F32) / (damping[:, 0] + damping[:, 1]).astype(F32)
    damps = lax.optimization_barrier(jnp.broadcast_to(damps[:, None], (STEPS, 128)))
    for step in range(STEPS):
        last = step + 1 == STEPS
        own, known, needed, arriving = chip_sum(payload, arriving)
        held = held + (arriving,)
        remote = swapped(needed, 1, 1)
        shape = (rows, width) if last else (2 * rows, half)
        pieces = in_vmem(
            functools.partial(half_kernel, len(own), blocks, step, last),
            [((width, half), F32)]
            + [((width, half), jnp.bfloat16)] * 2
            + [((shape[0], width), jnp.bfloat16)] * 2
            + [((width, half), F32), ((half, half), F32), ((1, half), F32)]
            + [((shape[0], half), jnp.bfloat16)] * 2,
            damps,
            *own,
            *held,
        )
        moved, other_coupling, scale = in_vmem(
            functools.partial(lower_kernel, len(known) + 1, blocks, last),
            [(shape, F32), ((width, half), F32), ((8, 128), F32)],
            *pieces[1:],
            *known,
            remote,
            *held,
        )
        coupling = (pieces[0], other_coupling)
        if last:
            break
        moved = column_shift(moved, 1)
        gram_left, norm_upper, upper = in_vmem(
            functools.partial(upper_kernel, blocks),
            [((width, 6 * rows), jnp.bfloat16), ((1, width), F32), (whole, F32)],
            weight,
            *coupling,
            scale,
            *held,
        )
        blocks, held, arriving = later_blocks, (upper, moved), swapped(moved, 1, 1)
        (payload,) = in_vmem(gram_kernel, [((width + 8, half), F32)], gram_left, norm_upper, weight, moved)
    moved = column_shift(moved, 1 - STEPS)
    out_shape = jax.ShapeDtypeStruct((rows, columns), F32)
    rotated = pl.pallas_call(
        functools.partial(last_upper_kernel, blocks),
        out_shape=out_shape,
        in_specs=[ON_CHIP] * (3 + len(held)),
        out_specs=ANYWHERE,
        scratch_shapes=[pltpu.VMEM((rows, width), F32), pltpu.SemaphoreType.DMA(())],
        compiler_params=GRANT,
    )(*coupling, scale, *held)
    return pl.pallas_call(
        last_lower_kernel,
        out_shape=out_shape,
        in_specs=[ON_CHIP, ANYWHERE],
        out_specs=ANYWHERE,
        scratch_shapes=[pltpu.SemaphoreType.DMA(())],
        input_output_aliases={1: 0},
        compiler_params=GRANT,
    )(moved, rotated)


def solution(mesh):
    placed = (P("pts", "cols"), P("pts"), P())
    return jax.shard_map(
        body, mesh=mesh, in_specs=placed, out_specs=P("pts", "cols"), check_vma=False
    )
```

```python
import functools

import jax
import jax.numpy as jnp
from jax import lax
from jax.experimental import pallas as pl
from jax.experimental.pallas import tpu as pltpu
from jax.sharding import PartitionSpec as P

STEPS = 3
EPSILON = 1e-06
F32 = jnp.float32


def column_shift(value, steps):
    points, columns = lax.axis_size("pts"), lax.axis_size("cols")
    pairs = [
        (point * columns + column, (point ^ 1) * columns + (column + steps) % columns)
        for point in range(points)
        for column in range(columns)
    ]
    return lax.ppermute(value, ("pts", "cols"), pairs)


def swapped(value, even_bits, odd_bits):
    count = lax.axis_size("pts")
    pairs = [(source, source ^ (odd_bits if source % 2 else even_bits)) for source in range(count)]
    return lax.ppermute(value, "pts", pairs)


def chip_sum(value, beside):
    count = lax.axis_size("pts")
    bit = 2
    own, known, needed = (value,), (), value
    while bit < count:
        if 2 * bit < count:
            for _ in range(2):
                near = swapped(value, 1, 1)
                far = swapped(value, 2 * bit ^ 1, bit ^ 1)
                own, known, needed = (near, far), (value,), far
                value = far + near
                value, beside = lax.optimization_barrier((value, beside))
        else:
            value = value + swapped(value, bit, bit)
            own, known, needed = (value,), (), value
        bit *= 4
    return own, known, needed, beside


def two_parts(value):
    high = value.astype(jnp.bfloat16)
    return high, (value - high.astype(F32)).astype(jnp.bfloat16)


def first_columns(parts, columns):
    return parts[0][:, :columns], parts[1][:, :columns]


def product(left, right, left_axis=1, right_axis=0):
    return lax.dot_general(
        jnp.concatenate([left[0], left[0], left[1]], axis=left_axis),
        jnp.concatenate([right[0], right[1], right[0]], axis=right_axis),
        (((left_axis,), (right_axis,)), ((), ())),
        preferred_element_type=F32,
    )


def halves_swapped(value):
    half = value.shape[0] // 2
    return jnp.concatenate([value[half:], value[:half]], axis=0)


def times_inverse_root(left_parts, square, scale, columns):
    rows = lax.broadcasted_iota(jnp.int32, square.shape, 0)
    identity = jnp.where(rows == lax.broadcasted_iota(jnp.int32, square.shape, 1), 1.0, 0.0)
    base = (identity + square) * (1.0 / scale)
    base_parts = two_parts(base)
    second = product(base_parts, base_parts)
    left_base = product(left_parts, base_parts)
    first_square = two_parts(2.25 * identity - 1.5 * base + 0.25 * second)
    cubic = product(two_parts(1.5 * base - 0.5 * second), first_square)
    both = two_parts(2.25 * identity - 0.75 * base - 0.5 * cubic)
    both_first = first_columns(both, columns)
    both_square = product(both, both_first)
    left_cubic = product(two_parts(left_base), both)
    left_both = product(left_parts, both_first)
    left_last = product(two_parts(left_cubic), two_parts(both_square))
    return (1.5 * left_both - 0.5 * left_last) * lax.rsqrt(scale)


def joined(own, other):
    return jnp.concatenate([own, halves_swapped(other)], axis=1)


def own_half(half):
    own = (lax.axis_index("pts") % 2) * half
    return pl.multiple_of(own, half), pl.multiple_of(half - own, half)


def start_blocks(near, far):
    width = near.shape[1] // 2
    own, other = own_half(width // 2)

    def taken(start):
        piece = (slice(None), pl.ds(start, width // 2))
        return jnp.concatenate([near[piece], far[piece]], axis=0)

    upper = jnp.concatenate([taken(own), taken(other)], axis=1)
    return upper, jnp.concatenate([taken(width + own), taken(width + other)], axis=1)


def later_blocks(upper, own, other):
    return upper[...], jnp.concatenate([halves_swapped(own[...]), other[...]], axis=1)


def stored(ref, value):
    half = ref.shape[1] // 2
    own, other = own_half(half)
    ref[:, pl.ds(own, half)] = value[:, :half]
    ref[:, pl.ds(other, half)] = value[:, half:]


def norm_rows(norm_lower, norm_upper, norm_upper_other):
    rows = lax.broadcasted_iota(jnp.int32, (8, norm_lower.shape[1]), 0)
    uppers = jnp.where(rows == 1, norm_upper, jnp.where(rows == 2, norm_upper_other, 0.0))
    return jnp.where(rows == 0, norm_lower, uppers)


def start_kernel(near_ref, weight_ref, own_part, other_part, near, weight, near_sent, weight_sent):
    copies = [
        pltpu.make_async_copy(near_ref, near, near_sent),
        pltpu.make_async_copy(weight_ref, weight, weight_sent),
    ]
    for copy in copies:
        copy.start()
    for copy in copies:
        copy.wait()
    width = near.shape[1] // 2
    half = width // 2
    own, other = own_half(half)
    point_weight = jnp.broadcast_to(weight[...], (8, weight.shape[1])).T[:, 0:1]
    upper_own, upper_other = near[:, pl.ds(own, half)], near[:, pl.ds(other, half)]
    upper_parts = two_parts(jnp.concatenate([upper_own, upper_other], axis=1))
    orders = ((upper_own, upper_other), (upper_other, upper_own))
    for start, order, out in zip((own, other), orders, (own_part, other_part)):
        lower = near[:, pl.ds(width + start, half)]
        weighted = point_weight * lower
        gram = product(upper_parts, two_parts(weighted), 0, 0)
        out[:width] = gram if out is own_part else halves_swapped(gram)
        norm_lower = jnp.sum(weighted * lower, axis=0, keepdims=True)
        uppers = [jnp.sum(point_weight * value * value, axis=0, keepdims=True) for value in order]
        out[width:] = norm_rows(norm_lower, *uppers)


def taken_rows(last, rows):
    return slice(rows, 2 * rows) if last else slice(0, rows)


def total(refs):
    return sum((ref[...] for ref in refs[1:]), refs[0][...])


def half_kernel(addends, blocks, step, last, damps, *refs):
    *ins, own_coupling, own_high, own_low, upper_high, upper_low, left_scale, square, norm, high, low = refs
    own_sum, block_refs = total(ins[:addends]), ins[addends:]
    width, half = own_coupling.shape
    upper, lower = blocks(*block_refs)
    inverse = lax.rsqrt(own_sum[width:] + EPSILON)
    uppers = jnp.broadcast_to(jnp.concatenate([inverse[1:2], inverse[2:3]], axis=1), (8, width))
    scaled = damps[step : step + 1, 0:1] * uppers.T[:, 0:1]
    left_scale[...] = jnp.broadcast_to(scaled, left_scale.shape)
    coupling = own_sum[:width] * scaled * inverse[0:1]
    own_coupling[...] = coupling
    norm[...] = jnp.sum(coupling * coupling, axis=0, keepdims=True)
    parts = own_high[...], own_low[...] = two_parts(coupling)
    square[...] = product(parts, parts, 0, 0)
    taken = taken_rows(last, high.shape[0])
    upper_parts = upper_high[...], upper_low[...] = two_parts(upper[taken])
    high[...], low[...] = two_parts(lower[taken, :half] + product(upper_parts, parts))


def lower_kernel(
    addends, blocks, last, own_high, own_low, upper_high, upper_low, left_scale, own_square, norm, high, low, *refs
):
    *ins, moved, other_coupling, scale_out = refs
    other_sum, block_refs = total(ins[:addends]), ins[addends:]
    width, half = own_high.shape
    _, lower = blocks(*block_refs)
    inverse = lax.rsqrt(other_sum[width : width + 1] + EPSILON)
    coupling = halves_swapped(other_sum[:width]) * left_scale[...] * inverse
    other_coupling[...] = coupling
    other_parts = two_parts(coupling)
    own_parts = own_high[...], own_low[...]
    parts = [jnp.concatenate(pair, axis=1) for pair in zip(own_parts, other_parts)]
    crossed = product(other_parts, own_parts, 0, 0)
    square = jnp.concatenate(
        [jnp.concatenate([own_square[...], crossed], axis=0), product(parts, other_parts, 0, 0)], axis=1
    )
    norms = norm[...] + jnp.sum(coupling * coupling, axis=0, keepdims=True)
    scale = 1.0 + jnp.sum(norms, keepdims=True)
    scale_out[...] = jnp.broadcast_to(scale, scale_out.shape)
    rows, columns = moved.shape
    taken = taken_rows(last, rows)
    other_mixed = lower[taken, half:] + product((upper_high[...], upper_low[...]), other_parts)
    mixed = [jnp.concatenate(pair, axis=1) for pair in zip((high[...], low[...]), two_parts(other_mixed))]
    result = times_inverse_root(mixed, square, scale, columns)
    if last:
        stored(moved, result)
    else:
        moved[...] = result


def rotated_upper(blocks, rows, own_coupling, other_coupling, scale_ref, *block_refs):
    coupling = jnp.concatenate([own_coupling[...], other_coupling[...]], axis=1)
    upper, lower = blocks(*block_refs)
    parts = two_parts(coupling)
    mixed = upper[:rows] - product(two_parts(lower[:rows]), parts, 1, 1)
    square = product(parts, parts, 1, 1)
    return times_inverse_root(two_parts(mixed), square, scale_ref[0:1, 0:1], coupling.shape[1])


def upper_kernel(blocks, weight, *refs):
    *ins, gram_left, norm_out, upper_out = refs
    upper = rotated_upper(blocks, upper_out.shape[0], *ins)
    upper_out[...] = upper
    weighted = weight[...] * upper
    norm_out[...] = jnp.sum(weighted * upper, axis=0, keepdims=True)
    high, low = two_parts(weighted.T)
    gram_left[...] = jnp.concatenate([high, high, low], axis=1)


def last_upper_kernel(blocks, *refs):
    *ins, out, held, sent = refs
    stored(held, rotated_upper(blocks, held.shape[0], *ins))
    copy = pltpu.make_async_copy(held, out.at[:, pl.ds(0, held.shape[1])], sent)
    copy.start()
    copy.wait()


def last_lower_kernel(lower, filled, out, sent):
    del filled
    width = lower.shape[1]
    copy = pltpu.make_async_copy(lower, out.at[:, pl.ds(width, width)], sent)
    copy.start()
    copy.wait()


def gram_kernel(gram_left, norm_upper, weight, own_ref, payload):
    width = gram_left.shape[0]
    own = halves_swapped(own_ref[...])
    high, low = two_parts(own)
    right = jnp.concatenate([high, low, high], axis=0)
    payload[:width] = jnp.dot(gram_left[...], right, preferred_element_type=F32)
    norm_lower = jnp.sum(weight[...] * own * own, axis=0, keepdims=True)
    half = own.shape[1]
    payload[width:] = norm_rows(norm_lower, norm_upper[:, :half], norm_upper[:, half:])


ON_CHIP = pl.BlockSpec(memory_space=pltpu.VMEM)
ANYWHERE = pl.BlockSpec(memory_space=pl.ANY)
GRANT = pltpu.CompilerParams(vmem_limit_bytes=24 << 20)


def in_vmem(kernel, outs, *args):
    return pl.pallas_call(
        kernel,
        out_shape=[jax.ShapeDtypeStruct(shape, dtype) for shape, dtype in outs],
        in_specs=[ON_CHIP] * len(args),
        out_specs=[ON_CHIP] * len(outs),
        compiler_params=GRANT,
    )(*args)


def body(snapshot, weights, damping):
    rows, columns = snapshot.shape
    width = columns // 2
    half = width // 2
    whole = (2 * rows, width)
    own_part, other_part, near = pl.pallas_call(
        start_kernel,
        out_shape=[jax.ShapeDtypeStruct((width + 8, half), F32)] * 2 + [jax.ShapeDtypeStruct(snapshot.shape, F32)],
        in_specs=[pl.BlockSpec(memory_space=pltpu.HBM)] * 2,
        out_specs=[ON_CHIP] * 3,
        scratch_shapes=[
            pltpu.VMEM((1, rows), F32),
            pltpu.SemaphoreType.DMA(()),
            pltpu.SemaphoreType.DMA(()),
        ],
        compiler_params=GRANT,
    )(*(pltpu.with_memory_space_constraint(value, pltpu.HBM) for value in (snapshot, weights[None])))
    own_part, other_part, damping = lax.optimization_barrier((own_part, other_part, damping))
    payload = own_part + swapped(other_part, 1, 1)
    weight = jnp.concatenate([weights, swapped(weights, 1, 1)])[:, None]
    blocks, held, arriving = start_blocks, (near,), swapped(near, 1, 1)
    damps = damping[:, 0].astype(F32) / (damping[:, 0] + damping[:, 1]).astype(F32)
    damps = lax.optimization_barrier(jnp.broadcast_to(damps[:, None], (STEPS, 128)))
    for step in range(STEPS):
        last = step + 1 == STEPS
        own, known, needed, arriving = chip_sum(payload, arriving)
        held = held + (arriving,)
        remote = swapped(needed, 1, 1)
        shape = (rows, width) if last else (2 * rows, half)
        pieces = in_vmem(
            functools.partial(half_kernel, len(own), blocks, step, last),
            [((width, half), F32)]
            + [((width, half), jnp.bfloat16)] * 2
            + [((shape[0], width), jnp.bfloat16)] * 2
            + [((width, half), F32), ((half, half), F32), ((1, half), F32)]
            + [((shape[0], half), jnp.bfloat16)] * 2,
            damps,
            *own,
            *held,
        )
        moved, other_coupling, scale = in_vmem(
            functools.partial(lower_kernel, len(known) + 1, blocks, last),
            [(shape, F32), ((width, half), F32), ((8, 128), F32)],
            *pieces[1:],
            *known,
            remote,
            *held,
        )
        coupling = (pieces[0], other_coupling)
        if last:
            break
        moved = column_shift(moved, 1)
        gram_left, norm_upper, upper = in_vmem(
            functools.partial(upper_kernel, blocks),
            [((width, 6 * rows), jnp.bfloat16), ((1, width), F32), (whole, F32)],
            weight,
            *coupling,
            scale,
            *held,
        )
        blocks, held, arriving = later_blocks, (upper, moved), swapped(moved, 1, 1)
        (payload,) = in_vmem(gram_kernel, [((width + 8, half), F32)], gram_left, norm_upper, weight, moved)
    moved = column_shift(moved, 1 - STEPS)
    out_shape = jax.ShapeDtypeStruct((rows, columns), F32)
    rotated = pl.pallas_call(
        functools.partial(last_upper_kernel, blocks),
        out_shape=out_shape,
        in_specs=[ON_CHIP] * (3 + len(held)),
        out_specs=ANYWHERE,
        scratch_shapes=[pltpu.VMEM((rows, width), F32), pltpu.SemaphoreType.DMA(())],
        compiler_params=GRANT,
    )(*coupling, scale, *held)
    return pl.pallas_call(
        last_lower_kernel,
        out_shape=out_shape,
        in_specs=[ON_CHIP, ANYWHERE],
        out_specs=ANYWHERE,
        scratch_shapes=[pltpu.SemaphoreType.DMA(())],
        input_output_aliases={1: 0},
        compiler_params=GRANT,
    )(moved, rotated)


def solution(mesh):
    placed = (P("pts", "cols"), P("pts"), P())
    return jax.shard_map(
        body, mesh=mesh, in_specs=placed, out_specs=P("pts", "cols"), check_vma=False
    )
```

```python
import functools

import jax
import jax.numpy as jnp
from jax import lax
from jax.experimental import pallas as pl
from jax.experimental.pallas import tpu as pltpu
from jax.sharding import PartitionSpec as P

STEPS = 3
EPSILON = 1e-06
F32 = jnp.float32


def column_shift(value, steps):
    points, columns = lax.axis_size("pts"), lax.axis_size("cols")
    pairs = [
        (point * columns + column, (point ^ 1) * columns + (column + steps) % columns)
        for point in range(points)
        for column in range(columns)
    ]
    return lax.ppermute(value, ("pts", "cols"), pairs)


def swapped(value, even_bits, odd_bits):
    count = lax.axis_size("pts")
    pairs = [(source, source ^ (odd_bits if source % 2 else even_bits)) for source in range(count)]
    return lax.ppermute(value, "pts", pairs)


def chip_sum(value, beside):
    count = lax.axis_size("pts")
    bit = 2
    own, known, needed = (value,), (), value
    while bit < count:
        if 2 * bit < count:
            for _ in range(2):
                near = swapped(value, 1, 1)
                far = swapped(value, 2 * bit ^ 1, bit ^ 1)
                own, known, needed = (near, far), (value,), far
                value = far + near
                value, beside = lax.optimization_barrier((value, beside))
        else:
            value = value + swapped(value, bit, bit)
            own, known, needed = (value,), (), value
        bit *= 4
    return own, known, needed, beside


def two_parts(value):
    high = value.astype(jnp.bfloat16)
    return high, (value - high.astype(F32)).astype(jnp.bfloat16)


def first_columns(parts, columns):
    return parts[0][:, :columns], parts[1][:, :columns]


def product(left, right, left_axis=1, right_axis=0):
    return lax.dot_general(
        jnp.concatenate([left[0], left[0], left[1]], axis=left_axis),
        jnp.concatenate([right[0], right[1], right[0]], axis=right_axis),
        (((left_axis,), (right_axis,)), ((), ())),
        preferred_element_type=F32,
    )


def halves_swapped(value):
    half = value.shape[0] // 2
    return jnp.concatenate([value[half:], value[:half]], axis=0)


def times_inverse_root(left_parts, square, scale, columns):
    rows = lax.broadcasted_iota(jnp.int32, square.shape, 0)
    identity = jnp.where(rows == lax.broadcasted_iota(jnp.int32, square.shape, 1), 1.0, 0.0)
    base = (identity + square) * (1.0 / scale)
    base_parts = two_parts(base)
    second = product(base_parts, base_parts)
    left_base = product(left_parts, base_parts)
    first_square = two_parts(2.25 * identity - 1.5 * base + 0.25 * second)
    cubic = product(two_parts(1.5 * base - 0.5 * second), first_square)
    both = two_parts(2.25 * identity - 0.75 * base - 0.5 * cubic)
    both_first = first_columns(both, columns)
    both_square = product(both, both_first)
    left_cubic = product(two_parts(left_base), both)
    left_both = product(left_parts, both_first)
    left_last = product(two_parts(left_cubic), two_parts(both_square))
    root = lax.rsqrt(scale)
    return left_both * (1.5 * root) - left_last * (0.5 * root)


def joined(own, other):
    return jnp.concatenate([own, halves_swapped(other)], axis=1)


def own_half(half):
    own = (lax.axis_index("pts") % 2) * half
    return pl.multiple_of(own, half), pl.multiple_of(half - own, half)


def start_blocks(near, far):
    width = near.shape[1] // 2
    own, other = own_half(width // 2)

    def taken(start):
        piece = (slice(None), pl.ds(start, width // 2))
        return jnp.concatenate([near[piece], far[piece]], axis=0)

    upper = jnp.concatenate([taken(own), taken(other)], axis=1)
    return upper, jnp.concatenate([taken(width + own), taken(width + other)], axis=1)


def later_blocks(upper, own, other):
    return upper[...], jnp.concatenate([halves_swapped(own[...]), other[...]], axis=1)


def stored(ref, value):
    half = ref.shape[1] // 2
    own, other = own_half(half)
    ref[:, pl.ds(own, half)] = value[:, :half]
    ref[:, pl.ds(other, half)] = value[:, half:]


def norm_rows(norm_lower, norm_upper, norm_upper_other):
    rows = lax.broadcasted_iota(jnp.int32, (8, norm_lower.shape[1]), 0)
    uppers = jnp.where(rows == 1, norm_upper, jnp.where(rows == 2, norm_upper_other, 0.0))
    return jnp.where(rows == 0, norm_lower, uppers)


def start_kernel(near_ref, weight_ref, own_part, other_part, near, weight, near_sent, weight_sent):
    copies = [
        pltpu.make_async_copy(near_ref, near, near_sent),
        pltpu.make_async_copy(weight_ref, weight, weight_sent),
    ]
    for copy in copies:
        copy.start()
    for copy in copies:
        copy.wait()
    width = near.shape[1] // 2
    half = width // 2
    own, other = own_half(half)
    point_weight = jnp.broadcast_to(weight[...], (8, weight.shape[1])).T[:, 0:1]
    upper_own, upper_other = near[:, pl.ds(own, half)], near[:, pl.ds(other, half)]
    upper_parts = two_parts(jnp.concatenate([upper_own, upper_other], axis=1))
    orders = ((upper_own, upper_other), (upper_other, upper_own))
    for start, order, out in zip((own, other), orders, (own_part, other_part)):
        lower = near[:, pl.ds(width + start, half)]
        weighted = point_weight * lower
        gram = product(upper_parts, two_parts(weighted), 0, 0)
        out[:width] = gram if out is own_part else halves_swapped(gram)
        norm_lower = jnp.sum(weighted * lower, axis=0, keepdims=True)
        uppers = [jnp.sum(point_weight * value * value, axis=0, keepdims=True) for value in order]
        out[width:] = norm_rows(norm_lower, *uppers)


def taken_rows(last, rows):
    return slice(rows, 2 * rows) if last else slice(0, rows)


def total(refs):
    return sum((ref[...] for ref in refs[1:]), refs[0][...])


def half_kernel(addends, blocks, step, last, damps, *refs):
    *ins, own_coupling, own_high, own_low, upper_high, upper_low, left_scale, square, norm, high, low = refs
    own_sum, block_refs = total(ins[:addends]), ins[addends:]
    width, half = own_coupling.shape
    upper, lower = blocks(*block_refs)
    inverse = lax.rsqrt(own_sum[width:] + EPSILON)
    uppers = jnp.broadcast_to(jnp.concatenate([inverse[1:2], inverse[2:3]], axis=1), (8, width))
    scaled = damps[step : step + 1, 0:1] * uppers.T[:, 0:1]
    left_scale[...] = jnp.broadcast_to(scaled, left_scale.shape)
    coupling = own_sum[:width] * scaled * inverse[0:1]
    own_coupling[...] = coupling
    norm[...] = jnp.sum(coupling * coupling, axis=0, keepdims=True)
    parts = own_high[...], own_low[...] = two_parts(coupling)
    square[...] = product(parts, parts, 0, 0)
    taken = taken_rows(last, high.shape[0])
    upper_parts = upper_high[...], upper_low[...] = two_parts(upper[taken])
    high[...], low[...] = two_parts(lower[taken, :half] + product(upper_parts, parts))


def lower_kernel(
    addends, blocks, last, own_high, own_low, upper_high, upper_low, left_scale, own_square, norm, high, low, *refs
):
    *ins, moved, other_coupling, scale_out = refs
    other_sum, block_refs = total(ins[:addends]), ins[addends:]
    width, half = own_high.shape
    _, lower = blocks(*block_refs)
    inverse = lax.rsqrt(other_sum[width : width + 1] + EPSILON)
    coupling = halves_swapped(other_sum[:width]) * left_scale[...] * inverse
    other_coupling[...] = coupling
    other_parts = two_parts(coupling)
    own_parts = own_high[...], own_low[...]
    parts = [jnp.concatenate(pair, axis=1) for pair in zip(own_parts, other_parts)]
    crossed = product(other_parts, own_parts, 0, 0)
    square = jnp.concatenate(
        [jnp.concatenate([own_square[...], crossed], axis=0), product(parts, other_parts, 0, 0)], axis=1
    )
    norms = norm[...] + jnp.sum(coupling * coupling, axis=0, keepdims=True)
    scale = 1.0 + jnp.sum(norms, keepdims=True)
    scale_out[...] = jnp.broadcast_to(scale, scale_out.shape)
    rows, columns = moved.shape
    taken = taken_rows(last, rows)
    other_mixed = lower[taken, half:] + product((upper_high[...], upper_low[...]), other_parts)
    mixed = [jnp.concatenate(pair, axis=1) for pair in zip((high[...], low[...]), two_parts(other_mixed))]
    result = times_inverse_root(mixed, square, scale, columns)
    if last:
        stored(moved, result)
    else:
        moved[...] = result


def rotated_upper(blocks, rows, own_coupling, other_coupling, scale_ref, *block_refs):
    coupling = jnp.concatenate([own_coupling[...], other_coupling[...]], axis=1)
    upper, lower = blocks(*block_refs)
    parts = two_parts(coupling)
    mixed = upper[:rows] - product(two_parts(lower[:rows]), parts, 1, 1)
    square = product(parts, parts, 1, 1)
    return times_inverse_root(two_parts(mixed), square, scale_ref[0:1, 0:1], coupling.shape[1])


def upper_kernel(blocks, weight, *refs):
    *ins, gram_left, norm_out, upper_out = refs
    upper = rotated_upper(blocks, upper_out.shape[0], *ins)
    upper_out[...] = upper
    weighted = weight[...] * upper
    norm_out[...] = jnp.sum(weighted * upper, axis=0, keepdims=True)
    high, low = two_parts(weighted.T)
    gram_left[...] = jnp.concatenate([high, high, low], axis=1)


def last_upper_kernel(blocks, *refs):
    *ins, out, held, sent = refs
    stored(held, rotated_upper(blocks, held.shape[0], *ins))
    copy = pltpu.make_async_copy(held, out.at[:, pl.ds(0, held.shape[1])], sent)
    copy.start()
    copy.wait()


def last_lower_kernel(lower, filled, out, sent):
    del filled
    width = lower.shape[1]
    copy = pltpu.make_async_copy(lower, out.at[:, pl.ds(width, width)], sent)
    copy.start()
    copy.wait()


def gram_kernel(gram_left, norm_upper, weight, own_ref, payload):
    width = gram_left.shape[0]
    own = halves_swapped(own_ref[...])
    high, low = two_parts(own)
    right = jnp.concatenate([high, low, high], axis=0)
    payload[:width] = jnp.dot(gram_left[...], right, preferred_element_type=F32)
    norm_lower = jnp.sum(weight[...] * own * own, axis=0, keepdims=True)
    half = own.shape[1]
    payload[width:] = norm_rows(norm_lower, norm_upper[:, :half], norm_upper[:, half:])


ON_CHIP = pl.BlockSpec(memory_space=pltpu.VMEM)
ANYWHERE = pl.BlockSpec(memory_space=pl.ANY)
GRANT = pltpu.CompilerParams(vmem_limit_bytes=24 << 20)


def in_vmem(kernel, outs, *args):
    return pl.pallas_call(
        kernel,
        out_shape=[jax.ShapeDtypeStruct(shape, dtype) for shape, dtype in outs],
        in_specs=[ON_CHIP] * len(args),
        out_specs=[ON_CHIP] * len(outs),
        compiler_params=GRANT,
    )(*args)


def body(snapshot, weights, damping):
    rows, columns = snapshot.shape
    width = columns // 2
    half = width // 2
    whole = (2 * rows, width)
    own_part, other_part, near = pl.pallas_call(
        start_kernel,
        out_shape=[jax.ShapeDtypeStruct((width + 8, half), F32)] * 2 + [jax.ShapeDtypeStruct(snapshot.shape, F32)],
        in_specs=[pl.BlockSpec(memory_space=pltpu.HBM)] * 2,
        out_specs=[ON_CHIP] * 3,
        scratch_shapes=[
            pltpu.VMEM((1, rows), F32),
            pltpu.SemaphoreType.DMA(()),
            pltpu.SemaphoreType.DMA(()),
        ],
        compiler_params=GRANT,
    )(*(pltpu.with_memory_space_constraint(value, pltpu.HBM) for value in (snapshot, weights[None])))
    own_part, other_part, damping = lax.optimization_barrier((own_part, other_part, damping))
    payload = own_part + swapped(other_part, 1, 1)
    weight = jnp.concatenate([weights, swapped(weights, 1, 1)])[:, None]
    blocks, held, arriving = start_blocks, (near,), swapped(near, 1, 1)
    damps = damping[:, 0].astype(F32) / (damping[:, 0] + damping[:, 1]).astype(F32)
    damps = lax.optimization_barrier(jnp.broadcast_to(damps[:, None], (STEPS, 128)))
    for step in range(STEPS):
        last = step + 1 == STEPS
        own, known, needed, arriving = chip_sum(payload, arriving)
        held = held + (arriving,)
        remote = swapped(needed, 1, 1)
        shape = (rows, width) if last else (2 * rows, half)
        pieces = in_vmem(
            functools.partial(half_kernel, len(own), blocks, step, last),
            [((width, half), F32)]
            + [((width, half), jnp.bfloat16)] * 2
            + [((shape[0], width), jnp.bfloat16)] * 2
            + [((width, half), F32), ((half, half), F32), ((1, half), F32)]
            + [((shape[0], half), jnp.bfloat16)] * 2,
            damps,
            *own,
            *held,
        )
        moved, other_coupling, scale = in_vmem(
            functools.partial(lower_kernel, len(known) + 1, blocks, last),
            [(shape, F32), ((width, half), F32), ((8, 128), F32)],
            *pieces[1:],
            *known,
            remote,
            *held,
        )
        coupling = (pieces[0], other_coupling)
        if last:
            break
        moved = column_shift(moved, 1)
        gram_left, norm_upper, upper = in_vmem(
            functools.partial(upper_kernel, blocks),
            [((width, 6 * rows), jnp.bfloat16), ((1, width), F32), (whole, F32)],
            weight,
            *coupling,
            scale,
            *held,
        )
        blocks, held, arriving = later_blocks, (upper, moved), swapped(moved, 1, 1)
        (payload,) = in_vmem(gram_kernel, [((width + 8, half), F32)], gram_left, norm_upper, weight, moved)
    moved = column_shift(moved, 1 - STEPS)
    out_shape = jax.ShapeDtypeStruct((rows, columns), F32)
    rotated = pl.pallas_call(
        functools.partial(last_upper_kernel, blocks),
        out_shape=out_shape,
        in_specs=[ON_CHIP] * (3 + len(held)),
        out_specs=ANYWHERE,
        scratch_shapes=[pltpu.VMEM((rows, width), F32), pltpu.SemaphoreType.DMA(())],
        compiler_params=GRANT,
    )(*coupling, scale, *held)
    return pl.pallas_call(
        last_lower_kernel,
        out_shape=out_shape,
        in_specs=[ON_CHIP, ANYWHERE],
        out_specs=ANYWHERE,
        scratch_shapes=[pltpu.SemaphoreType.DMA(())],
        input_output_aliases={1: 0},
        compiler_params=GRANT,
    )(moved, rotated)


def solution(mesh):
    placed = (P("pts", "cols"), P("pts"), P())
    return jax.shard_map(
        body, mesh=mesh, in_specs=placed, out_specs=P("pts", "cols"), check_vma=False
    )
```

```python
import functools

import jax
import jax.numpy as jnp
from jax import lax
from jax.experimental import pallas as pl
from jax.experimental.pallas import tpu as pltpu
from jax.sharding import PartitionSpec as P

STEPS = 3
EPSILON = 1e-06
F32 = jnp.float32


def column_shift(value, steps):
    points, columns = lax.axis_size("pts"), lax.axis_size("cols")
    pairs = [
        (point * columns + column, (point ^ 1) * columns + (column + steps) % columns)
        for point in range(points)
        for column in range(columns)
    ]
    return lax.ppermute(value, ("pts", "cols"), pairs)


def swapped(value, even_bits, odd_bits):
    count = lax.axis_size("pts")
    pairs = [(source, source ^ (odd_bits if source % 2 else even_bits)) for source in range(count)]
    return lax.ppermute(value, "pts", pairs)


def chip_sum(value, beside):
    count = lax.axis_size("pts")
    bit = 2
    own, known, needed = (value,), (), value
    while bit < count:
        if 2 * bit < count:
            for _ in range(2):
                near = swapped(value, 1, 1)
                far = swapped(value, 2 * bit ^ 1, bit ^ 1)
                own, known, needed = (near, far), (value,), far
                value = far + near
                value, beside = lax.optimization_barrier((value, beside))
        else:
            value = value + swapped(value, bit, bit)
            own, known, needed = (value,), (), value
        bit *= 4
    return own, known, needed, beside


def two_parts(value):
    high = value.astype(jnp.bfloat16)
    return high, (value - high.astype(F32)).astype(jnp.bfloat16)


def first_columns(parts, columns):
    return parts[0][:, :columns], parts[1][:, :columns]


def product(left, right, left_axis=1, right_axis=0):
    return lax.dot_general(
        jnp.concatenate([left[0], left[0], left[1]], axis=left_axis),
        jnp.concatenate([right[0], right[1], right[0]], axis=right_axis),
        (((left_axis,), (right_axis,)), ((), ())),
        preferred_element_type=F32,
    )


def halves_swapped(value):
    half = value.shape[0] // 2
    return jnp.concatenate([value[half:], value[:half]], axis=0)


def times_inverse_root(left_parts, square, scale, columns):
    rows = lax.broadcasted_iota(jnp.int32, square.shape, 0)
    identity = jnp.where(rows == lax.broadcasted_iota(jnp.int32, square.shape, 1), 1.0, 0.0)
    base = (identity + square) * (1.0 / scale)
    base_parts = two_parts(base)
    second = product(base_parts, base_parts)
    left_base = product(left_parts, base_parts)
    first_square = two_parts(2.25 * identity - 1.5 * base + 0.25 * second)
    cubic = product(two_parts(0.25 * second - 0.75 * base), first_square)
    both = two_parts((2.25 * identity - 0.75 * base) + cubic)
    both_first = first_columns(both, columns)
    both_square = product(both, both_first)
    left_cubic = product(two_parts(left_base), both)
    left_both = product(left_parts, both_first)
    left_last = product(two_parts(left_cubic), two_parts(both_square))
    root = lax.rsqrt(scale)
    return left_both * (1.5 * root) - left_last * (0.5 * root)


def joined(own, other):
    return jnp.concatenate([own, halves_swapped(other)], axis=1)


def own_half(half):
    own = (lax.axis_index("pts") % 2) * half
    return pl.multiple_of(own, half), pl.multiple_of(half - own, half)


def start_blocks(near, far):
    width = near.shape[1] // 2
    own, other = own_half(width // 2)

    def taken(start):
        piece = (slice(None), pl.ds(start, width // 2))
        return jnp.concatenate([near[piece], far[piece]], axis=0)

    upper = jnp.concatenate([taken(own), taken(other)], axis=1)
    return upper, jnp.concatenate([taken(width + own), taken(width + other)], axis=1)


def later_blocks(upper, own, other):
    return upper[...], jnp.concatenate([halves_swapped(own[...]), other[...]], axis=1)


def stored(ref, value):
    half = ref.shape[1] // 2
    own, other = own_half(half)
    ref[:, pl.ds(own, half)] = value[:, :half]
    ref[:, pl.ds(other, half)] = value[:, half:]


def norm_rows(norm_lower, norm_upper, norm_upper_other):
    rows = lax.broadcasted_iota(jnp.int32, (8, norm_lower.shape[1]), 0)
    uppers = jnp.where(rows == 1, norm_upper, jnp.where(rows == 2, norm_upper_other, 0.0))
    return jnp.where(rows == 0, norm_lower, uppers)


def start_kernel(near_ref, weight_ref, own_part, other_part, near, weight, near_sent, weight_sent):
    copies = [
        pltpu.make_async_copy(near_ref, near, near_sent),
        pltpu.make_async_copy(weight_ref, weight, weight_sent),
    ]
    for copy in copies:
        copy.start()
    for copy in copies:
        copy.wait()
    width = near.shape[1] // 2
    half = width // 2
    own, other = own_half(half)
    point_weight = jnp.broadcast_to(weight[...], (8, weight.shape[1])).T[:, 0:1]
    upper_own, upper_other = near[:, pl.ds(own, half)], near[:, pl.ds(other, half)]
    upper_parts = two_parts(jnp.concatenate([upper_own, upper_other], axis=1))
    orders = ((upper_own, upper_other), (upper_other, upper_own))
    for start, order, out in zip((own, other), orders, (own_part, other_part)):
        lower = near[:, pl.ds(width + start, half)]
        weighted = point_weight * lower
        gram = product(upper_parts, two_parts(weighted), 0, 0)
        out[:width] = gram if out is own_part else halves_swapped(gram)
        norm_lower = jnp.sum(weighted * lower, axis=0, keepdims=True)
        uppers = [jnp.sum(point_weight * value * value, axis=0, keepdims=True) for value in order]
        out[width:] = norm_rows(norm_lower, *uppers)


def taken_rows(last, rows):
    return slice(rows, 2 * rows) if last else slice(0, rows)


def total(refs):
    return sum((ref[...] for ref in refs[1:]), refs[0][...])


def half_kernel(addends, blocks, step, last, damps, *refs):
    *ins, own_coupling, own_high, own_low, upper_high, upper_low, left_scale, square, norm, high, low = refs
    own_sum, block_refs = total(ins[:addends]), ins[addends:]
    width, half = own_coupling.shape
    upper, lower = blocks(*block_refs)
    inverse = lax.rsqrt(own_sum[width:] + EPSILON)
    uppers = jnp.broadcast_to(jnp.concatenate([inverse[1:2], inverse[2:3]], axis=1), (8, width))
    scaled = damps[step : step + 1, 0:1] * uppers.T[:, 0:1]
    left_scale[...] = jnp.broadcast_to(scaled, left_scale.shape)
    coupling = own_sum[:width] * scaled * inverse[0:1]
    own_coupling[...] = coupling
    norm[...] = jnp.sum(coupling * coupling, axis=0, keepdims=True)
    parts = own_high[...], own_low[...] = two_parts(coupling)
    square[...] = product(parts, parts, 0, 0)
    taken = taken_rows(last, high.shape[0])
    upper_parts = upper_high[...], upper_low[...] = two_parts(upper[taken])
    high[...], low[...] = two_parts(lower[taken, :half] + product(upper_parts, parts))


def lower_kernel(
    addends, blocks, last, own_high, own_low, upper_high, upper_low, left_scale, own_square, norm, high, low, *refs
):
    *ins, moved, other_coupling, scale_out = refs
    other_sum, block_refs = total(ins[:addends]), ins[addends:]
    width, half = own_high.shape
    _, lower = blocks(*block_refs)
    inverse = lax.rsqrt(other_sum[width : width + 1] + EPSILON)
    coupling = halves_swapped(other_sum[:width]) * left_scale[...] * inverse
    other_coupling[...] = coupling
    other_parts = two_parts(coupling)
    own_parts = own_high[...], own_low[...]
    parts = [jnp.concatenate(pair, axis=1) for pair in zip(own_parts, other_parts)]
    crossed = product(other_parts, own_parts, 0, 0)
    square = jnp.concatenate(
        [jnp.concatenate([own_square[...], crossed], axis=0), product(parts, other_parts, 0, 0)], axis=1
    )
    norms = norm[...] + jnp.sum(coupling * coupling, axis=0, keepdims=True)
    scale = 1.0 + jnp.sum(norms, keepdims=True)
    scale_out[...] = jnp.broadcast_to(scale, scale_out.shape)
    rows, columns = moved.shape
    taken = taken_rows(last, rows)
    other_mixed = lower[taken, half:] + product((upper_high[...], upper_low[...]), other_parts)
    mixed = [jnp.concatenate(pair, axis=1) for pair in zip((high[...], low[...]), two_parts(other_mixed))]
    result = times_inverse_root(mixed, square, scale, columns)
    if last:
        stored(moved, result)
    else:
        moved[...] = result


def rotated_upper(blocks, rows, own_coupling, other_coupling, scale_ref, *block_refs):
    coupling = jnp.concatenate([own_coupling[...], other_coupling[...]], axis=1)
    upper, lower = blocks(*block_refs)
    parts = two_parts(coupling)
    mixed = upper[:rows] - product(two_parts(lower[:rows]), parts, 1, 1)
    square = product(parts, parts, 1, 1)
    return times_inverse_root(two_parts(mixed), square, scale_ref[0:1, 0:1], coupling.shape[1])


def upper_kernel(blocks, weight, *refs):
    *ins, gram_left, norm_out, upper_out = refs
    upper = rotated_upper(blocks, upper_out.shape[0], *ins)
    upper_out[...] = upper
    weighted = weight[...] * upper
    norm_out[...] = jnp.sum(weighted * upper, axis=0, keepdims=True)
    high, low = two_parts(weighted.T)
    gram_left[...] = jnp.concatenate([high, high, low], axis=1)


def last_upper_kernel(blocks, *refs):
    *ins, out, held, sent = refs
    stored(held, rotated_upper(blocks, held.shape[0], *ins))
    copy = pltpu.make_async_copy(held, out.at[:, pl.ds(0, held.shape[1])], sent)
    copy.start()
    copy.wait()


def last_lower_kernel(lower, filled, out, sent):
    del filled
    width = lower.shape[1]
    copy = pltpu.make_async_copy(lower, out.at[:, pl.ds(width, width)], sent)
    copy.start()
    copy.wait()


def gram_kernel(gram_left, norm_upper, weight, own_ref, payload):
    width = gram_left.shape[0]
    own = halves_swapped(own_ref[...])
    high, low = two_parts(own)
    right = jnp.concatenate([high, low, high], axis=0)
    payload[:width] = jnp.dot(gram_left[...], right, preferred_element_type=F32)
    norm_lower = jnp.sum(weight[...] * own * own, axis=0, keepdims=True)
    half = own.shape[1]
    payload[width:] = norm_rows(norm_lower, norm_upper[:, :half], norm_upper[:, half:])


ON_CHIP = pl.BlockSpec(memory_space=pltpu.VMEM)
ANYWHERE = pl.BlockSpec(memory_space=pl.ANY)
GRANT = pltpu.CompilerParams(vmem_limit_bytes=24 << 20)


def in_vmem(kernel, outs, *args):
    return pl.pallas_call(
        kernel,
        out_shape=[jax.ShapeDtypeStruct(shape, dtype) for shape, dtype in outs],
        in_specs=[ON_CHIP] * len(args),
        out_specs=[ON_CHIP] * len(outs),
        compiler_params=GRANT,
    )(*args)


def body(snapshot, weights, damping):
    rows, columns = snapshot.shape
    width = columns // 2
    half = width // 2
    whole = (2 * rows, width)
    own_part, other_part, near = pl.pallas_call(
        start_kernel,
        out_shape=[jax.ShapeDtypeStruct((width + 8, half), F32)] * 2 + [jax.ShapeDtypeStruct(snapshot.shape, F32)],
        in_specs=[pl.BlockSpec(memory_space=pltpu.HBM)] * 2,
        out_specs=[ON_CHIP] * 3,
        scratch_shapes=[
            pltpu.VMEM((1, rows), F32),
            pltpu.SemaphoreType.DMA(()),
            pltpu.SemaphoreType.DMA(()),
        ],
        compiler_params=GRANT,
    )(*(pltpu.with_memory_space_constraint(value, pltpu.HBM) for value in (snapshot, weights[None])))
    own_part, other_part, damping = lax.optimization_barrier((own_part, other_part, damping))
    payload = own_part + swapped(other_part, 1, 1)
    weight = jnp.concatenate([weights, swapped(weights, 1, 1)])[:, None]
    blocks, held, arriving = start_blocks, (near,), swapped(near, 1, 1)
    damps = damping[:, 0].astype(F32) / (damping[:, 0] + damping[:, 1]).astype(F32)
    damps = lax.optimization_barrier(jnp.broadcast_to(damps[:, None], (STEPS, 128)))
    for step in range(STEPS):
        last = step + 1 == STEPS
        own, known, needed, arriving = chip_sum(payload, arriving)
        held = held + (arriving,)
        remote = swapped(needed, 1, 1)
        shape = (rows, width) if last else (2 * rows, half)
        pieces = in_vmem(
            functools.partial(half_kernel, len(own), blocks, step, last),
            [((width, half), F32)]
            + [((width, half), jnp.bfloat16)] * 2
            + [((shape[0], width), jnp.bfloat16)] * 2
            + [((width, half), F32), ((half, half), F32), ((1, half), F32)]
            + [((shape[0], half), jnp.bfloat16)] * 2,
            damps,
            *own,
            *held,
        )
        moved, other_coupling, scale = in_vmem(
            functools.partial(lower_kernel, len(known) + 1, blocks, last),
            [(shape, F32), ((width, half), F32), ((8, 128), F32)],
            *pieces[1:],
            *known,
            remote,
            *held,
        )
        coupling = (pieces[0], other_coupling)
        if last:
            break
        moved = column_shift(moved, 1)
        gram_left, norm_upper, upper = in_vmem(
            functools.partial(upper_kernel, blocks),
            [((width, 6 * rows), jnp.bfloat16), ((1, width), F32), (whole, F32)],
            weight,
            *coupling,
            scale,
            *held,
        )
        blocks, held, arriving = later_blocks, (upper, moved), swapped(moved, 1, 1)
        (payload,) = in_vmem(gram_kernel, [((width + 8, half), F32)], gram_left, norm_upper, weight, moved)
    moved = column_shift(moved, 1 - STEPS)
    out_shape = jax.ShapeDtypeStruct((rows, columns), F32)
    rotated = pl.pallas_call(
        functools.partial(last_upper_kernel, blocks),
        out_shape=out_shape,
        in_specs=[ON_CHIP] * (3 + len(held)),
        out_specs=ANYWHERE,
        scratch_shapes=[pltpu.VMEM((rows, width), F32), pltpu.SemaphoreType.DMA(())],
        compiler_params=GRANT,
    )(*coupling, scale, *held)
    return pl.pallas_call(
        last_lower_kernel,
        out_shape=out_shape,
        in_specs=[ON_CHIP, ANYWHERE],
        out_specs=ANYWHERE,
        scratch_shapes=[pltpu.SemaphoreType.DMA(())],
        input_output_aliases={1: 0},
        compiler_params=GRANT,
    )(moved, rotated)


def solution(mesh):
    placed = (P("pts", "cols"), P("pts"), P())
    return jax.shard_map(
        body, mesh=mesh, in_specs=placed, out_specs=P("pts", "cols"), check_vma=False
    )
```
